128 devices in a mesh: tm: 4 (over y), region: 32 (over z, x, core).
Axes of the slice: x: 4, y: 4, z: 4, core: 2. Of those that a mesh axis runs over, the one named last changes fastest.
Arguments:
- search_one: float32 [4, 548, 32768], P('tm', None, 'region'), may hold values from -6 to 6
- search_two: float32 [4, 548, 32768], P('tm', None, 'region'), may hold values from -6 to 6
- column_gain: float32 [4, 548, 32768], P('tm', None, 'region'), may hold values from 0.5 to 1.25
- model_matrix: float32 [4, 548, 548], P('tm'), may hold values from -0.25 to 0.25
- obs_owner: int32 [4, 32768], P('tm', 'region'), may hold values from 0 to 31, as said below
- observe_matrix: float32 [4, 32, 548, 1024], P('tm', 'region'), may hold values from -0.25 to 0.25
- error_weight: float32 [4, 32, 1024], P('tm', 'region'), may hold values from 0.25 to 4
- channel_mask: int32 [4, 32, 1024], P('tm', 'region'), may hold values 0 or 1
Outputs:
- forward_state: float32 [4, 548, 32768], P('tm', None, 'region')
- gradient: float32 [4, 548, 32768], P('tm', None, 'region')
The draws below stay inside these ranges and needn't reach their ends.
Inputs may be any that keep to these rules, and one draw needn't show every extreme that they name: `obs_owner`: among the 1024 columns of one device (one subwindow, one aligned block of 1024 columns) no owner appears more than 48 times; in every subwindow one owner appears exactly 48 times in every block.
All inputs are finite; a program needn't handle non-finite values. No bound on the sum of `channel_mask` on one device may be relied on, other than what follows from the above.
Results may differ from the reference program's by a relative error of at most 0.0003.
Values sent between devices are 32-bit elements; how exact they have to be, the bound alone decides.
A program may use at most 128 MiB of HBM per device.

```python
import math
import jax
import jax.numpy as jnp
from jax import lax

NV = 548
CH = 1024
COLS = 1024
COLS_TOTAL = 32768
CAP = 48
N_TM = 4
N_REGION = 32


def draw_obs_owner(key, part):
    hottest = jax.random.randint(jax.random.fold_in(key, 7), (N_TM,), 0, N_REGION)

    def one_block(index):
        owner_hot = hottest[index // N_REGION]
        block_key = jax.random.fold_in(key, index + 11)
        others = (owner_hot + 1 + jnp.arange(N_REGION - 1, dtype=jnp.int32)) % N_REGION
        pool = jnp.repeat(others, CAP)
        picked = pool[jax.random.permutation(jax.random.fold_in(block_key, 1), pool.shape[0])[:COLS - CAP]]
        whole = jnp.concatenate([jnp.full((CAP,), owner_hot, jnp.int32), picked.astype(jnp.int32)])
        return whole[jax.random.permutation(jax.random.fold_in(block_key, 2), COLS)]
    blocks = jax.vmap(one_block)(jnp.arange(N_TM * N_REGION, dtype=jnp.int32))
    return blocks.reshape(N_TM, N_REGION * COLS).astype(jnp.int32)


def touch_ends(drawn, rng, low, high):
    place = [jax.random.randint(jax.random.fold_in(rng, axis), (), 0, length) for axis, length in enumerate(drawn.shape)]
    widest = drawn.shape.index(max(drawn.shape))
    neighbour = place[:widest] + [(place[widest] + 1) % drawn.shape[widest]] + place[widest + 1:]
    return drawn.at[tuple(place)].set(low).at[tuple(neighbour)].set(high)


def block_scale(stream_key, dims, split, least, largest):
    loudness = 1.0
    for axis_at, blocks in split:
        heights = jax.random.uniform(jax.random.fold_in(jax.random.fold_in(stream_key, 6), axis_at), (blocks,), jnp.float32, least / len(split), largest / len(split))
        loudness = loudness * jnp.repeat(jnp.exp(heights), dims[axis_at] // blocks).reshape((-1,) + (1,) * (len(dims) - 1 - axis_at))
    return loudness


def centred(own_key, extent, deviation, limit, shards=(), kind=jnp.bfloat16):
    array = jax.random.normal(own_key, extent, jnp.float32) * deviation
    if len(shards) > 0:
        array = block_scale(own_key, extent, shards, -0.22, 0.18) * array
    return jnp.clip(array, min=-limit, max=limit).astype(kind)


def setup_inputs(seed: int = 0) -> dict:
    streams_of = jax.random.split(jax.random.key(seed), 9)
    search_one = centred(streams_of[0], (N_TM, NV, COLS_TOTAL), 1.0, 6.0, ((0, 4), (2, 32)), jnp.float32)
    search_two = centred(streams_of[1], (N_TM, NV, COLS_TOTAL), 1.0, 6.0, ((0, 4), (2, 32)), jnp.float32)
    column_gain = jnp.clip(jnp.exp(math.log(1.25) - 0.916290732 * jax.random.uniform(streams_of[2], (N_TM, NV, COLS_TOTAL), jnp.float32) ** block_scale(streams_of[2], (N_TM, NV, COLS_TOTAL), ((0, 4), (2, 32)), -0.2, 0.2)), 0.5, 1.25)
    model_matrix = centred(streams_of[3], (N_TM, NV, NV), NV ** -0.5, 0.25, ((0, 4),), jnp.float32)
    obs_owner = draw_obs_owner(jax.random.fold_in(streams_of[8], 71), 0)
    observe_matrix = centred(streams_of[5], (N_TM, N_REGION, NV, CH), NV ** -0.5, 0.25, ((0, 4), (1, 32)), jnp.float32)
    error_weight = jnp.clip(jnp.exp(math.log(4.0) - 2.7725887 * jax.random.uniform(streams_of[6], (N_TM, N_REGION, CH), jnp.float32) ** block_scale(streams_of[6], (N_TM, N_REGION, CH), ((0, 4), (1, 32)), -0.2, 0.2)), 0.25, 4.0)
    channel_mask = touch_ends((jax.random.randint(streams_of[7], (N_TM, N_REGION, CH), 0, 4) < 3).astype(jnp.int32), jax.random.fold_in(streams_of[7], 1), 0, 1)
    return dict(search_one=search_one, search_two=search_two, column_gain=column_gain, model_matrix=model_matrix, obs_owner=obs_owner, observe_matrix=observe_matrix, error_weight=error_weight, channel_mask=channel_mask)


def high_dot(left, right):
    return jnp.dot(left, right, precision=lax.Precision.HIGHEST, preferred_element_type=jnp.float32)


def high_tdot(left, right):
    return lax.dot_general(left, right, (((0,), (0,)), ((), ())), precision=lax.Precision.HIGHEST, preferred_element_type=jnp.float32)


def observe(state, owners, matrices, weights):
    most = N_REGION * CAP
    order = jnp.argsort(owners, stable=True).astype(jnp.int32)
    counts = jnp.sum((owners[None, :] == jnp.arange(N_REGION, dtype=jnp.int32)[:, None]).astype(jnp.int32), axis=1).astype(jnp.int32)
    starts = (jnp.cumsum(counts) - counts).astype(jnp.int32)
    padded = jnp.concatenate([order, jnp.zeros((most,), jnp.int32)])

    def one_owner(accum, inputs):
        matrix, weight, start, count = inputs
        index = lax.dynamic_slice(padded, (start,), (most,)).astype(jnp.int32)
        valid = jnp.arange(most, dtype=jnp.int32) < count
        columns = jnp.take(state, index, axis=1)
        seen = high_tdot(matrix, columns) * weight[:, None]
        back = high_dot(matrix, seen)
        back = jnp.where(valid[None, :], back, jnp.zeros_like(back))
        return accum.at[:, index].add(back), None

    result, _ = lax.scan(one_owner, jnp.zeros_like(state), (matrices, weights, starts, counts))
    return result


def reference(search_one, search_two, column_gain, model_matrix, obs_owner, observe_matrix, error_weight, channel_mask):
    forward = [search_one[0]]
    for step in range(1, N_TM):
        forward.append(search_one[step] + column_gain[step] * high_dot(model_matrix[step], forward[-1]))
    swept = [search_two[N_TM - 1]]
    for step in range(N_TM - 2, -1, -1):
        swept.insert(0, search_two[step] + high_tdot(model_matrix[step + 1], column_gain[step + 1] * swept[0]))
    weights = error_weight * channel_mask.astype(error_weight.dtype)
    gradient = []
    for step in range(N_TM):
        observed = observe(forward[step], obs_owner[step], observe_matrix[step], weights[step])
        gradient.append(swept[step] + observed)
    return jnp.stack(forward), jnp.stack(gradient)
```

```python
import jax
import jax.numpy as jnp
from jax import lax
from jax.experimental import pallas as pl
from jax.experimental.pallas import tpu as pltpu
from jax.sharding import PartitionSpec as P

F32 = jnp.float32
BF16 = jnp.bfloat16
MESH = pl.DeviceIdType.MESH

OFFDIAG = ((0, 1), (0, 2), (0, 3), (1, 2), (1, 3), (2, 3))
FOLD_AT = 768
TAIL_AT = 1024
TAIL = 40
PACKED = TAIL_AT + 5 * TAIL
HALVES = ((0, 616, 312), (616, 608, 304))
SLOT = 64
CHUNK = 128


def split(x):
    high = x.astype(BF16)
    return high, (x - high.astype(F32)).astype(BF16)


def dot(a, b):
    return jnp.dot(a, b, preferred_element_type=F32)


def dot_nt(a, b):
    return lax.dot_general(a, b, (((1,), (1,)), ((), ())), preferred_element_type=F32)


def pack_kernel(matrix_ref, error_ref, mask_ref, out_ref):
    weight = error_ref[...] * mask_ref[...].astype(F32)
    matrix = matrix_ref[...]
    high, low = split(matrix)
    whigh, wlow = split(matrix * weight)

    def product(r0, r1, c0, c1):
        a, b = slice(r0, r1), slice(c0, c1)
        return dot_nt(whigh[a], high[b]) + (dot_nt(whigh[a], low[b]) + dot_nt(wlow[a], high[b]))

    top = product(0, 256, 0, 512)
    mid = product(256, 512, 256, 512)
    nv = matrix.shape[0]
    tail = product(512, nv, 0, nv)

    def block(i, j):
        if i < 2:
            return top[128 * i : 128 * i + 128, 128 * j : 128 * j + 128]
        return mid[128 * i - 256 : 128 * i - 128, 128 * j - 256 : 128 * j - 128]

    for at, (i, j) in enumerate(OFFDIAG):
        out_ref[128 * at : 128 * at + 128, :] = block(i, j)
    row = lax.broadcasted_iota(jnp.int32, (128, 128), 0)
    col = lax.broadcasted_iota(jnp.int32, (128, 128), 1)
    for pair in range(2):
        upper, lower = block(2 * pair, 2 * pair), block(2 * pair + 1, 2 * pair + 1)
        at = FOLD_AT + 128 * pair
        out_ref[at : at + 128, :] = jnp.where(row <= col, upper, lower)
    rest = nv - 512
    for j in range(5):
        at = TAIL_AT + TAIL * j
        if j < 4:
            out_ref[at : at + rest, :] = tail[:, 128 * j : 128 * j + 128]
            if j % 2 == 1:
                line = jnp.sum(jnp.where(row == col, block(j, j), 0.0), axis=0, keepdims=True)
            else:
                line = jnp.zeros((1, 128), F32)
            out_ref[at + rest : at + TAIL, :] = jnp.broadcast_to(line, (TAIL - rest, 128))
        else:
            out_ref[at : at + TAIL, :] = jnp.zeros((TAIL, 128), F32)
            out_ref[at : at + rest, 0:rest] = tail[:, 512:nv]


def pack(jacobian, error, mask):
    return pl.pallas_call(
        pack_kernel,
        out_shape=jax.ShapeDtypeStruct((PACKED, 128), F32),
        name="pack",
    )(jacobian, error, mask)


def sweep_kernel(
    one_ref, two_ref, gain_ref, matrix_ref, turned_ref, packed_ref,
    forward_ref, swept_ref, gathered_ref,
    into_f, into_b, out_b, m_high, m_low, t_high, t_low,
    f_send, f_recv, b_send, b_recv, g_send, g_recv, p_send, p_recv, own_sem,
):
    k = lax.axis_index("tm")
    region = lax.axis_index("region")
    core = region % 2
    x = (region // 2) % 4
    z = region // 8
    chunks = into_f.shape[0]

    def chip(dz, dx):
        return ((z + dz + 4) % 4 * 4 + (x + dx + 4) % 4) * 2 + core

    partner = region + 1 - 2 * core
    barrier = pltpu.get_barrier_semaphore()
    around = [(k, chip(1, 0)), (k, chip(-1, 0)), (k, chip(0, 1)), (k, chip(0, -1)), (k, partner),
              ((k + 1) % 4, region), ((k + 3) % 4, region)]
    for who in around:
        pl.semaphore_signal(barrier, inc=1, device_id=who, device_id_type=MESH)
    pl.semaphore_wait(barrier, len(around))

    def columns(c):
        return pl.ds(pl.multiple_of(c * CHUNK, CHUNK), CHUNK)

    def send_f(src, c):
        return pltpu.make_async_remote_copy(
            src_ref=src, dst_ref=into_f.at[c], send_sem=f_send.at[c], recv_sem=f_recv.at[c],
            device_id=((k + 1) % 4, region), device_id_type=MESH,
        )

    def send_b(c):
        return pltpu.make_async_remote_copy(
            src_ref=out_b.at[c], dst_ref=into_b.at[c], send_sem=b_send.at[c], recv_sem=b_recv.at[c],
            device_id=((k + 3) % 4, region), device_id_type=MESH,
        )

    def step_to(primary, by):
        return chip(by, 0) if primary == "z" else chip(0, by)

    def block_at(half, dp, dq):
        if half == 0:
            return chip(dq, dp)
        return chip(dp, dq)

    axes = (("x", "z"), ("z", "x"))
    sends = []

    def relay(half, dp, dq, piece, axis, by):
        start, size, cut = HALVES[half]
        if piece == 0:
            start, size = start, cut
        elif piece == 1:
            start, size = start + cut, size - cut
        block = block_at(half, dp, dq)
        own = dp == 0 and dq == 0
        rows = pl.ds(start, size)
        number = len(sends)
        rp, rq = dp % 4, dq % 4
        if axis == axes[half][0]:
            rp = (dp - by) % 4
        else:
            rq = (dq - by) % 4
        copy = pltpu.make_async_remote_copy(
            src_ref=packed_ref.at[rows] if own else gathered_ref.at[block, rows],
            dst_ref=gathered_ref.at[block, rows],
            send_sem=g_send.at[number],
            recv_sem=g_recv.at[half, rp * 4 + rq, 1 if piece == 1 else 0],
            device_id=(k, step_to(axis, by)),
            device_id_type=MESH,
        )
        copy.start()
        sends.append(copy)

    def arrived(half, dp, dq, piece):
        start, size, cut = HALVES[half]
        if piece == 0:
            start, size = start, cut
        elif piece == 1:
            start, size = start + cut, size - cut
        block = block_at(half, dp, dq)
        ref = gathered_ref.at[block, pl.ds(start, size)]
        sem = g_recv.at[half, dp % 4 * 4 + dq % 4, 1 if piece == 1 else 0]
        pltpu.make_async_copy(ref, ref, sem).wait()

    shared = []

    def share(half, dp, dq):
        start, size, _ = HALVES[half]
        block = block_at(half, dp, dq)
        rows = pl.ds(start, size)
        own = dp == 0 and dq == 0
        at = dp % 4 * 4 + dq % 4
        copy = pltpu.make_async_remote_copy(
            src_ref=packed_ref.at[rows] if own else gathered_ref.at[block, rows],
            dst_ref=gathered_ref.at[block, rows],
            send_sem=p_send.at[half, at],
            recv_sem=p_recv.at[half, at],
            device_id=(k, partner),
            device_id_type=MESH,
        )
        copy.start()
        shared.append((half, dp, dq, copy))

    def first(half, by):
        main, other = axes[half]
        arrived(half, by, 0, None)
        relay(half, by, 0, 0 if by == -1 else 1, main, -by)
        relay(half, by, 0, None, other, 1)
        relay(half, by, 0, None, other, -1)
        share(half, by, 0)

    def opposite(half):
        _, other = axes[half]
        arrived(half, 2, 0, 0)
        arrived(half, 2, 0, 1)
        relay(half, 2, 0, None, other, 1)
        relay(half, 2, 0, None, other, -1)
        share(half, 2, 0)

    def second(half, dp, by):
        _, other = axes[half]
        arrived(half, dp, by, None)
        relay(half, dp, by, 0 if by == -1 else 1, other, -by)
        share(half, dp, by)

    def last(half, dp):
        arrived(half, dp, 2, 0)
        arrived(half, dp, 2, 1)
        share(half, dp, 2)

    for half in range(2):
        main, _ = axes[half]
        relay(half, 0, 0, None, main, 1)
        relay(half, 0, 0, None, main, -1)
    for half in range(2):
        _, other = axes[half]
        relay(half, 0, 0, None, other, 1)
        relay(half, 0, 0, None, other, -1)

    @pl.when(k == 0)
    def _():
        for c in range(chunks):
            send_f(one_ref.at[:, c * CHUNK : (c + 1) * CHUNK], c).start()

    for half in range(2):
        share(half, 0, 0)
    own_copy = pltpu.make_async_copy(packed_ref, gathered_ref.at[region], own_sem)
    own_copy.start()

    high, low = split(matrix_ref[...])
    m_high[...], m_low[...] = high, low
    high, low = split(turned_ref[...])
    t_high[...], t_low[...] = high, low

    def times(a_high, a_low, v):
        v_high, v_low = split(v)
        both = dot(a_high[...], jnp.concatenate([v_high, v_low], axis=1))
        return both[:, :CHUNK] + (both[:, CHUNK:] + dot(a_low[...], v_high))

    events = {
        1: [(first, 0, -1), (first, 1, -1), (first, 0, 1), (first, 1, 1)],
        3: [(second, 0, 0, -1), (second, 1, 0, -1), (second, 0, 0, 1), (second, 1, 0, 1)],
        4: [(opposite, 0), (opposite, 1)],
        5: [(second, 0, -1, -1), (second, 1, -1, -1), (second, 0, -1, 1), (second, 1, -1, 1)],
        6: [(second, 0, 1, -1), (second, 1, 1, -1), (second, 0, 1, 1), (second, 1, 1, 1)],
        7: [(last, 0, 0), (last, 1, 0)],
        8: [(second, 0, 2, -1), (second, 1, 2, -1), (second, 0, 2, 1), (second, 1, 2, 1)],
        9: [(last, 0, -1), (last, 1, -1), (last, 0, 1), (last, 1, 1)],
        10: [(last, 0, 2), (last, 1, 2)],
    }

    def tick(t, carry):
        cb = t - (3 - k)

        @pl.when((cb >= 0) & (cb < chunks))
        def _():
            @pl.when(k < 3)
            def _():
                send_b(cb).wait_recv()
                swept_ref[:, columns(cb)] = two_ref[:, columns(cb)] + into_b[cb]

            @pl.when(k == 3)
            def _():
                swept_ref[:, columns(cb)] = two_ref[:, columns(cb)]

            @pl.when(k > 0)
            def _():
                out_b[cb] = times(t_high, t_low, gain_ref[:, columns(cb)] * swept_ref[:, columns(cb)])
                send_b(cb).start()

        cf = t - k

        @pl.when((cf >= 0) & (cf < chunks) & (k > 0))
        def _():
            send_f(into_f.at[cf], cf).wait_recv()
            forward_ref[:, columns(cf)] = one_ref[:, columns(cf)] + gain_ref[:, columns(cf)] * times(
                m_high, m_low, into_f[cf]
            )

            @pl.when(k < 3)
            def _():
                send_f(forward_ref.at[:, columns(cf)], cf).start()

        return carry

    at = 0
    for tick_end in sorted(events):
        lax.fori_loop(at, tick_end + 1, tick, 0)
        at = tick_end + 1
        for event in events[tick_end]:
            event[0](*event[1:])
    lax.fori_loop(at, chunks + 3, tick, 0)

    @pl.when(k == 0)
    def _():
        forward_ref[...] = one_ref[...]

    @pl.when(k < 3)
    def _():
        for c in range(chunks):
            send_f(into_f.at[c], c).wait_send()

    @pl.when(k > 0)
    def _():
        for c in range(chunks):
            send_b(c).wait_send()

    own_copy.wait()
    for copy in sends:
        copy.wait_send()
    for half, dp, dq, copy in shared:
        copy.wait_send()
        start, size, _ = HALVES[half]
        block = block_at(half, dp, dq) + 1 - 2 * core
        ref = gathered_ref.at[block, pl.ds(start, size)]
        pltpu.make_async_copy(ref, ref, p_recv.at[half, dp % 4 * 4 + dq % 4]).wait()


def sweep(one, two, gain, matrix, turned, packed):
    rows, cols = one.shape
    chunks = cols // CHUNK
    vmem = pl.BlockSpec(memory_space=pltpu.VMEM)
    return pl.pallas_call(
        sweep_kernel,
        out_shape=(
            jax.ShapeDtypeStruct((rows, cols), F32),
            jax.ShapeDtypeStruct((rows, cols), F32),
            jax.ShapeDtypeStruct((32, PACKED, 128), F32),
        ),
        in_specs=[vmem] * 6,
        out_specs=(vmem, vmem, pl.BlockSpec(memory_space=pl.ANY)),
        scratch_shapes=[
            pltpu.VMEM((chunks, rows, CHUNK), F32),
            pltpu.VMEM((chunks, rows, CHUNK), F32),
            pltpu.VMEM((chunks, rows, CHUNK), F32),
            pltpu.VMEM((rows, rows), BF16),
            pltpu.VMEM((rows, rows), BF16),
            pltpu.VMEM((rows, rows), BF16),
            pltpu.VMEM((rows, rows), BF16),
            pltpu.SemaphoreType.DMA((chunks,)),
            pltpu.SemaphoreType.DMA((chunks,)),
            pltpu.SemaphoreType.DMA((chunks,)),
            pltpu.SemaphoreType.DMA((chunks,)),
            pltpu.SemaphoreType.DMA((40,)),
            pltpu.SemaphoreType.DMA((2, 16, 2)),
            pltpu.SemaphoreType.DMA((2, 16)),
            pltpu.SemaphoreType.DMA((2, 16)),
            pltpu.SemaphoreType.DMA,
        ],
        compiler_params=pltpu.CompilerParams(
            collective_id=0, has_side_effects=True, vmem_limit_bytes=60 * 1024 * 1024
        ),
        name="sweep",
    )(one, two, gain, matrix, turned, packed)


def apply_kernel(
    owner_ref, forward_ref, swept_ref, gathered_ref,
    state_ref, gradient_ref,
    x_high, x_low, slot_row, slot_col, full, right,
):
    step = pl.program_id(0)
    rows, cols = forward_ref.shape
    pad = full.shape[1] // 2

    @pl.when(step == 0)
    def _():
        owner = owner_ref[...]
        onehot = (owner == lax.broadcasted_iota(jnp.int32, (32, cols), 0)).astype(F32)
        earlier = (
            lax.broadcasted_iota(jnp.int32, (cols, cols), 0) < lax.broadcasted_iota(jnp.int32, (cols, cols), 1)
        ).astype(F32)
        before = dot(onehot.astype(BF16), earlier.astype(BF16))
        placed = jnp.sum(before * onehot, axis=0, keepdims=True)
        slot = owner.astype(F32) * SLOT + placed
        slot_row[...] = jnp.broadcast_to(slot, slot_row.shape)
        slot_col[...] = jnp.broadcast_to(slot, (128, cols)).T
        high, low = split(forward_ref[...])
        x_high[...], x_low[...] = high, low
        state_ref[...] = forward_ref[...]
        gradient_ref[...] = swept_ref[...]
        right[...] = jnp.zeros_like(right)
        full[...] = jnp.zeros_like(full)

    wide = 4 * SLOT
    base = (step * wide).astype(F32)
    lane = lax.broadcasted_iota(jnp.int32, (cols, 128), 1).astype(F32) + base
    pick = jnp.concatenate(
        [(slot_col[...] == lane).astype(BF16), (slot_col[...] == lane + 128.0).astype(BF16)], axis=1
    )
    line = lax.broadcasted_iota(jnp.int32, (wide, cols), 0).astype(F32) + base
    place = (jnp.broadcast_to(slot_row[0:1, :], (wide, cols)) == line).astype(BF16)
    s_high = dot(x_high[...], pick)
    s_low = dot(x_low[...], pick)

    row = lax.broadcasted_iota(jnp.int32, (128, 128), 0)
    col = lax.broadcasted_iota(jnp.int32, (128, 128), 1)
    left_lanes = lax.broadcasted_iota(jnp.int32, (rows, 128), 1) < SLOT
    rest = rows - 512

    def put(at_row, at_col, value):
        high, low = split(value)
        r, c = value.shape
        full[at_row : at_row + r, at_col : at_col + c] = high
        full[at_row : at_row + r, pad + at_col : pad + at_col + c] = low

    answers = []
    for pair in range(2):
        lanes = slice(128 * pair, 128 * pair + 128)
        high = s_high[:, lanes]
        low = pltpu.roll(s_low[:, lanes], SLOT, 1)
        outs = []
        for side in range(2):
            mine = left_lanes if side == 0 else jnp.logical_not(left_lanes)
            right[0:rows, :] = jnp.where(mine, high, low).astype(BF16)
            right[pad : pad + rows, :] = jnp.where(mine, high, 0.0).astype(BF16)
            g = gathered_ref.at[2 * pair + side]
            for at, (i, j) in enumerate(OFFDIAG):
                value = g[128 * at : 128 * at + 128, :]
                put(128 * i, 128 * j, value)
                put(128 * j, 128 * i, value.T)
            for fold in range(2):
                at = FOLD_AT + 128 * fold
                value = g[at : at + 128, :]
                turned = value.T
                put(256 * fold, 256 * fold, jnp.where(row <= col, value, turned))
                line_at = TAIL_AT + TAIL * (2 * fold + 1) + rest
                diagonal = jnp.broadcast_to(g[line_at : line_at + 1, :], (128, 128))
                lower = jnp.where(row > col, value, jnp.where(row < col, turned, diagonal))
                put(256 * fold + 128, 256 * fold + 128, lower)
            for j in range(5):
                at = TAIL_AT + TAIL * j
                value = g[at : at + rest, :]
                put(512, 128 * j, value)
                if j < 4:
                    tall = jnp.concatenate([value, jnp.zeros((128 - rest, 128), F32)], axis=0)
                    put(128 * j, 512, tall.T)
            outs.append(dot(full[...], right[...]))
        even, odd = outs
        answers.append(
            jnp.where(left_lanes, even + pltpu.roll(even, SLOT, 1), odd + pltpu.roll(odd, SLOT, 1))
        )
    high, low = split(jnp.concatenate(answers, axis=1))
    gradient_ref[...] += dot(high, place) + dot(low, place)


def apply(owner, forward, swept, gathered):
    rows, cols = forward.shape
    whole = pl.BlockSpec((rows, cols), lambda i: (0, 0))
    pad = 640
    return pl.pallas_call(
        apply_kernel,
        grid=(8,),
        out_shape=(jax.ShapeDtypeStruct((rows, cols), F32), jax.ShapeDtypeStruct((rows, cols), F32)),
        in_specs=[
            pl.BlockSpec((1, cols), lambda i: (0, 0)),
            whole,
            whole,
            pl.BlockSpec((4, PACKED, 128), lambda i: (i, 0, 0)),
        ],
        out_specs=(whole, whole),
        scratch_shapes=[
            pltpu.VMEM((rows, cols), BF16),
            pltpu.VMEM((rows, cols), BF16),
            pltpu.VMEM((8, cols), F32),
            pltpu.VMEM((cols, 128), F32),
            pltpu.VMEM((rows, 2 * pad), BF16),
            pltpu.VMEM((2 * pad, 128), BF16),
        ],
        compiler_params=pltpu.CompilerParams(vmem_limit_bytes=60 * 1024 * 1024),
        name="apply",
    )(owner, forward, swept, gathered)


def body(search_one, search_two, column_gain, model_matrix, obs_owner, observe_matrix, error_weight, channel_mask):
    packed = pack(observe_matrix[0, 0], error_weight[0], channel_mask[0])
    forward, swept, gathered = sweep(
        search_one[0], search_two[0], column_gain[0], model_matrix[0], model_matrix[0].T, packed
    )
    state, gradient = apply(obs_owner, forward, swept, gathered)
    return state[None], gradient[None]


def solution(mesh):
    return jax.shard_map(
        body,
        mesh=mesh,
        in_specs=(
            P("tm", None, "region"),
            P("tm", None, "region"),
            P("tm", None, "region"),
            P("tm", None, None),
            P("tm", "region"),
            P("tm", "region", None, None),
            P("tm", "region", None),
            P("tm", "region", None),
        ),
        out_specs=(P("tm", None, "region"), P("tm", None, "region")),
        check_vma=False,
    )
```

```python
import jax
import jax.numpy as jnp
from jax import lax
from jax.experimental import pallas as pl
from jax.experimental.pallas import tpu as pltpu
from jax.sharding import PartitionSpec as P

F32 = jnp.float32
BF16 = jnp.bfloat16
MESH = pl.DeviceIdType.MESH

OFFDIAG = ((0, 1), (0, 2), (0, 3), (1, 2), (1, 3), (2, 3))
FOLD_AT = 768
TAIL_AT = 1024
TAIL = 40
PACKED = TAIL_AT + 5 * TAIL
HALVES = ((0, 616, 312), (616, 608, 304))
SLOT = 64
CHUNK = 128


def split(x):
    high = x.astype(BF16)
    return high, (x - high.astype(F32)).astype(BF16)


def dot(a, b):
    return jnp.dot(a, b, preferred_element_type=F32)


def dot_nt(a, b):
    return lax.dot_general(a, b, (((1,), (1,)), ((), ())), preferred_element_type=F32)


def form_packed(matrix, weight, out_ref):
    high, low = split(matrix)
    whigh, wlow = split(matrix * weight)

    def product(r0, r1, c0, c1):
        a, b = slice(r0, r1), slice(c0, c1)
        return dot_nt(whigh[a], high[b]) + (dot_nt(whigh[a], low[b]) + dot_nt(wlow[a], high[b]))

    top = product(0, 256, 0, 512)
    mid = product(256, 512, 256, 512)
    nv = matrix.shape[0]
    tail = product(512, nv, 0, nv)

    def block(i, j):
        if i < 2:
            return top[128 * i : 128 * i + 128, 128 * j : 128 * j + 128]
        return mid[128 * i - 256 : 128 * i - 128, 128 * j - 256 : 128 * j - 128]

    for at, (i, j) in enumerate(OFFDIAG):
        out_ref[128 * at : 128 * at + 128, :] = block(i, j)
    row = lax.broadcasted_iota(jnp.int32, (128, 128), 0)
    col = lax.broadcasted_iota(jnp.int32, (128, 128), 1)
    for pair in range(2):
        upper, lower = block(2 * pair, 2 * pair), block(2 * pair + 1, 2 * pair + 1)
        at = FOLD_AT + 128 * pair
        out_ref[at : at + 128, :] = jnp.where(row <= col, upper, lower)
    rest = nv - 512
    for j in range(5):
        at = TAIL_AT + TAIL * j
        if j < 4:
            out_ref[at : at + rest, :] = tail[:, 128 * j : 128 * j + 128]
            if j % 2 == 1:
                line = jnp.sum(jnp.where(row == col, block(j, j), 0.0), axis=0, keepdims=True)
            else:
                line = jnp.zeros((1, 128), F32)
            out_ref[at + rest : at + TAIL, :] = jnp.broadcast_to(line, (TAIL - rest, 128))
        else:
            out_ref[at : at + TAIL, :] = jnp.zeros((TAIL, 128), F32)
            out_ref[at : at + rest, 0:rest] = tail[:, 512:nv]


def sweep_kernel(
    one_hbm, two_hbm, gain_hbm, matrix_hbm, jacobian_hbm, error_ref, mask_ref,
    forward_out, swept_out, gathered_ref,
    one, two, gain, forward, swept, into_f, into_b, out_b, matrix, jacobian, packed_ref,
    m_high, m_low, t_high, t_low,
    load_sem, store_sem, matrix_sem, f_send, f_recv, b_send, b_recv, g_send, g_recv, p_send, p_recv, own_sem,
):
    k = lax.axis_index("tm")
    region = lax.axis_index("region")
    core = region % 2
    x = (region // 2) % 4
    z = region // 8
    chunks = into_f.shape[0]

    def chip(dz, dx):
        return ((z + dz + 4) % 4 * 4 + (x + dx + 4) % 4) * 2 + core

    partner = region + 1 - 2 * core

    def load(which, c):
        hbm, vmem = ((one_hbm, one), (two_hbm, two), (gain_hbm, gain))[which]
        return pltpu.make_async_copy(
            hbm.at[:, 0, pl.ds(c * CHUNK, CHUNK)], vmem.at[c], load_sem.at[which, c]
        )

    def load_at(which, c):
        hbm, vmem = ((one_hbm, one), (two_hbm, two), (gain_hbm, gain))[which]
        return pltpu.make_async_copy(
            hbm.at[:, 0, pl.ds(pl.multiple_of(c * CHUNK, CHUNK), CHUNK)], vmem.at[c], load_sem.at[which, c]
        )

    matrix_copy = pltpu.make_async_copy(matrix_hbm.at[:, 0, :], matrix, matrix_sem.at[0])
    jacobian_copy = pltpu.make_async_copy(jacobian_hbm.at[:, 0, :], jacobian, matrix_sem.at[1])
    load(0, 0).start()
    matrix_copy.start()
    load(1, 0).start()
    load(2, 0).start()
    jacobian_copy.start()
    for c in range(1, chunks):
        for which in range(3):
            load(which, c).start()

    def store_f(src, c):
        return pltpu.make_async_copy(src, forward_out.at[c], store_sem.at[0, c])

    def store_b(src, c):
        return pltpu.make_async_copy(src, swept_out.at[c], store_sem.at[1, c])

    barrier = pltpu.get_barrier_semaphore()
    around = [(k, chip(1, 0)), (k, chip(-1, 0)), (k, chip(0, 1)), (k, chip(0, -1)), (k, partner),
              ((k + 1) % 4, region), ((k + 3) % 4, region)]
    for who in around:
        pl.semaphore_signal(barrier, inc=1, device_id=who, device_id_type=MESH)
    pl.semaphore_wait(barrier, len(around))

    def send_f(src, c):
        return pltpu.make_async_remote_copy(
            src_ref=src, dst_ref=into_f.at[c], send_sem=f_send.at[c], recv_sem=f_recv.at[c],
            device_id=((k + 1) % 4, region), device_id_type=MESH,
        )

    def send_b(c):
        return pltpu.make_async_remote_copy(
            src_ref=out_b.at[c], dst_ref=into_b.at[c], send_sem=b_send.at[c], recv_sem=b_recv.at[c],
            device_id=((k + 3) % 4, region), device_id_type=MESH,
        )

    def step_to(primary, by):
        return chip(by, 0) if primary == "z" else chip(0, by)

    def block_at(half, dp, dq):
        if half == 0:
            return chip(dq, dp)
        return chip(dp, dq)

    axes = (("x", "z"), ("z", "x"))
    sends = []

    def relay(half, dp, dq, piece, axis, by):
        start, size, cut = HALVES[half]
        if piece == 0:
            start, size = start, cut
        elif piece == 1:
            start, size = start + cut, size - cut
        block = block_at(half, dp, dq)
        own = dp == 0 and dq == 0
        rows = pl.ds(start, size)
        number = len(sends)
        rp, rq = dp % 4, dq % 4
        if axis == axes[half][0]:
            rp = (dp - by) % 4
        else:
            rq = (dq - by) % 4
        copy = pltpu.make_async_remote_copy(
            src_ref=packed_ref.at[rows] if own else gathered_ref.at[block, rows],
            dst_ref=gathered_ref.at[block, rows],
            send_sem=g_send.at[number],
            recv_sem=g_recv.at[half, rp * 4 + rq, 1 if piece == 1 else 0],
            device_id=(k, step_to(axis, by)),
            device_id_type=MESH,
        )
        copy.start()
        sends.append(copy)

    def arrived(half, dp, dq, piece):
        start, size, cut = HALVES[half]
        if piece == 0:
            start, size = start, cut
        elif piece == 1:
            start, size = start + cut, size - cut
        block = block_at(half, dp, dq)
        ref = gathered_ref.at[block, pl.ds(start, size)]
        sem = g_recv.at[half, dp % 4 * 4 + dq % 4, 1 if piece == 1 else 0]
        pltpu.make_async_copy(ref, ref, sem).wait()

    shared = []

    def share(half, dp, dq):
        start, size, _ = HALVES[half]
        block = block_at(half, dp, dq)
        rows = pl.ds(start, size)
        own = dp == 0 and dq == 0
        at = dp % 4 * 4 + dq % 4
        copy = pltpu.make_async_remote_copy(
            src_ref=packed_ref.at[rows] if own else gathered_ref.at[block, rows],
            dst_ref=gathered_ref.at[block, rows],
            send_sem=p_send.at[half, at],
            recv_sem=p_recv.at[half, at],
            device_id=(k, partner),
            device_id_type=MESH,
        )
        copy.start()
        shared.append((half, dp, dq, copy))

    def first(half, by):
        main, other = axes[half]
        arrived(half, by, 0, None)
        relay(half, by, 0, 0 if by == -1 else 1, main, -by)
        relay(half, by, 0, None, other, 1)
        relay(half, by, 0, None, other, -1)
        share(half, by, 0)

    def opposite(half):
        _, other = axes[half]
        arrived(half, 2, 0, 0)
        arrived(half, 2, 0, 1)
        relay(half, 2, 0, None, other, 1)
        relay(half, 2, 0, None, other, -1)
        share(half, 2, 0)

    def second(half, dp, by):
        _, other = axes[half]
        arrived(half, dp, by, None)
        relay(half, dp, by, 0 if by == -1 else 1, other, -by)
        share(half, dp, by)

    def last(half, dp):
        arrived(half, dp, 2, 0)
        arrived(half, dp, 2, 1)
        share(half, dp, 2)

    @pl.when(k == 0)
    def _():
        for c in range(chunks):
            load(0, c).wait()
            send_f(one.at[c], c).start()
            store_f(one.at[c], c).start()

    matrix_copy.wait()
    high, low = split(matrix[...])
    m_high[...], m_low[...] = high, low
    high, low = split(matrix[...].T)
    t_high[...], t_low[...] = high, low

    def times(a_high, a_low, v):
        v_high, v_low = split(v)
        both = dot(a_high[...], jnp.concatenate([v_high, v_low], axis=1))
        return both[:, :CHUNK] + (both[:, CHUNK:] + dot(a_low[...], v_high))

    events = {
        1: [(first, 0, -1), (first, 1, -1), (first, 0, 1), (first, 1, 1)],
        3: [(second, 0, 0, -1), (second, 1, 0, -1), (second, 0, 0, 1), (second, 1, 0, 1)],
        4: [(opposite, 0), (opposite, 1)],
        5: [(second, 0, -1, -1), (second, 1, -1, -1), (second, 0, -1, 1), (second, 1, -1, 1)],
        6: [(second, 0, 1, -1), (second, 1, 1, -1), (second, 0, 1, 1), (second, 1, 1, 1)],
        7: [(last, 0, 0), (last, 1, 0)],
        8: [(second, 0, 2, -1), (second, 1, 2, -1), (second, 0, 2, 1), (second, 1, 2, 1)],
        9: [(last, 0, -1), (last, 1, -1), (last, 0, 1), (last, 1, 1)],
        10: [(last, 0, 2), (last, 1, 2)],
    }

    def tick(t, carry):
        cf = t - k

        @pl.when((cf >= 0) & (cf < chunks) & (k > 0))
        def _():
            load_at(0, cf).wait()

            @pl.when(k == 1)
            def _():
                load_at(2, cf).wait()

            send_f(into_f.at[cf], cf).wait_recv()
            forward[cf] = one[cf] + gain[cf] * times(m_high, m_low, into_f[cf])

            @pl.when(k < 3)
            def _():
                send_f(forward.at[cf], cf).start()

            store_f(forward.at[cf], cf).start()

        cb = t - (3 - k)

        @pl.when((cb >= 0) & (cb < chunks))
        def _():
            load_at(1, cb).wait()

            @pl.when(k != 1)
            def _():
                load_at(2, cb).wait()

            @pl.when(k < 3)
            def _():
                send_b(cb).wait_recv()
                swept[cb] = two[cb] + into_b[cb]

            @pl.when(k == 3)
            def _():
                swept[cb] = two[cb]

            @pl.when(k > 0)
            def _():
                out_b[cb] = times(t_high, t_low, gain[cb] * swept[cb])
                send_b(cb).start()

            store_b(swept.at[cb], cb).start()

        return carry

    lax.fori_loop(0, 1, tick, 0)
    jacobian_copy.wait()
    form_packed(jacobian[...], error_ref[...] * mask_ref[...].astype(F32), packed_ref)
    for half in range(2):
        main, _ = axes[half]
        relay(half, 0, 0, None, main, 1)
        relay(half, 0, 0, None, main, -1)
    for half in range(2):
        _, other = axes[half]
        relay(half, 0, 0, None, other, 1)
        relay(half, 0, 0, None, other, -1)
    for half in range(2):
        share(half, 0, 0)
    own_copy = pltpu.make_async_copy(packed_ref, gathered_ref.at[region], own_sem)
    own_copy.start()

    at = 1
    for tick_end in sorted(events):
        lax.fori_loop(at, tick_end + 1, tick, 0)
        at = tick_end + 1
        for event in events[tick_end]:
            event[0](*event[1:])
    lax.fori_loop(at, chunks + 3, tick, 0)

    for c in range(chunks):
        store_f(forward.at[c], c).wait()
        store_b(swept.at[c], c).wait()

    @pl.when(k < 3)
    def _():
        for c in range(chunks):
            send_f(into_f.at[c], c).wait_send()

    @pl.when(k > 0)
    def _():
        for c in range(chunks):
            send_b(c).wait_send()

    own_copy.wait()
    for copy in sends:
        copy.wait_send()
    for half, dp, dq, copy in shared:
        copy.wait_send()
        start, size, _ = HALVES[half]
        block = block_at(half, dp, dq) + 1 - 2 * core
        ref = gathered_ref.at[block, pl.ds(start, size)]
        pltpu.make_async_copy(ref, ref, p_recv.at[half, dp % 4 * 4 + dq % 4]).wait()


def sweep(one, two, gain, matrix, jacobian, error, mask):
    rows, _, cols = one.shape
    chunks = cols // CHUNK
    vmem = pl.BlockSpec(memory_space=pltpu.VMEM)
    hbm = pl.BlockSpec(memory_space=pl.ANY)
    chunked = (chunks, rows, CHUNK)
    square = (rows, rows)
    return pl.pallas_call(
        sweep_kernel,
        out_shape=(
            jax.ShapeDtypeStruct(chunked, F32),
            jax.ShapeDtypeStruct(chunked, F32),
            jax.ShapeDtypeStruct((32, PACKED, 128), F32),
        ),
        in_specs=[hbm] * 5 + [vmem] * 2,
        out_specs=(hbm, hbm, hbm),
        scratch_shapes=[pltpu.VMEM(chunked, F32)] * 8
        + [pltpu.VMEM(square, F32), pltpu.VMEM((rows, cols), F32), pltpu.VMEM((PACKED, 128), F32)]
        + [pltpu.VMEM(square, BF16)] * 4
        + [
            pltpu.SemaphoreType.DMA((3, chunks)),
            pltpu.SemaphoreType.DMA((2, chunks)),
            pltpu.SemaphoreType.DMA((2,)),
            pltpu.SemaphoreType.DMA((chunks,)),
            pltpu.SemaphoreType.DMA((chunks,)),
            pltpu.SemaphoreType.DMA((chunks,)),
            pltpu.SemaphoreType.DMA((chunks,)),
            pltpu.SemaphoreType.DMA((40,)),
            pltpu.SemaphoreType.DMA((2, 16, 2)),
            pltpu.SemaphoreType.DMA((2, 16)),
            pltpu.SemaphoreType.DMA((2, 16)),
            pltpu.SemaphoreType.DMA,
        ],
        compiler_params=pltpu.CompilerParams(
            collective_id=0, has_side_effects=True, vmem_limit_bytes=60 * 1024 * 1024
        ),
        name="sweep",
    )(one, two, gain, matrix, jacobian, error, mask)


def apply_kernel(
    owner_ref, forward_ref, swept_ref, gathered_ref,
    state_ref, gradient_ref,
    x_high, x_low, slot_row, slot_col, full, right, total,
):
    step = pl.program_id(0)
    rows, cols = total.shape
    chunks = cols // CHUNK
    pad = full.shape[1] // 2

    @pl.when(step == 0)
    def _():
        owner = owner_ref[...]
        onehot = (owner == lax.broadcasted_iota(jnp.int32, (32, cols), 0)).astype(F32)
        earlier = (
            lax.broadcasted_iota(jnp.int32, (cols, cols), 0) < lax.broadcasted_iota(jnp.int32, (cols, cols), 1)
        ).astype(F32)
        before = dot(onehot.astype(BF16), earlier.astype(BF16))
        placed = jnp.sum(before * onehot, axis=0, keepdims=True)
        slot = owner.astype(F32) * SLOT + placed
        slot_row[...] = jnp.broadcast_to(slot, slot_row.shape)
        slot_col[...] = jnp.broadcast_to(slot, (128, cols)).T
        for c in range(chunks):
            value = forward_ref[c]
            high, low = split(value)
            lanes = slice(c * CHUNK, (c + 1) * CHUNK)
            x_high[:, lanes], x_low[:, lanes] = high, low
            state_ref[:, c, :] = value
            total[:, lanes] = swept_ref[c]
        right[...] = jnp.zeros_like(right)
        full[...] = jnp.zeros_like(full)

    wide = 4 * SLOT
    base = (step * wide).astype(F32)
    lane = lax.broadcasted_iota(jnp.int32, (cols, 128), 1).astype(F32) + base
    pick = jnp.concatenate(
        [(slot_col[...] == lane).astype(BF16), (slot_col[...] == lane + 128.0).astype(BF16)], axis=1
    )
    line = lax.broadcasted_iota(jnp.int32, (wide, cols), 0).astype(F32) + base
    place = (jnp.broadcast_to(slot_row[0:1, :], (wide, cols)) == line).astype(BF16)
    s_high = dot(x_high[...], pick)
    s_low = dot(x_low[...], pick)

    row = lax.broadcasted_iota(jnp.int32, (128, 128), 0)
    col = lax.broadcasted_iota(jnp.int32, (128, 128), 1)
    left_lanes = lax.broadcasted_iota(jnp.int32, (rows, 128), 1) < SLOT
    rest = rows - 512

    def put(at_row, at_col, value):
        high, low = split(value)
        r, c = value.shape
        full[at_row : at_row + r, at_col : at_col + c] = high
        full[at_row : at_row + r, pad + at_col : pad + at_col + c] = low

    answers = []
    for pair in range(2):
        lanes = slice(128 * pair, 128 * pair + 128)
        high = s_high[:, lanes]
        low = pltpu.roll(s_low[:, lanes], SLOT, 1)
        outs = []
        for side in range(2):
            mine = left_lanes if side == 0 else jnp.logical_not(left_lanes)
            right[0:rows, :] = jnp.where(mine, high, low).astype(BF16)
            right[pad : pad + rows, :] = jnp.where(mine, high, 0.0).astype(BF16)
            g = gathered_ref.at[2 * pair + side]
            for at, (i, j) in enumerate(OFFDIAG):
                value = g[128 * at : 128 * at + 128, :]
                put(128 * i, 128 * j, value)
                put(128 * j, 128 * i, value.T)
            for fold in range(2):
                at = FOLD_AT + 128 * fold
                value = g[at : at + 128, :]
                turned = value.T
                put(256 * fold, 256 * fold, jnp.where(row <= col, value, turned))
                line_at = TAIL_AT + TAIL * (2 * fold + 1) + rest
                diagonal = jnp.broadcast_to(g[line_at : line_at + 1, :], (128, 128))
                lower = jnp.where(row > col, value, jnp.where(row < col, turned, diagonal))
                put(256 * fold + 128, 256 * fold + 128, lower)
            for j in range(5):
                at = TAIL_AT + TAIL * j
                value = g[at : at + rest, :]
                put(512, 128 * j, value)
                if j < 4:
                    tall = jnp.concatenate([value, jnp.zeros((128 - rest, 128), F32)], axis=0)
                    put(128 * j, 512, tall.T)
            outs.append(dot(full[...], right[...]))
        even, odd = outs
        answers.append(
            jnp.where(left_lanes, even + pltpu.roll(even, SLOT, 1), odd + pltpu.roll(odd, SLOT, 1))
        )
    high, low = split(jnp.concatenate(answers, axis=1))
    total[...] += dot(high, place) + dot(low, place)

    @pl.when(step == pl.num_programs(0) - 1)
    def _():
        for c in range(chunks):
            gradient_ref[:, c, :] = total[:, c * CHUNK : (c + 1) * CHUNK]


def apply(owner, forward, swept, gathered):
    chunks, rows, _ = forward.shape
    cols = chunks * CHUNK
    whole = pl.BlockSpec((chunks, rows, CHUNK), lambda i: (0, 0, 0))
    result = pl.BlockSpec((rows, chunks, CHUNK), lambda i: (0, 0, 0))
    pad = 640
    return pl.pallas_call(
        apply_kernel,
        grid=(8,),
        out_shape=(jax.ShapeDtypeStruct((rows, chunks, CHUNK), F32),) * 2,
        in_specs=[
            pl.BlockSpec((1, cols), lambda i: (0, 0)),
            whole,
            whole,
            pl.BlockSpec((4, PACKED, 128), lambda i: (i, 0, 0)),
        ],
        out_specs=(result, result),
        scratch_shapes=[
            pltpu.VMEM((rows, cols), BF16),
            pltpu.VMEM((rows, cols), BF16),
            pltpu.VMEM((8, cols), F32),
            pltpu.VMEM((cols, 128), F32),
            pltpu.VMEM((rows, 2 * pad), BF16),
            pltpu.VMEM((2 * pad, 128), BF16),
            pltpu.VMEM((rows, cols), F32),
        ],
        compiler_params=pltpu.CompilerParams(vmem_limit_bytes=60 * 1024 * 1024),
        name="apply",
    )(owner, forward, swept, gathered)


def by_row(x):
    return jnp.transpose(x, (1, 0, 2))


def body(search_one, search_two, column_gain, model_matrix, obs_owner, observe_matrix, error_weight, channel_mask):
    rows, cols = search_one.shape[1:]
    forward, swept, gathered = sweep(
        by_row(search_one), by_row(search_two), by_row(column_gain), by_row(model_matrix),
        by_row(observe_matrix[0]), error_weight[0], channel_mask[0],
    )
    state, gradient = apply(obs_owner, forward, swept, gathered)
    return tuple(by_row(out.reshape(rows, 1, cols)) for out in (state, gradient))


def solution(mesh):
    return jax.shard_map(
        body,
        mesh=mesh,
        in_specs=(
            P("tm", None, "region"),
            P("tm", None, "region"),
            P("tm", None, "region"),
            P("tm", None, None),
            P("tm", "region"),
            P("tm", "region", None, None),
            P("tm", "region", None),
            P("tm", "region", None),
        ),
        out_specs=(P("tm", None, "region"), P("tm", None, "region")),
        check_vma=False,
    )
```

```python
import jax
import jax.numpy as jnp
from jax import lax
from jax.experimental import pallas as pl
from jax.experimental.pallas import tpu as pltpu
from jax.sharding import PartitionSpec as P

F32 = jnp.float32
BF16 = jnp.bfloat16
MESH = pl.DeviceIdType.MESH

OFFDIAG = ((0, 1), (0, 2), (0, 3), (1, 2), (1, 3), (2, 3))
FOLD_AT = 768
TAIL_AT = 1024
TAIL = 40
PACKED = TAIL_AT + 5 * TAIL
HALVES = ((0, 616, 312), (616, 608, 304))
SLOT = 64
CHUNK = 128
FOLDED = 276


def split(x):
    high = x.astype(BF16)
    return high, (x - high.astype(F32)).astype(BF16)


def dot(a, b):
    return jnp.dot(a, b, preferred_element_type=F32)


def dot_nt(a, b):
    return lax.dot_general(a, b, (((1,), (1,)), ((), ())), preferred_element_type=F32)


def form_packed(matrix, weight, out_ref):
    high, low = split(matrix)
    whigh, wlow = split(matrix * weight)

    def product(r0, r1, c0, c1):
        a, b = slice(r0, r1), slice(c0, c1)
        return dot_nt(whigh[a], high[b]) + (dot_nt(whigh[a], low[b]) + dot_nt(wlow[a], high[b]))

    top = product(0, 256, 0, 512)
    mid = product(256, 512, 256, 512)
    nv = matrix.shape[0]
    tail = product(512, nv, 0, nv)

    def block(i, j):
        if i < 2:
            return top[128 * i : 128 * i + 128, 128 * j : 128 * j + 128]
        return mid[128 * i - 256 : 128 * i - 128, 128 * j - 256 : 128 * j - 128]

    for at, (i, j) in enumerate(OFFDIAG):
        out_ref[128 * at : 128 * at + 128, :] = block(i, j)
    row = lax.broadcasted_iota(jnp.int32, (128, 128), 0)
    col = lax.broadcasted_iota(jnp.int32, (128, 128), 1)
    for pair in range(2):
        upper, lower = block(2 * pair, 2 * pair), block(2 * pair + 1, 2 * pair + 1)
        at = FOLD_AT + 128 * pair
        out_ref[at : at + 128, :] = jnp.where(row <= col, upper, lower)
    rest = nv - 512
    for j in range(5):
        at = TAIL_AT + TAIL * j
        if j < 4:
            out_ref[at : at + rest, :] = tail[:, 128 * j : 128 * j + 128]
            if j % 2 == 1:
                line = jnp.sum(jnp.where(row == col, block(j, j), 0.0), axis=0, keepdims=True)
            else:
                line = jnp.zeros((1, 128), F32)
            out_ref[at + rest : at + TAIL, :] = jnp.broadcast_to(line, (TAIL - rest, 128))
        else:
            out_ref[at : at + TAIL, :] = jnp.zeros((TAIL, 128), F32)
            out_ref[at : at + rest, 0:rest] = tail[:, 512:nv]


def sweep_kernel(
    one_hbm, two_hbm, gain_hbm, matrix_hbm, jacobian_hbm, error_ref, mask_ref,
    forward_out, swept_out, gathered_ref,
    one, two, gain, forward, swept, into_f, into_b, out_f, out_b, matrix, jacobian, packed_ref,
    m_high, m_low, t_high, t_low,
    load_sem, store_sem, matrix_sem, f_send, f_recv, b_send, b_recv, g_send, g_recv, p_send, p_recv, own_sem,
):
    k = lax.axis_index("tm")
    region = lax.axis_index("region")
    core = region % 2
    x = (region // 2) % 4
    z = region // 8
    chunks, rows, _ = one.shape
    pieces = 2 * chunks
    cut = rows - FOLDED

    def chip(dz, dx):
        return ((z + dz + 4) % 4 * 4 + (x + dx + 4) % 4) * 2 + core

    partner = region + 1 - 2 * core

    def load(which, c):
        hbm, vmem = ((one_hbm, one), (two_hbm, two), (gain_hbm, gain))[which]
        return pltpu.make_async_copy(
            hbm.at[:, 0, pl.ds(c * CHUNK, CHUNK)], vmem.at[c], load_sem.at[which, c]
        )

    def load_at(which, c):
        hbm, vmem = ((one_hbm, one), (two_hbm, two), (gain_hbm, gain))[which]
        return pltpu.make_async_copy(
            hbm.at[:, 0, pl.ds(pl.multiple_of(c * CHUNK, CHUNK), CHUNK)], vmem.at[c], load_sem.at[which, c]
        )

    matrix_copy = pltpu.make_async_copy(matrix_hbm.at[:, 0, :], matrix, matrix_sem.at[0])
    jacobian_copy = pltpu.make_async_copy(jacobian_hbm.at[:, 0, :], jacobian, matrix_sem.at[1])
    load(0, 0).start()
    matrix_copy.start()
    load(1, 0).start()
    load(2, 0).start()
    jacobian_copy.start()
    for c in range(1, chunks):
        for which in range(3):
            load(which, c).start()

    def store_f(src, c):
        return pltpu.make_async_copy(src, forward_out.at[c], store_sem.at[0, c])

    def store_b(src, c):
        return pltpu.make_async_copy(src, swept_out.at[c], store_sem.at[1, c])

    barrier = pltpu.get_barrier_semaphore()
    around = [(k, chip(1, 0)), (k, chip(-1, 0)), (k, chip(0, 1)), (k, chip(0, -1)), (k, partner),
              ((k + 1) % 4, region), ((k + 3) % 4, region)]
    for who in around:
        pl.semaphore_signal(barrier, inc=1, device_id=who, device_id_type=MESH)
    pl.semaphore_wait(barrier, len(around))

    def send_f(s):
        return pltpu.make_async_remote_copy(
            src_ref=out_f.at[s], dst_ref=into_f.at[s], send_sem=f_send.at[s], recv_sem=f_recv.at[s],
            device_id=((k + 1) % 4, region), device_id_type=MESH,
        )

    def send_b(s):
        return pltpu.make_async_remote_copy(
            src_ref=out_b.at[s], dst_ref=into_b.at[s], send_sem=b_send.at[s], recv_sem=b_recv.at[s],
            device_id=((k + 3) % 4, region), device_id_type=MESH,
        )

    def step_to(primary, by):
        return chip(by, 0) if primary == "z" else chip(0, by)

    def block_at(half, dp, dq):
        if half == 0:
            return chip(dq, dp)
        return chip(dp, dq)

    axes = (("x", "z"), ("z", "x"))
    sends = []

    def span(half, piece):
        start, size, first_part = HALVES[half]
        if piece == 0:
            return start, first_part
        if piece == 1:
            return start + first_part, size - first_part
        return start, size

    def relay_copy(number, half, dp, dq, piece, axis, by):
        start, size = span(half, piece)
        block = block_at(half, dp, dq)
        own = dp == 0 and dq == 0
        place = pl.ds(start, size)
        rp, rq = dp % 4, dq % 4
        if axis == axes[half][0]:
            rp = (dp - by) % 4
        else:
            rq = (dq - by) % 4
        return pltpu.make_async_remote_copy(
            src_ref=packed_ref.at[place] if own else gathered_ref.at[block, place],
            dst_ref=gathered_ref.at[block, place],
            send_sem=g_send.at[number],
            recv_sem=g_recv.at[half, rp * 4 + rq, 1 if piece == 1 else 0],
            device_id=(k, step_to(axis, by)),
            device_id_type=MESH,
        )

    def relay(*what):
        relay_copy(len(sends), *what).start()
        sends.append(what)

    def arrived(half, dp, dq, piece):
        start, size = span(half, piece)
        block = block_at(half, dp, dq)
        ref = gathered_ref.at[block, pl.ds(start, size)]
        sem = g_recv.at[half, dp % 4 * 4 + dq % 4, 1 if piece == 1 else 0]
        pltpu.make_async_copy(ref, ref, sem).wait()

    shared = []

    def share_copy(half, dp, dq):
        start, size = span(half, None)
        block = block_at(half, dp, dq)
        place = pl.ds(start, size)
        own = dp == 0 and dq == 0
        at = dp % 4 * 4 + dq % 4
        return pltpu.make_async_remote_copy(
            src_ref=packed_ref.at[place] if own else gathered_ref.at[block, place],
            dst_ref=gathered_ref.at[block, place],
            send_sem=p_send.at[half, at],
            recv_sem=p_recv.at[half, at],
            device_id=(k, partner),
            device_id_type=MESH,
        )

    def share(*what):
        share_copy(*what).start()
        shared.append(what)

    def first(half, by):
        main, other = axes[half]
        arrived(half, by, 0, None)
        relay(half, by, 0, 0 if by == -1 else 1, main, -by)
        relay(half, by, 0, None, other, 1)
        relay(half, by, 0, None, other, -1)
        share(half, by, 0)

    def opposite(half):
        _, other = axes[half]
        arrived(half, 2, 0, 0)
        arrived(half, 2, 0, 1)
        relay(half, 2, 0, None, other, 1)
        relay(half, 2, 0, None, other, -1)
        share(half, 2, 0)

    def second(half, dp, by):
        _, other = axes[half]
        arrived(half, dp, by, None)
        relay(half, dp, by, 0 if by == -1 else 1, other, -by)
        share(half, dp, by)

    def last(half, dp):
        arrived(half, dp, 2, 0)
        arrived(half, dp, 2, 1)
        share(half, dp, 2)

    left = lax.broadcasted_iota(jnp.int32, (FOLDED, CHUNK), 1) < CHUNK // 2

    def fold(v, h):
        top = pltpu.roll(v[0:FOLDED], CHUNK // 2 * h, 1)
        low = pltpu.roll(v[cut:rows], CHUNK // 2 * (1 - h), 1)
        return jnp.where(left, top, low)

    def unfold(target, c, one_half, other_half, add):
        turned, returned = pltpu.roll(one_half, CHUNK // 2, 1), pltpu.roll(other_half, CHUNK // 2, 1)
        top, low = jnp.where(left, one_half, returned), jnp.where(left, turned, other_half)
        if add is not None:
            top, low = add[0:FOLDED] + top, add[cut:rows] + low
        target[c, 0:FOLDED, :] = top
        target[c, cut:rows, :] = low

    def times(a_high, a_low, v):
        high = v.astype(BF16).astype(F32)
        low = pltpu.roll(v - high, CHUNK // 2, 1)
        both = jnp.concatenate(
            [jnp.where(left, high, low)[0:cut].astype(BF16), jnp.where(left, low, high).astype(BF16)], axis=0
        )
        alone = jnp.concatenate(
            [jnp.where(left, high, 0.0)[0:cut].astype(BF16), jnp.where(left, 0.0, high).astype(BF16)], axis=0
        )
        total = dot(a_high[...], both) + dot(a_low[...], alone)
        total = total + pltpu.roll(total, CHUNK // 2, 1)
        return jnp.where(left, total[0:FOLDED], total[cut:rows])

    def leave(c):
        load_at(0, c).wait()
        value = one[c]
        for h in range(2):
            out_f[2 * c + h] = fold(value, h)
            send_f(2 * c + h).start()
        store_f(one.at[c], c).start()

    def prepare():
        matrix_copy.wait()
        value = matrix[...]
        m_high[...], m_low[...] = split(value)
        t_high[...], t_low[...] = split(value.T)

    def forward_step(s):
        c, h = s // 2, s % 2

        @pl.when(h == 0)
        def _():
            load_at(0, c).wait()

            @pl.when(k == 1)
            def _():
                load_at(2, c).wait()

        send_f(s).wait_recv()
        out_f[s] = fold(one[c], h) + fold(gain[c], h) * times(m_high, m_low, into_f[s])

        @pl.when(k < 3)
        def _():
            send_f(s).start()

        @pl.when(h == 1)
        def _():
            unfold(forward, c, out_f[s - 1], out_f[s], None)
            store_f(forward.at[c], c).start()

    def backward_step(s):
        c, h = s // 2, s % 2

        @pl.when(h == 0)
        def _():
            load_at(1, c).wait()

            @pl.when(k != 1)
            def _():
                load_at(2, c).wait()

        @pl.when(k < 3)
        def _():
            send_b(s).wait_recv()

        @pl.when(k == 3)
        def _():
            into_b[s] = jnp.zeros((FOLDED, CHUNK), F32)

        @pl.when(k > 0)
        def _():
            out_b[s] = times(t_high, t_low, fold(gain[c], h) * (fold(two[c], h) + into_b[s]))
            send_b(s).start()

        @pl.when(h == 1)
        def _():
            unfold(swept, c, into_b[s - 1], into_b[s], two[c])
            store_b(swept.at[c], c).start()

    @pl.when(k == 0)
    def _():
        leave(0)
        leave(1)

    @pl.when(k == 3)
    def _():
        prepare()
        backward_step(0)

    jacobian_copy.wait()
    form_packed(jacobian[...], error_ref[...] * mask_ref[...].astype(F32), packed_ref)
    for half in range(2):
        main, _ = axes[half]
        relay(half, 0, 0, None, main, 1)
        relay(half, 0, 0, None, main, -1)
    for half in range(2):
        _, other = axes[half]
        relay(half, 0, 0, None, other, 1)
        relay(half, 0, 0, None, other, -1)
    for half in range(2):
        share(half, 0, 0)
    own_copy = pltpu.make_async_copy(packed_ref, gathered_ref.at[region], own_sem)
    own_copy.start()

    @pl.when(k != 3)
    def _():
        prepare()

    events = {
        2: [(first, 0, -1), (first, 1, -1), (first, 0, 1), (first, 1, 1)],
        4: [(second, 0, 0, -1), (second, 1, 0, -1), (second, 0, 0, 1), (second, 1, 0, 1)],
        5: [(opposite, 0), (opposite, 1)],
        7: [(second, 0, -1, -1), (second, 1, -1, -1), (second, 0, -1, 1), (second, 1, -1, 1)],
        9: [(second, 0, 1, -1), (second, 1, 1, -1), (second, 0, 1, 1), (second, 1, 1, 1)],
        11: [(last, 0, 0), (last, 1, 0)],
        13: [(second, 0, 2, -1), (second, 1, 2, -1), (second, 0, 2, 1), (second, 1, 2, 1)],
        15: [(last, 0, -1), (last, 1, -1), (last, 0, 1), (last, 1, 1)],
        18: [(last, 0, 2), (last, 1, 2)],
    }

    def tick(t, carry):
        @pl.when((k == 0) & (t >= 1) & (t < chunks - 1))
        def _():
            leave(t + 1)

        cf = t - k

        @pl.when((cf >= 0) & (cf < pieces) & (k > 0))
        def _():
            forward_step(cf)

        cb = t - (3 - k)

        @pl.when((cb >= jnp.where(k == 3, 1, 0)) & (cb < pieces))
        def _():
            backward_step(cb)

        for when, what in events.items():

            @pl.when(t == when)
            def _():
                for event in what:
                    event[0](*event[1:])

        return carry

    lax.fori_loop(0, pieces + 3, tick, 0)

    for c in range(chunks):
        store_f(forward.at[c], c).wait()
        store_b(swept.at[c], c).wait()

    @pl.when(k < 3)
    def _():
        for s in range(pieces):
            send_f(s).wait_send()

    @pl.when(k > 0)
    def _():
        for s in range(pieces):
            send_b(s).wait_send()

    own_copy.wait()
    for number, what in enumerate(sends):
        relay_copy(number, *what).wait_send()
    for what in shared:
        share_copy(*what).wait_send()
        half, dp, dq = what
        start, size = span(half, None)
        block = block_at(half, dp, dq) + 1 - 2 * core
        ref = gathered_ref.at[block, pl.ds(start, size)]
        pltpu.make_async_copy(ref, ref, p_recv.at[half, dp % 4 * 4 + dq % 4]).wait()


def sweep(one, two, gain, matrix, jacobian, error, mask):
    rows, _, cols = one.shape
    chunks = cols // CHUNK
    vmem = pl.BlockSpec(memory_space=pltpu.VMEM)
    hbm = pl.BlockSpec(memory_space=pl.ANY)
    chunked = (chunks, rows, CHUNK)
    square = (rows, rows)
    return pl.pallas_call(
        sweep_kernel,
        out_shape=(
            jax.ShapeDtypeStruct(chunked, F32),
            jax.ShapeDtypeStruct(chunked, F32),
            jax.ShapeDtypeStruct((32, PACKED, 128), F32),
        ),
        in_specs=[hbm] * 5 + [vmem] * 2,
        out_specs=(hbm, hbm, hbm),
        scratch_shapes=[pltpu.VMEM(chunked, F32)] * 5
        + [pltpu.VMEM((2 * chunks, FOLDED, CHUNK), F32)] * 4
        + [pltpu.VMEM(square, F32), pltpu.VMEM((rows, cols), F32), pltpu.VMEM((PACKED, 128), F32)]
        + [pltpu.VMEM(square, BF16)] * 4
        + [
            pltpu.SemaphoreType.DMA((3, chunks)),
            pltpu.SemaphoreType.DMA((2, chunks)),
            pltpu.SemaphoreType.DMA((2,)),
            pltpu.SemaphoreType.DMA((2 * chunks,)),
            pltpu.SemaphoreType.DMA((2 * chunks,)),
            pltpu.SemaphoreType.DMA((2 * chunks,)),
            pltpu.SemaphoreType.DMA((2 * chunks,)),
            pltpu.SemaphoreType.DMA((40,)),
            pltpu.SemaphoreType.DMA((2, 16, 2)),
            pltpu.SemaphoreType.DMA((2, 16)),
            pltpu.SemaphoreType.DMA((2, 16)),
            pltpu.SemaphoreType.DMA,
        ],
        compiler_params=pltpu.CompilerParams(
            collective_id=0, has_side_effects=True, vmem_limit_bytes=60 * 1024 * 1024
        ),
        name="sweep",
    )(one, two, gain, matrix, jacobian, error, mask)


def apply_kernel(
    owner_ref, forward_hbm, swept_hbm, gathered_hbm,
    state_hbm, gradient_hbm,
    forward, swept, packed, x_high, x_low, slot_col, place, full, right, y_high, y_low,
    in_sem, packed_sem, out_sem,
):
    chunks, rows, _ = forward.shape
    groups, wide, cols = place.shape
    pad = full.shape[2] // 2
    depth = packed.shape[0]
    each = wide // SLOT
    load_f = [pltpu.make_async_copy(forward_hbm.at[c], forward.at[c], in_sem.at[0, c]) for c in range(chunks)]
    load_s = [pltpu.make_async_copy(swept_hbm.at[c], swept.at[c], in_sem.at[1, c]) for c in range(chunks)]

    def load_g(group, at):
        return pltpu.make_async_copy(
            gathered_hbm.at[pl.ds(group * each, each)], packed.at[at], packed_sem.at[at]
        )

    def store(source, target, which, c):
        return pltpu.make_async_copy(
            source.at[c], target.at[:, 0, pl.ds(c * CHUNK, CHUNK)], out_sem.at[which, c]
        )

    for copy in load_f:
        copy.start()
    for at in range(depth):
        load_g(at, at).start()
    for copy in load_s:
        copy.start()

    owner = owner_ref[...]
    onehot = (owner == lax.broadcasted_iota(jnp.int32, (32, cols), 0)).astype(F32)
    earlier = (
        lax.broadcasted_iota(jnp.int32, (cols, cols), 0) < lax.broadcasted_iota(jnp.int32, (cols, cols), 1)
    ).astype(BF16)
    before = dot(onehot.astype(BF16), earlier)
    placed = jnp.sum(before * onehot, axis=0, keepdims=True)
    slot = owner.astype(F32) * SLOT + placed
    slot_col[...] = jnp.broadcast_to(slot, (128, cols)).T
    line = lax.broadcasted_iota(jnp.int32, (wide, cols), 0).astype(F32)
    for group in range(groups):
        place[group] = (jnp.broadcast_to(slot - group * wide, (wide, cols)) == line).astype(BF16)
    right[...] = jnp.zeros_like(right)
    full[...] = jnp.zeros_like(full)

    for c in range(chunks):
        load_f[c].wait()
        lanes = slice(c * CHUNK, (c + 1) * CHUNK)
        x_high[:, lanes], x_low[:, lanes] = split(forward[c])
        store(forward, state_hbm, 0, c).start()

    row = lax.broadcasted_iota(jnp.int32, (128, 128), 0)
    col = lax.broadcasted_iota(jnp.int32, (128, 128), 1)
    left_lanes = lax.broadcasted_iota(jnp.int32, (rows, 128), 1) < SLOT
    rest = rows - 512

    def put(full, at_row, at_col, value):
        high, low = split(value)
        r, c = value.shape
        full[at_row : at_row + r, at_col : at_col + c] = high
        full[at_row : at_row + r, pad + at_col : pad + at_col + c] = low

    def unpack(g, full):
        for at, (i, j) in enumerate(OFFDIAG):
            value = g[128 * at : 128 * at + 128, :]
            put(full, 128 * i, 128 * j, value)
            put(full, 128 * j, 128 * i, value.T)
        for fold in range(2):
            at = FOLD_AT + 128 * fold
            value = g[at : at + 128, :]
            turned = value.T
            put(full, 256 * fold, 256 * fold, jnp.where(row <= col, value, turned))
            line_at = TAIL_AT + TAIL * (2 * fold + 1) + rest
            diagonal = jnp.broadcast_to(g[line_at : line_at + 1, :], (128, 128))
            lower = jnp.where(row > col, value, jnp.where(row < col, turned, diagonal))
            put(full, 256 * fold + 128, 256 * fold + 128, lower)
        for j in range(5):
            at = TAIL_AT + TAIL * j
            value = g[at : at + rest, :]
            put(full, 512, 128 * j, value)
            if j < 4:
                tall = jnp.concatenate([value, jnp.zeros((128 - rest, 128), F32)], axis=0)
                put(full, 128 * j, 512, tall.T)

    def one_group(group, carry):
        at = lax.rem(group, depth)
        base = (group * wide).astype(F32)
        lane = lax.broadcasted_iota(jnp.int32, (cols, 128), 1).astype(F32) + base
        pick = jnp.concatenate(
            [(slot_col[...] == lane).astype(BF16), (slot_col[...] == lane + 128.0).astype(BF16)], axis=1
        )
        s_high = dot(x_high[...], pick)
        s_low = dot(x_low[...], pick)
        load_g(group, at).wait()
        for pair in range(each // 2):
            lanes = slice(128 * pair, 128 * pair + 128)
            high = s_high[:, lanes]
            low = pltpu.roll(s_low[:, lanes], SLOT, 1)
            outs = []
            for side in range(2):
                mine = left_lanes if side == 0 else jnp.logical_not(left_lanes)
                right[side, 0:rows, :] = jnp.where(mine, high, low).astype(BF16)
                right[side, pad : pad + rows, :] = jnp.where(mine, high, 0.0).astype(BF16)
                unpack(packed.at[at, 2 * pair + side], full.at[side])
                outs.append(dot(full[side], right[side]))
            even, odd = outs
            answer = jnp.where(left_lanes, even + pltpu.roll(even, SLOT, 1), odd + pltpu.roll(odd, SLOT, 1))
            y_high[group, :, lanes], y_low[group, :, lanes] = split(answer)

        @pl.when(group + depth < groups)
        def _():
            load_g(group + depth, at).start()

        return carry

    lax.fori_loop(0, groups, one_group, 0)

    for c in range(chunks):
        load_s[c].wait()
    for tile in range(cols // 256):
        value = None
        lanes = slice(256 * tile, 256 * tile + 256)
        for group in range(groups):
            part = dot(y_high[group], place[group, :, lanes]) + dot(y_low[group], place[group, :, lanes])
            value = part if value is None else value + part
        for c in (2 * tile, 2 * tile + 1):
            swept[c] = swept[c] + value[:, (c % 2) * CHUNK : (c % 2 + 1) * CHUNK]
            store(swept, gradient_hbm, 1, c).start()
    for c in range(chunks):
        store(forward, state_hbm, 0, c).wait()
        store(swept, gradient_hbm, 1, c).wait()


def apply(owner, forward, swept, gathered):
    chunks, rows, _ = forward.shape
    cols = chunks * CHUNK
    hbm = pl.BlockSpec(memory_space=pl.ANY)
    pad = 640
    groups, wide, depth = 8, 4 * SLOT, 3
    return pl.pallas_call(
        apply_kernel,
        out_shape=(jax.ShapeDtypeStruct((rows, 1, cols), F32),) * 2,
        in_specs=[pl.BlockSpec(memory_space=pltpu.VMEM)] + [hbm] * 3,
        out_specs=(hbm, hbm),
        scratch_shapes=[
            pltpu.VMEM((chunks, rows, CHUNK), F32),
            pltpu.VMEM((chunks, rows, CHUNK), F32),
            pltpu.VMEM((depth, wide // SLOT, PACKED, 128), F32),
            pltpu.VMEM((rows, cols), BF16),
            pltpu.VMEM((rows, cols), BF16),
            pltpu.VMEM((cols, 128), F32),
            pltpu.VMEM((groups, wide, cols), BF16),
            pltpu.VMEM((2, rows, 2 * pad), BF16),
            pltpu.VMEM((2, 2 * pad, 128), BF16),
            pltpu.VMEM((groups, rows, wide), BF16),
            pltpu.VMEM((groups, rows, wide), BF16),
            pltpu.SemaphoreType.DMA((2, chunks)),
            pltpu.SemaphoreType.DMA((depth,)),
            pltpu.SemaphoreType.DMA((2, chunks)),
        ],
        compiler_params=pltpu.CompilerParams(vmem_limit_bytes=60 * 1024 * 1024),
        name="apply",
    )(owner, forward, swept, gathered)


def by_row(x):
    return jnp.transpose(x, (1, 0, 2))


def body(search_one, search_two, column_gain, model_matrix, obs_owner, observe_matrix, error_weight, channel_mask):
    forward, swept, gathered = sweep(
        by_row(search_one), by_row(search_two), by_row(column_gain), by_row(model_matrix),
        by_row(observe_matrix[0]), error_weight[0], channel_mask[0],
    )
    state, gradient = apply(obs_owner, forward, swept, gathered)
    return by_row(state), by_row(gradient)


def solution(mesh):
    return jax.shard_map(
        body,
        mesh=mesh,
        in_specs=(
            P("tm", None, "region"),
            P("tm", None, "region"),
            P("tm", None, "region"),
            P("tm", None, None),
            P("tm", "region"),
            P("tm", "region", None, None),
            P("tm", "region", None),
            P("tm", "region", None),
        ),
        out_specs=(P("tm", None, "region"), P("tm", None, "region")),
        check_vma=False,
    )
```

```python
import jax
import jax.numpy as jnp
from jax import lax
from jax.experimental import pallas as pl
from jax.experimental.pallas import tpu as pltpu
from jax.sharding import PartitionSpec as P

F32 = jnp.float32
BF16 = jnp.bfloat16
MESH = pl.DeviceIdType.MESH

OFFDIAG = ((0, 1), (0, 2), (0, 3), (1, 2), (1, 3), (2, 3))
FOLD_AT = 768
TAIL_AT = 1024
TAIL = 40
PACKED = TAIL_AT + 5 * TAIL
HALVES = ((0, 616, 312), (616, 608, 304))
SLOT = 64
CHUNK = 128
FOLDED = 276
LAG = 2


def split(x):
    high = x.astype(BF16)
    return high, (x - high.astype(F32)).astype(BF16)


def dot(a, b):
    return jnp.dot(a, b, preferred_element_type=F32)


def dot_nt(a, b):
    return lax.dot_general(a, b, (((1,), (1,)), ((), ())), preferred_element_type=F32)


def form_packed(matrix, weight, out_ref):
    high, low = split(matrix)
    whigh, wlow = split(matrix * weight)

    def product(r0, r1, c0, c1):
        a, b = slice(r0, r1), slice(c0, c1)
        return dot_nt(whigh[a], high[b]) + (dot_nt(whigh[a], low[b]) + dot_nt(wlow[a], high[b]))

    top = product(0, 256, 0, 512)
    mid = product(256, 512, 256, 512)
    nv = matrix.shape[0]
    tail = product(512, nv, 0, nv)

    def block(i, j):
        if i < 2:
            return top[128 * i : 128 * i + 128, 128 * j : 128 * j + 128]
        return mid[128 * i - 256 : 128 * i - 128, 128 * j - 256 : 128 * j - 128]

    for at, (i, j) in enumerate(OFFDIAG):
        out_ref[128 * at : 128 * at + 128, :] = block(i, j)
    row = lax.broadcasted_iota(jnp.int32, (128, 128), 0)
    col = lax.broadcasted_iota(jnp.int32, (128, 128), 1)
    for pair in range(2):
        upper, lower = block(2 * pair, 2 * pair), block(2 * pair + 1, 2 * pair + 1)
        at = FOLD_AT + 128 * pair
        out_ref[at : at + 128, :] = jnp.where(row <= col, upper, lower)
    rest = nv - 512
    for j in range(5):
        at = TAIL_AT + TAIL * j
        if j < 4:
            out_ref[at : at + rest, :] = tail[:, 128 * j : 128 * j + 128]
            if j % 2 == 1:
                line = jnp.sum(jnp.where(row == col, block(j, j), 0.0), axis=0, keepdims=True)
            else:
                line = jnp.zeros((1, 128), F32)
            out_ref[at + rest : at + TAIL, :] = jnp.broadcast_to(line, (TAIL - rest, 128))
        else:
            out_ref[at : at + TAIL, :] = jnp.zeros((TAIL, 128), F32)
            out_ref[at : at + rest, 0:rest] = tail[:, 512:nv]


def sweep_kernel(
    one_hbm, two_hbm, gain_hbm, matrix_hbm, jacobian_hbm, error_ref, mask_ref,
    forward_out, swept_out, gathered_ref,
    one, two, gain, forward, swept, into_f, into_b, out_f, out_b, matrix, jacobian, packed_ref,
    m_high, m_low, t_high, t_low,
    load_sem, store_sem, matrix_sem, f_send, f_recv, b_send, b_recv, g_send, g_recv, p_send, p_recv, own_sem,
):
    k = lax.axis_index("tm")
    region = lax.axis_index("region")
    core = region % 2
    x = (region // 2) % 4
    z = region // 8
    chunks, rows, _ = one.shape
    pieces = 2 * chunks
    cut = rows - FOLDED

    def chip(dz, dx):
        return ((z + dz + 4) % 4 * 4 + (x + dx + 4) % 4) * 2 + core

    partner = region + 1 - 2 * core

    def load(which, c):
        hbm, vmem = ((one_hbm, one), (two_hbm, two), (gain_hbm, gain))[which]
        return pltpu.make_async_copy(
            hbm.at[:, 0, pl.ds(c * CHUNK, CHUNK)], vmem.at[c], load_sem.at[which, c]
        )

    def load_at(which, c):
        hbm, vmem = ((one_hbm, one), (two_hbm, two), (gain_hbm, gain))[which]
        return pltpu.make_async_copy(
            hbm.at[:, 0, pl.ds(pl.multiple_of(c * CHUNK, CHUNK), CHUNK)], vmem.at[c], load_sem.at[which, c]
        )

    matrix_copy = pltpu.make_async_copy(matrix_hbm.at[:, 0, :], matrix, matrix_sem.at[0])
    jacobian_copy = pltpu.make_async_copy(jacobian_hbm.at[:, 0, :], jacobian, matrix_sem.at[1])
    load(0, 0).start()
    matrix_copy.start()
    load(1, 0).start()
    load(2, 0).start()
    jacobian_copy.start()
    for c in range(1, chunks):
        for which in range(3):
            load(which, c).start()

    def store_f(src, c):
        return pltpu.make_async_copy(src, forward_out.at[c], store_sem.at[0, c])

    def store_b(src, c):
        return pltpu.make_async_copy(src, swept_out.at[c], store_sem.at[1, c])

    barrier = pltpu.get_barrier_semaphore()
    around = [(k, chip(1, 0)), (k, chip(-1, 0)), (k, chip(0, 1)), (k, chip(0, -1)), (k, partner),
              ((k + 1) % 4, region), ((k + 3) % 4, region)]
    for who in around:
        pl.semaphore_signal(barrier, inc=1, device_id=who, device_id_type=MESH)
    pl.semaphore_wait(barrier, len(around))

    def send_f(s):
        return pltpu.make_async_remote_copy(
            src_ref=out_f.at[s], dst_ref=into_f.at[s], send_sem=f_send.at[s], recv_sem=f_recv.at[s],
            device_id=((k + 1) % 4, region), device_id_type=MESH,
        )

    def send_b(s):
        return pltpu.make_async_remote_copy(
            src_ref=out_b.at[s], dst_ref=into_b.at[s], send_sem=b_send.at[s], recv_sem=b_recv.at[s],
            device_id=((k + 3) % 4, region), device_id_type=MESH,
        )

    def step_to(primary, by):
        return chip(by, 0) if primary == "z" else chip(0, by)

    def block_at(half, dp, dq):
        if half == 0:
            return chip(dq, dp)
        return chip(dp, dq)

    axes = (("x", "z"), ("z", "x"))
    sends = []

    def span(half, piece):
        start, size, first_part = HALVES[half]
        if piece == 0:
            return start, first_part
        if piece == 1:
            return start + first_part, size - first_part
        return start, size

    def relay_copy(number, half, dp, dq, piece, axis, by):
        start, size = span(half, piece)
        block = block_at(half, dp, dq)
        own = dp == 0 and dq == 0
        place = pl.ds(start, size)
        rp, rq = dp % 4, dq % 4
        if axis == axes[half][0]:
            rp = (dp - by) % 4
        else:
            rq = (dq - by) % 4
        return pltpu.make_async_remote_copy(
            src_ref=packed_ref.at[place] if own else gathered_ref.at[block, place],
            dst_ref=gathered_ref.at[block, place],
            send_sem=g_send.at[number],
            recv_sem=g_recv.at[half, rp * 4 + rq, 1 if piece == 1 else 0],
            device_id=(k, step_to(axis, by)),
            device_id_type=MESH,
        )

    def relay(*what):
        relay_copy(len(sends), *what).start()
        sends.append(what)

    def arrived(half, dp, dq, piece):
        start, size = span(half, piece)
        block = block_at(half, dp, dq)
        ref = gathered_ref.at[block, pl.ds(start, size)]
        sem = g_recv.at[half, dp % 4 * 4 + dq % 4, 1 if piece == 1 else 0]
        pltpu.make_async_copy(ref, ref, sem).wait()

    shared = []

    def share_copy(half, dp, dq):
        start, size = span(half, None)
        block = block_at(half, dp, dq)
        place = pl.ds(start, size)
        own = dp == 0 and dq == 0
        at = dp % 4 * 4 + dq % 4
        return pltpu.make_async_remote_copy(
            src_ref=packed_ref.at[place] if own else gathered_ref.at[block, place],
            dst_ref=gathered_ref.at[block, place],
            send_sem=p_send.at[half, at],
            recv_sem=p_recv.at[half, at],
            device_id=(k, partner),
            device_id_type=MESH,
        )

    def share(*what):
        share_copy(*what).start()
        shared.append(what)

    def first(half, by):
        main, other = axes[half]
        arrived(half, by, 0, None)
        relay(half, by, 0, 0 if by == -1 else 1, main, -by)
        relay(half, by, 0, None, other, 1)
        relay(half, by, 0, None, other, -1)
        share(half, by, 0)

    def opposite(half):
        _, other = axes[half]
        arrived(half, 2, 0, 0)
        arrived(half, 2, 0, 1)
        relay(half, 2, 0, None, other, 1)
        relay(half, 2, 0, None, other, -1)
        share(half, 2, 0)

    def second(half, dp, by):
        _, other = axes[half]
        arrived(half, dp, by, None)
        relay(half, dp, by, 0 if by == -1 else 1, other, -by)
        share(half, dp, by)

    def last(half, dp):
        arrived(half, dp, 2, 0)
        arrived(half, dp, 2, 1)
        share(half, dp, 2)

    left = lax.broadcasted_iota(jnp.int32, (FOLDED, CHUNK), 1) < CHUNK // 2

    def fold(v, h):
        top = pltpu.roll(v[0:FOLDED], CHUNK // 2 * h, 1)
        low = pltpu.roll(v[cut:rows], CHUNK // 2 * (1 - h), 1)
        return jnp.where(left, top, low)

    def unfold(target, c, one_half, other_half, add):
        turned, returned = pltpu.roll(one_half, CHUNK // 2, 1), pltpu.roll(other_half, CHUNK // 2, 1)
        top, low = jnp.where(left, one_half, returned), jnp.where(left, turned, other_half)
        if add is not None:
            top, low = add[0:FOLDED] + top, add[cut:rows] + low
        target[c, 0:FOLDED, :] = top
        target[c, cut:rows, :] = low

    def times(a_high, a_low, v):
        high = v.astype(BF16).astype(F32)
        low = pltpu.roll(v - high, CHUNK // 2, 1)
        both = jnp.concatenate(
            [jnp.where(left, high, low)[0:cut].astype(BF16), jnp.where(left, low, high).astype(BF16)], axis=0
        )
        alone = jnp.concatenate(
            [jnp.where(left, high, 0.0)[0:cut].astype(BF16), jnp.where(left, 0.0, high).astype(BF16)], axis=0
        )
        total = dot(a_high[...], both) + dot(a_low[...], alone)
        total = total + pltpu.roll(total, CHUNK // 2, 1)
        return jnp.where(left, total[0:FOLDED], total[cut:rows])

    def leave(c):
        load_at(0, c).wait()
        value = one[c]
        for h in range(2):
            out_f[2 * c + h] = fold(value, h)
            send_f(2 * c + h).start()
        store_f(one.at[c], c).start()

    def prepare():
        matrix_copy.wait()
        value = matrix[...]
        m_high[...], m_low[...] = split(value)
        t_high[...], t_low[...] = split(value.T)

    def forward_step(s):
        c, h = s // 2, s % 2

        @pl.when(h == 0)
        def _():
            load_at(0, c).wait()

            @pl.when(k == 1)
            def _():
                load_at(2, c).wait()

        send_f(s).wait_recv()
        out_f[s] = fold(one[c], h) + fold(gain[c], h) * times(m_high, m_low, into_f[s])

        @pl.when(k < 3)
        def _():
            send_f(s).start()

        @pl.when(h == 1)
        def _():
            unfold(forward, c, out_f[s - 1], out_f[s], None)
            store_f(forward.at[c], c).start()

    def backward_step(s):
        c, h = s // 2, s % 2

        @pl.when(h == 0)
        def _():
            load_at(1, c).wait()

            @pl.when(k != 1)
            def _():
                load_at(2, c).wait()

        @pl.when(k < 3)
        def _():
            send_b(s).wait_recv()

        @pl.when(k == 3)
        def _():
            into_b[s] = jnp.zeros((FOLDED, CHUNK), F32)

        @pl.when(k > 0)
        def _():
            out_b[s] = times(t_high, t_low, fold(gain[c], h) * (fold(two[c], h) + into_b[s]))
            send_b(s).start()

        @pl.when(h == 1)
        def _():
            unfold(swept, c, into_b[s - 1], into_b[s], two[c])
            store_b(swept.at[c], c).start()

    @pl.when(k == 0)
    def _():
        leave(0)
        leave(1)

    @pl.when(k == 3)
    def _():
        prepare()
        backward_step(0)

    jacobian_copy.wait()
    form_packed(jacobian[...], error_ref[...] * mask_ref[...].astype(F32), packed_ref)
    for half in range(2):
        main, _ = axes[half]
        relay(half, 0, 0, None, main, 1)
        relay(half, 0, 0, None, main, -1)
    for half in range(2):
        _, other = axes[half]
        relay(half, 0, 0, None, other, 1)
        relay(half, 0, 0, None, other, -1)
    for half in range(2):
        share(half, 0, 0)
    own_copy = pltpu.make_async_copy(packed_ref, gathered_ref.at[region], own_sem)
    own_copy.start()

    @pl.when(k != 3)
    def _():
        prepare()

    events = {
        3: [(first, 0, -1), (first, 1, -1), (first, 0, 1), (first, 1, 1)],
        6: [(second, 0, 0, -1), (second, 1, 0, -1), (second, 0, 0, 1), (second, 1, 0, 1)],
        8: [(opposite, 0), (opposite, 1)],
        10: [(second, 0, -1, -1), (second, 1, -1, -1), (second, 0, -1, 1), (second, 1, -1, 1)],
        12: [(second, 0, 1, -1), (second, 1, 1, -1), (second, 0, 1, 1), (second, 1, 1, 1)],
        14: [(last, 0, 0), (last, 1, 0)],
        16: [(second, 0, 2, -1), (second, 1, 2, -1), (second, 0, 2, 1), (second, 1, 2, 1)],
        18: [(last, 0, -1), (last, 1, -1), (last, 0, 1), (last, 1, 1)],
        21: [(last, 0, 2), (last, 1, 2)],
    }

    def tick(t, carry):
        @pl.when((k == 0) & (t >= 1) & (t < chunks - 1))
        def _():
            leave(t + 1)

        cf = t - LAG * k

        @pl.when((cf >= 0) & (cf < pieces) & (k > 0))
        def _():
            forward_step(cf)

        cb = t - LAG * (3 - k)

        @pl.when((cb >= jnp.where(k == 3, 1, 0)) & (cb < pieces))
        def _():
            backward_step(cb)

        for when, what in events.items():

            @pl.when(t == when)
            def _():
                for event in what:
                    event[0](*event[1:])

        return carry

    lax.fori_loop(0, pieces + 3 * LAG, tick, 0)

    for c in range(chunks):
        store_f(forward.at[c], c).wait()
        store_b(swept.at[c], c).wait()

    @pl.when(k < 3)
    def _():
        for s in range(pieces):
            send_f(s).wait_send()

    @pl.when(k > 0)
    def _():
        for s in range(pieces):
            send_b(s).wait_send()

    own_copy.wait()
    for number, what in enumerate(sends):
        relay_copy(number, *what).wait_send()
    for what in shared:
        share_copy(*what).wait_send()
        half, dp, dq = what
        start, size = span(half, None)
        block = block_at(half, dp, dq) + 1 - 2 * core
        ref = gathered_ref.at[block, pl.ds(start, size)]
        pltpu.make_async_copy(ref, ref, p_recv.at[half, dp % 4 * 4 + dq % 4]).wait()


def sweep(one, two, gain, matrix, jacobian, error, mask):
    rows, _, cols = one.shape
    chunks = cols // CHUNK
    vmem = pl.BlockSpec(memory_space=pltpu.VMEM)
    hbm = pl.BlockSpec(memory_space=pl.ANY)
    chunked = (chunks, rows, CHUNK)
    square = (rows, rows)
    return pl.pallas_call(
        sweep_kernel,
        out_shape=(
            jax.ShapeDtypeStruct(chunked, F32),
            jax.ShapeDtypeStruct(chunked, F32),
            jax.ShapeDtypeStruct((32, PACKED, 128), F32),
        ),
        in_specs=[hbm] * 5 + [vmem] * 2,
        out_specs=(hbm, hbm, hbm),
        scratch_shapes=[pltpu.VMEM(chunked, F32)] * 5
        + [pltpu.VMEM((2 * chunks, FOLDED, CHUNK), F32)] * 4
        + [pltpu.VMEM(square, F32), pltpu.VMEM((rows, cols), F32), pltpu.VMEM((PACKED, 128), F32)]
        + [pltpu.VMEM(square, BF16)] * 4
        + [
            pltpu.SemaphoreType.DMA((3, chunks)),
            pltpu.SemaphoreType.DMA((2, chunks)),
            pltpu.SemaphoreType.DMA((2,)),
            pltpu.SemaphoreType.DMA((2 * chunks,)),
            pltpu.SemaphoreType.DMA((2 * chunks,)),
            pltpu.SemaphoreType.DMA((2 * chunks,)),
            pltpu.SemaphoreType.DMA((2 * chunks,)),
            pltpu.SemaphoreType.DMA((40,)),
            pltpu.SemaphoreType.DMA((2, 16, 2)),
            pltpu.SemaphoreType.DMA((2, 16)),
            pltpu.SemaphoreType.DMA((2, 16)),
            pltpu.SemaphoreType.DMA,
        ],
        compiler_params=pltpu.CompilerParams(
            collective_id=0, has_side_effects=True, vmem_limit_bytes=60 * 1024 * 1024
        ),
        name="sweep",
    )(one, two, gain, matrix, jacobian, error, mask)


def apply_kernel(
    owner_ref, forward_hbm, swept_hbm, gathered_hbm,
    state_hbm, gradient_hbm,
    forward, swept, packed, x_high, x_low, slot_col, place, full, right, y_high, y_low,
    in_sem, packed_sem, out_sem,
):
    chunks, rows, _ = forward.shape
    groups, wide, cols = place.shape
    pad = full.shape[2] // 2
    depth = packed.shape[0]
    each = wide // SLOT
    load_f = [pltpu.make_async_copy(forward_hbm.at[c], forward.at[c], in_sem.at[0, c]) for c in range(chunks)]
    load_s = [pltpu.make_async_copy(swept_hbm.at[c], swept.at[c], in_sem.at[1, c]) for c in range(chunks)]

    def load_g(group, at):
        return pltpu.make_async_copy(
            gathered_hbm.at[pl.ds(group * each, each)], packed.at[at], packed_sem.at[at]
        )

    def store(source, target, which, c):
        return pltpu.make_async_copy(
            source.at[c], target.at[:, 0, pl.ds(c * CHUNK, CHUNK)], out_sem.at[which, c]
        )

    for copy in load_f:
        copy.start()
    for at in range(depth):
        load_g(at, at).start()
    for copy in load_s:
        copy.start()

    owner = owner_ref[...]
    onehot = (owner == lax.broadcasted_iota(jnp.int32, (32, cols), 0)).astype(F32)
    earlier = (
        lax.broadcasted_iota(jnp.int32, (cols, cols), 0) < lax.broadcasted_iota(jnp.int32, (cols, cols), 1)
    ).astype(BF16)
    before = dot(onehot.astype(BF16), earlier)
    placed = jnp.sum(before * onehot, axis=0, keepdims=True)
    slot = owner.astype(F32) * SLOT + placed
    slot_col[...] = jnp.broadcast_to(slot, (128, cols)).T
    line = lax.broadcasted_iota(jnp.int32, (wide, cols), 0).astype(F32)
    for group in range(groups):
        place[group] = (jnp.broadcast_to(slot - group * wide, (wide, cols)) == line).astype(BF16)
    right[...] = jnp.zeros_like(right)
    full[...] = jnp.zeros_like(full)

    for c in range(chunks):
        load_f[c].wait()
        lanes = slice(c * CHUNK, (c + 1) * CHUNK)
        x_high[:, lanes], x_low[:, lanes] = split(forward[c])
        store(forward, state_hbm, 0, c).start()

    row = lax.broadcasted_iota(jnp.int32, (128, 128), 0)
    col = lax.broadcasted_iota(jnp.int32, (128, 128), 1)
    left_lanes = lax.broadcasted_iota(jnp.int32, (rows, 128), 1) < SLOT
    rest = rows - 512

    def put(full, at_row, at_col, value):
        high, low = split(value)
        r, c = value.shape
        full[at_row : at_row + r, at_col : at_col + c] = high
        full[at_row : at_row + r, pad + at_col : pad + at_col + c] = low

    def unpack(g, full):
        for at, (i, j) in enumerate(OFFDIAG):
            value = g[128 * at : 128 * at + 128, :]
            put(full, 128 * i, 128 * j, value)
            put(full, 128 * j, 128 * i, value.T)
        for fold in range(2):
            at = FOLD_AT + 128 * fold
            value = g[at : at + 128, :]
            turned = value.T
            put(full, 256 * fold, 256 * fold, jnp.where(row <= col, value, turned))
            line_at = TAIL_AT + TAIL * (2 * fold + 1) + rest
            diagonal = jnp.broadcast_to(g[line_at : line_at + 1, :], (128, 128))
            lower = jnp.where(row > col, value, jnp.where(row < col, turned, diagonal))
            put(full, 256 * fold + 128, 256 * fold + 128, lower)
        for j in range(5):
            at = TAIL_AT + TAIL * j
            value = g[at : at + rest, :]
            put(full, 512, 128 * j, value)
            if j < 4:
                tall = jnp.concatenate([value, jnp.zeros((128 - rest, 128), F32)], axis=0)
                put(full, 128 * j, 512, tall.T)

    def one_group(group, carry):
        at = lax.rem(group, depth)
        base = (group * wide).astype(F32)
        lane = lax.broadcasted_iota(jnp.int32, (cols, 128), 1).astype(F32) + base
        pick = jnp.concatenate(
            [(slot_col[...] == lane).astype(BF16), (slot_col[...] == lane + 128.0).astype(BF16)], axis=1
        )
        s_high = dot(x_high[...], pick)
        s_low = dot(x_low[...], pick)
        load_g(group, at).wait()
        for pair in range(each // 2):
            lanes = slice(128 * pair, 128 * pair + 128)
            high = s_high[:, lanes]
            low = pltpu.roll(s_low[:, lanes], SLOT, 1)
            outs = []
            for side in range(2):
                mine = left_lanes if side == 0 else jnp.logical_not(left_lanes)
                right[side, 0:rows, :] = jnp.where(mine, high, low).astype(BF16)
                right[side, pad : pad + rows, :] = jnp.where(mine, high, 0.0).astype(BF16)
                unpack(packed.at[at, 2 * pair + side], full.at[side])
                outs.append(dot(full[side], right[side]))
            even, odd = outs
            answer = jnp.where(left_lanes, even + pltpu.roll(even, SLOT, 1), odd + pltpu.roll(odd, SLOT, 1))
            y_high[group, :, lanes], y_low[group, :, lanes] = split(answer)

        @pl.when(group + depth < groups)
        def _():
            load_g(group + depth, at).start()

        return carry

    lax.fori_loop(0, groups, one_group, 0)

    for c in range(chunks):
        load_s[c].wait()
    for tile in range(cols // 256):
        value = None
        lanes = slice(256 * tile, 256 * tile + 256)
        for group in range(groups):
            part = dot(y_high[group], place[group, :, lanes]) + dot(y_low[group], place[group, :, lanes])
            value = part if value is None else value + part
        for c in (2 * tile, 2 * tile + 1):
            swept[c] = swept[c] + value[:, (c % 2) * CHUNK : (c % 2 + 1) * CHUNK]
            store(swept, gradient_hbm, 1, c).start()
    for c in range(chunks):
        store(forward, state_hbm, 0, c).wait()
        store(swept, gradient_hbm, 1, c).wait()


def apply(owner, forward, swept, gathered):
    chunks, rows, _ = forward.shape
    cols = chunks * CHUNK
    hbm = pl.BlockSpec(memory_space=pl.ANY)
    pad = 640
    groups, wide, depth = 8, 4 * SLOT, 3
    return pl.pallas_call(
        apply_kernel,
        out_shape=(jax.ShapeDtypeStruct((rows, 1, cols), F32),) * 2,
        in_specs=[pl.BlockSpec(memory_space=pltpu.VMEM)] + [hbm] * 3,
        out_specs=(hbm, hbm),
        scratch_shapes=[
            pltpu.VMEM((chunks, rows, CHUNK), F32),
            pltpu.VMEM((chunks, rows, CHUNK), F32),
            pltpu.VMEM((depth, wide // SLOT, PACKED, 128), F32),
            pltpu.VMEM((rows, cols), BF16),
            pltpu.VMEM((rows, cols), BF16),
            pltpu.VMEM((cols, 128), F32),
            pltpu.VMEM((groups, wide, cols), BF16),
            pltpu.VMEM((2, rows, 2 * pad), BF16),
            pltpu.VMEM((2, 2 * pad, 128), BF16),
            pltpu.VMEM((groups, rows, wide), BF16),
            pltpu.VMEM((groups, rows, wide), BF16),
            pltpu.SemaphoreType.DMA((2, chunks)),
            pltpu.SemaphoreType.DMA((depth,)),
            pltpu.SemaphoreType.DMA((2, chunks)),
        ],
        compiler_params=pltpu.CompilerParams(vmem_limit_bytes=60 * 1024 * 1024),
        name="apply",
    )(owner, forward, swept, gathered)


def by_row(x):
    return jnp.transpose(x, (1, 0, 2))


def body(search_one, search_two, column_gain, model_matrix, obs_owner, observe_matrix, error_weight, channel_mask):
    forward, swept, gathered = sweep(
        by_row(search_one), by_row(search_two), by_row(column_gain), by_row(model_matrix),
        by_row(observe_matrix[0]), error_weight[0], channel_mask[0],
    )
    state, gradient = apply(obs_owner, forward, swept, gathered)
    return by_row(state), by_row(gradient)


def solution(mesh):
    return jax.shard_map(
        body,
        mesh=mesh,
        in_specs=(
            P("tm", None, "region"),
            P("tm", None, "region"),
            P("tm", None, "region"),
            P("tm", None, None),
            P("tm", "region"),
            P("tm", "region", None, None),
            P("tm", "region", None),
            P("tm", "region", None),
        ),
        out_specs=(P("tm", None, "region"), P("tm", None, "region")),
        check_vma=False,
    )
```

```python
import jax
import jax.numpy as jnp
from jax import lax
from jax.experimental import pallas as pl
from jax.experimental.pallas import tpu as pltpu
from jax.sharding import PartitionSpec as P

F32 = jnp.float32
BF16 = jnp.bfloat16
MESH = pl.DeviceIdType.MESH

OFFDIAG = ((0, 1), (0, 2), (0, 3), (1, 2), (1, 3), (2, 3))
FOLD_AT = 768
TAIL_AT = 1024
TAIL = 40
PACKED = TAIL_AT + 5 * TAIL
HALVES = ((0, 616, 312), (616, 608, 304))
SLOT = 64
CHUNK = 128
FOLDED = 276
LAG = 2


def split(x):
    high = x.astype(BF16)
    return high, (x - high.astype(F32)).astype(BF16)


def dot(a, b):
    return jnp.dot(a, b, preferred_element_type=F32)


def dot_nt(a, b):
    return lax.dot_general(a, b, (((1,), (1,)), ((), ())), preferred_element_type=F32)


def form_packed(matrix, weight, out_ref, depart):
    high, low = split(matrix)
    whigh, wlow = split(matrix * weight)

    def product(r0, r1, c0, c1):
        a, b = slice(r0, r1), slice(c0, c1)
        return dot_nt(whigh[a], high[b]) + (dot_nt(whigh[a], low[b]) + dot_nt(wlow[a], high[b]))

    nv = matrix.shape[0]
    rest = nv - 512
    row = lax.broadcasted_iota(jnp.int32, (128, 128), 0)
    col = lax.broadcasted_iota(jnp.int32, (128, 128), 1)
    top = product(0, 256, 0, 512)

    def block(i, j):
        if i < 2:
            return top[128 * i : 128 * i + 128, 128 * j : 128 * j + 128]
        return mid[128 * i - 256 : 128 * i - 128, 128 * j - 256 : 128 * j - 128]

    for at, (i, j) in enumerate(OFFDIAG[:5]):
        out_ref[128 * at : 128 * at + 128, :] = block(i, j)
    depart(0)
    mid = product(256, 512, 256, 512)
    tail = product(512, nv, 0, nv)
    out_ref[640:FOLD_AT, :] = block(2, 3)
    for pair in range(2):
        upper, lower = block(2 * pair, 2 * pair), block(2 * pair + 1, 2 * pair + 1)
        at = FOLD_AT + 128 * pair
        out_ref[at : at + 128, :] = jnp.where(row <= col, upper, lower)
    for j in range(5):
        at = TAIL_AT + TAIL * j
        if j < 4:
            out_ref[at : at + rest, :] = tail[:, 128 * j : 128 * j + 128]
            if j % 2 == 1:
                line = jnp.sum(jnp.where(row == col, block(j, j), 0.0), axis=0, keepdims=True)
            else:
                line = jnp.zeros((1, 128), F32)
            out_ref[at + rest : at + TAIL, :] = jnp.broadcast_to(line, (TAIL - rest, 128))
        else:
            out_ref[at : at + TAIL, :] = jnp.zeros((TAIL, 128), F32)
            out_ref[at : at + rest, 0:rest] = tail[:, 512:nv]
    depart(1)


def sweep_kernel(
    one_hbm, two_hbm, gain_hbm, matrix_hbm, jacobian_hbm, error_ref, mask_ref,
    forward_out, swept_out, gathered_ref,
    one, two, gain, forward, swept, into_f, into_b, out_f, out_b, matrix, jacobian, packed_ref,
    m_high, m_low, t_high, t_low,
    load_sem, store_sem, matrix_sem, f_send, f_recv, b_send, b_recv, g_send, g_recv, p_send, p_recv, own_sem,
):
    k = lax.axis_index("tm")
    region = lax.axis_index("region")
    core = region % 2
    x = (region // 2) % 4
    z = region // 8
    chunks, rows, _ = one.shape
    pieces = 2 * chunks
    cut = rows - FOLDED

    def chip(dz, dx):
        return ((z + dz + 4) % 4 * 4 + (x + dx + 4) % 4) * 2 + core

    partner = region + 1 - 2 * core

    def load(which, c):
        hbm, vmem = ((one_hbm, one), (two_hbm, two), (gain_hbm, gain))[which]
        return pltpu.make_async_copy(
            hbm.at[:, 0, pl.ds(c * CHUNK, CHUNK)], vmem.at[c], load_sem.at[which, c]
        )

    def load_at(which, c):
        hbm, vmem = ((one_hbm, one), (two_hbm, two), (gain_hbm, gain))[which]
        return pltpu.make_async_copy(
            hbm.at[:, 0, pl.ds(pl.multiple_of(c * CHUNK, CHUNK), CHUNK)], vmem.at[c], load_sem.at[which, c]
        )

    matrix_copy = pltpu.make_async_copy(matrix_hbm.at[:, 0, :], matrix, matrix_sem.at[0])
    jacobian_copy = pltpu.make_async_copy(jacobian_hbm.at[:, 0, :], jacobian, matrix_sem.at[1])
    load(0, 0).start()
    matrix_copy.start()
    load(1, 0).start()
    load(2, 0).start()
    jacobian_copy.start()
    for c in range(1, chunks):
        for which in range(3):
            load(which, c).start()

    def store_f(src, c):
        return pltpu.make_async_copy(src, forward_out.at[c], store_sem.at[0, c])

    def store_b(src, c):
        return pltpu.make_async_copy(src, swept_out.at[c], store_sem.at[1, c])

    barrier = pltpu.get_barrier_semaphore()
    around = [(k, chip(1, 0)), (k, chip(-1, 0)), (k, chip(0, 1)), (k, chip(0, -1)), (k, partner),
              ((k + 1) % 4, region), ((k + 3) % 4, region)]
    for who in around:
        pl.semaphore_signal(barrier, inc=1, device_id=who, device_id_type=MESH)
    pl.semaphore_wait(barrier, len(around))

    def send_f(s):
        return pltpu.make_async_remote_copy(
            src_ref=out_f.at[s], dst_ref=into_f.at[s], send_sem=f_send.at[s], recv_sem=f_recv.at[s],
            device_id=((k + 1) % 4, region), device_id_type=MESH,
        )

    def send_b(s):
        return pltpu.make_async_remote_copy(
            src_ref=out_b.at[s], dst_ref=into_b.at[s], send_sem=b_send.at[s], recv_sem=b_recv.at[s],
            device_id=((k + 3) % 4, region), device_id_type=MESH,
        )

    def step_to(primary, by):
        return chip(by, 0) if primary == "z" else chip(0, by)

    def block_at(half, dp, dq):
        if half == 0:
            return chip(dq, dp)
        return chip(dp, dq)

    axes = (("x", "z"), ("z", "x"))
    sends = []

    def span(half, piece):
        start, size, first_part = HALVES[half]
        if piece == 0:
            return start, first_part
        if piece == 1:
            return start + first_part, size - first_part
        return start, size

    def relay_copy(number, half, dp, dq, piece, axis, by):
        start, size = span(half, piece)
        block = block_at(half, dp, dq)
        own = dp == 0 and dq == 0
        place = pl.ds(start, size)
        rp, rq = dp % 4, dq % 4
        if axis == axes[half][0]:
            rp = (dp - by) % 4
        else:
            rq = (dq - by) % 4
        return pltpu.make_async_remote_copy(
            src_ref=packed_ref.at[place] if own else gathered_ref.at[block, place],
            dst_ref=gathered_ref.at[block, place],
            send_sem=g_send.at[number],
            recv_sem=g_recv.at[half, rp * 4 + rq, 1 if piece == 1 else 0],
            device_id=(k, step_to(axis, by)),
            device_id_type=MESH,
        )

    def relay(*what):
        relay_copy(len(sends), *what).start()
        sends.append(what)

    def arrived(half, dp, dq, piece):
        start, size = span(half, piece)
        block = block_at(half, dp, dq)
        ref = gathered_ref.at[block, pl.ds(start, size)]
        sem = g_recv.at[half, dp % 4 * 4 + dq % 4, 1 if piece == 1 else 0]
        pltpu.make_async_copy(ref, ref, sem).wait()

    shared = []

    def share_copy(half, dp, dq):
        start, size = span(half, None)
        block = block_at(half, dp, dq)
        place = pl.ds(start, size)
        own = dp == 0 and dq == 0
        at = dp % 4 * 4 + dq % 4
        return pltpu.make_async_remote_copy(
            src_ref=packed_ref.at[place] if own else gathered_ref.at[block, place],
            dst_ref=gathered_ref.at[block, place],
            send_sem=p_send.at[half, at],
            recv_sem=p_recv.at[half, at],
            device_id=(k, partner),
            device_id_type=MESH,
        )

    def share(*what):
        share_copy(*what).start()
        shared.append(what)

    def first(half, by):
        main, other = axes[half]
        arrived(half, by, 0, None)
        relay(half, by, 0, 0 if by == -1 else 1, main, -by)
        relay(half, by, 0, None, other, 1)
        relay(half, by, 0, None, other, -1)
        share(half, by, 0)

    def opposite(half):
        _, other = axes[half]
        arrived(half, 2, 0, 0)
        arrived(half, 2, 0, 1)
        relay(half, 2, 0, None, other, 1)
        relay(half, 2, 0, None, other, -1)
        share(half, 2, 0)

    def second(half, dp, by):
        _, other = axes[half]
        arrived(half, dp, by, None)
        relay(half, dp, by, 0 if by == -1 else 1, other, -by)
        share(half, dp, by)

    def last(half, dp):
        arrived(half, dp, 2, 0)
        arrived(half, dp, 2, 1)
        share(half, dp, 2)

    left = lax.broadcasted_iota(jnp.int32, (FOLDED, CHUNK), 1) < CHUNK // 2

    def fold(v, h):
        top = pltpu.roll(v[0:FOLDED], CHUNK // 2 * h, 1)
        low = pltpu.roll(v[cut:rows], CHUNK // 2 * (1 - h), 1)
        return jnp.where(left, top, low)

    def unfold(target, c, one_half, other_half, add):
        turned, returned = pltpu.roll(one_half, CHUNK // 2, 1), pltpu.roll(other_half, CHUNK // 2, 1)
        top, low = jnp.where(left, one_half, returned), jnp.where(left, turned, other_half)
        if add is not None:
            top, low = add[0:FOLDED] + top, add[cut:rows] + low
        target[c, 0:FOLDED, :] = top
        target[c, cut:rows, :] = low

    def times(a_high, a_low, v):
        high = v.astype(BF16).astype(F32)
        low = pltpu.roll(v - high, CHUNK // 2, 1)
        both = jnp.concatenate(
            [jnp.where(left, high, low)[0:cut].astype(BF16), jnp.where(left, low, high).astype(BF16)], axis=0
        )
        alone = jnp.concatenate(
            [jnp.where(left, high, 0.0)[0:cut].astype(BF16), jnp.where(left, 0.0, high).astype(BF16)], axis=0
        )
        total = dot(a_high[...], both) + dot(a_low[...], alone)
        total = total + pltpu.roll(total, CHUNK // 2, 1)
        return jnp.where(left, total[0:FOLDED], total[cut:rows])

    def leave(c):
        load_at(0, c).wait()
        value = one[c]
        for h in range(2):
            out_f[2 * c + h] = fold(value, h)
            send_f(2 * c + h).start()
        store_f(one.at[c], c).start()

    def prepare():
        matrix_copy.wait()
        value = matrix[...]
        m_high[...], m_low[...] = split(value)
        t_high[...], t_low[...] = split(value.T)

    def forward_step(s):
        c, h = s // 2, s % 2

        @pl.when(h == 0)
        def _():
            load_at(0, c).wait()

            @pl.when(k == 1)
            def _():
                load_at(2, c).wait()

        send_f(s).wait_recv()
        out_f[s] = fold(one[c], h) + fold(gain[c], h) * times(m_high, m_low, into_f[s])

        @pl.when(k < 3)
        def _():
            send_f(s).start()

        @pl.when(h == 1)
        def _():
            unfold(forward, c, out_f[s - 1], out_f[s], None)
            store_f(forward.at[c], c).start()

    def backward_step(s):
        c, h = s // 2, s % 2

        @pl.when(h == 0)
        def _():
            load_at(1, c).wait()

            @pl.when(k != 1)
            def _():
                load_at(2, c).wait()

        @pl.when(k < 3)
        def _():
            send_b(s).wait_recv()

        @pl.when(k == 3)
        def _():
            into_b[s] = jnp.zeros((FOLDED, CHUNK), F32)

        @pl.when(k > 0)
        def _():
            out_b[s] = times(t_high, t_low, fold(gain[c], h) * (fold(two[c], h) + into_b[s]))
            send_b(s).start()

        @pl.when(h == 1)
        def _():
            unfold(swept, c, into_b[s - 1], into_b[s], two[c])
            store_b(swept.at[c], c).start()

    @pl.when(k == 0)
    def _():
        leave(0)
        leave(1)

    prepare()

    @pl.when(k == 3)
    def _():
        backward_step(0)

    def depart(half):
        main, other = axes[half]
        for axis in (main, other):
            relay(half, 0, 0, None, axis, 1)
            relay(half, 0, 0, None, axis, -1)
        share(half, 0, 0)

    jacobian_copy.wait()
    form_packed(jacobian[...], error_ref[...] * mask_ref[...].astype(F32), packed_ref, depart)
    own_copy = pltpu.make_async_copy(packed_ref, gathered_ref.at[region], own_sem)
    own_copy.start()

    events = {
        5: [(first, 0, -1), (first, 1, -1), (first, 0, 1), (first, 1, 1)],
        8: [(second, 0, 0, -1), (second, 1, 0, -1), (second, 0, 0, 1), (second, 1, 0, 1)],
        9: [(opposite, 0), (opposite, 1)],
        12: [(second, 0, -1, -1), (second, 1, -1, -1), (second, 0, -1, 1), (second, 1, -1, 1)],
        14: [(second, 0, 1, -1), (second, 1, 1, -1), (second, 0, 1, 1), (second, 1, 1, 1)],
        15: [(last, 0, 0), (last, 1, 0)],
        17: [(second, 0, 2, -1), (second, 1, 2, -1), (second, 0, 2, 1), (second, 1, 2, 1)],
        19: [(last, 0, -1), (last, 1, -1), (last, 0, 1), (last, 1, 1)],
        21: [(last, 0, 2), (last, 1, 2)],
    }

    def tick(t, carry):
        @pl.when((k == 0) & (t >= 1) & (t < chunks - 1))
        def _():
            leave(t + 1)

        cf = t - LAG * k

        @pl.when((cf >= 0) & (cf < pieces) & (k > 0))
        def _():
            forward_step(cf)

        cb = t - LAG * (3 - k)

        @pl.when((cb >= jnp.where(k == 3, 1, 0)) & (cb < pieces))
        def _():
            backward_step(cb)

        for when, what in events.items():

            @pl.when(t == when)
            def _():
                for event in what:
                    event[0](*event[1:])

        return carry

    lax.fori_loop(0, pieces + 3 * LAG, tick, 0)

    for c in range(chunks):
        store_f(forward.at[c], c).wait()
        store_b(swept.at[c], c).wait()

    @pl.when(k < 3)
    def _():
        for s in range(pieces):
            send_f(s).wait_send()

    @pl.when(k > 0)
    def _():
        for s in range(pieces):
            send_b(s).wait_send()

    own_copy.wait()
    for number, what in enumerate(sends):
        relay_copy(number, *what).wait_send()
    for what in shared:
        share_copy(*what).wait_send()
        half, dp, dq = what
        start, size = span(half, None)
        block = block_at(half, dp, dq) + 1 - 2 * core
        ref = gathered_ref.at[block, pl.ds(start, size)]
        pltpu.make_async_copy(ref, ref, p_recv.at[half, dp % 4 * 4 + dq % 4]).wait()


def sweep(one, two, gain, matrix, jacobian, error, mask):
    rows, _, cols = one.shape
    chunks = cols // CHUNK
    vmem = pl.BlockSpec(memory_space=pltpu.VMEM)
    hbm = pl.BlockSpec(memory_space=pl.ANY)
    chunked = (chunks, rows, CHUNK)
    square = (rows, rows)
    return pl.pallas_call(
        sweep_kernel,
        out_shape=(
            jax.ShapeDtypeStruct(chunked, F32),
            jax.ShapeDtypeStruct(chunked, F32),
            jax.ShapeDtypeStruct((32, PACKED, 128), F32),
        ),
        in_specs=[hbm] * 5 + [vmem] * 2,
        out_specs=(hbm, hbm, hbm),
        scratch_shapes=[pltpu.VMEM(chunked, F32)] * 5
        + [pltpu.VMEM((2 * chunks, FOLDED, CHUNK), F32)] * 4
        + [pltpu.VMEM(square, F32), pltpu.VMEM((rows, cols), F32), pltpu.VMEM((PACKED, 128), F32)]
        + [pltpu.VMEM(square, BF16)] * 4
        + [
            pltpu.SemaphoreType.DMA((3, chunks)),
            pltpu.SemaphoreType.DMA((2, chunks)),
            pltpu.SemaphoreType.DMA((2,)),
            pltpu.SemaphoreType.DMA((2 * chunks,)),
            pltpu.SemaphoreType.DMA((2 * chunks,)),
            pltpu.SemaphoreType.DMA((2 * chunks,)),
            pltpu.SemaphoreType.DMA((2 * chunks,)),
            pltpu.SemaphoreType.DMA((40,)),
            pltpu.SemaphoreType.DMA((2, 16, 2)),
            pltpu.SemaphoreType.DMA((2, 16)),
            pltpu.SemaphoreType.DMA((2, 16)),
            pltpu.SemaphoreType.DMA,
        ],
        compiler_params=pltpu.CompilerParams(
            collective_id=0, has_side_effects=True, vmem_limit_bytes=60 * 1024 * 1024
        ),
        name="sweep",
    )(one, two, gain, matrix, jacobian, error, mask)


def apply_kernel(
    owner_ref, forward_hbm, swept_hbm, gathered_hbm,
    state_hbm, gradient_hbm,
    forward, swept, packed, x_high, x_low, slot_col, place, full, right, y_high, y_low,
    in_sem, packed_sem, out_sem,
):
    chunks, rows, _ = forward.shape
    groups, wide, cols = place.shape
    pad = full.shape[2] // 2
    depth = packed.shape[0]
    each = wide // SLOT
    load_f = [pltpu.make_async_copy(forward_hbm.at[c], forward.at[c], in_sem.at[0, c]) for c in range(chunks)]
    load_s = [pltpu.make_async_copy(swept_hbm.at[c], swept.at[c], in_sem.at[1, c]) for c in range(chunks)]

    def load_g(group, at):
        return pltpu.make_async_copy(
            gathered_hbm.at[pl.ds(group * each, each)], packed.at[at], packed_sem.at[at]
        )

    def store(source, target, which, c):
        return pltpu.make_async_copy(
            source.at[c], target.at[:, 0, pl.ds(c * CHUNK, CHUNK)], out_sem.at[which, c]
        )

    for copy in load_f:
        copy.start()
    for at in range(depth):
        load_g(at, at).start()
    for copy in load_s:
        copy.start()

    owner = owner_ref[...]
    onehot = (owner == lax.broadcasted_iota(jnp.int32, (32, cols), 0)).astype(F32)
    earlier = (
        lax.broadcasted_iota(jnp.int32, (cols, cols), 0) < lax.broadcasted_iota(jnp.int32, (cols, cols), 1)
    ).astype(BF16)
    before = dot(onehot.astype(BF16), earlier)
    placed = jnp.sum(before * onehot, axis=0, keepdims=True)
    slot = owner.astype(F32) * SLOT + placed
    slot_col[...] = jnp.broadcast_to(slot, (128, cols)).T
    line = lax.broadcasted_iota(jnp.int32, (wide, cols), 0).astype(F32)
    for group in range(groups):
        place[group] = (jnp.broadcast_to(slot - group * wide, (wide, cols)) == line).astype(BF16)
    right[...] = jnp.zeros_like(right)
    full[...] = jnp.zeros_like(full)

    for c in range(chunks):
        load_f[c].wait()
        lanes = slice(c * CHUNK, (c + 1) * CHUNK)
        x_high[:, lanes], x_low[:, lanes] = split(forward[c])
        store(forward, state_hbm, 0, c).start()

    row = lax.broadcasted_iota(jnp.int32, (128, 128), 0)
    col = lax.broadcasted_iota(jnp.int32, (128, 128), 1)
    left_lanes = lax.broadcasted_iota(jnp.int32, (rows, 128), 1) < SLOT
    rest = rows - 512

    def put(full, at_row, at_col, value):
        high, low = split(value)
        r, c = value.shape
        full[at_row : at_row + r, at_col : at_col + c] = high
        full[at_row : at_row + r, pad + at_col : pad + at_col + c] = low

    def unpack(g, full):
        for at, (i, j) in enumerate(OFFDIAG):
            value = g[128 * at : 128 * at + 128, :]
            put(full, 128 * i, 128 * j, value)
            put(full, 128 * j, 128 * i, value.T)
        for fold in range(2):
            at = FOLD_AT + 128 * fold
            value = g[at : at + 128, :]
            turned = value.T
            put(full, 256 * fold, 256 * fold, jnp.where(row <= col, value, turned))
            line_at = TAIL_AT + TAIL * (2 * fold + 1) + rest
            diagonal = jnp.broadcast_to(g[line_at : line_at + 1, :], (128, 128))
            lower = jnp.where(row > col, value, jnp.where(row < col, turned, diagonal))
            put(full, 256 * fold + 128, 256 * fold + 128, lower)
        for j in range(5):
            at = TAIL_AT + TAIL * j
            value = g[at : at + rest, :]
            put(full, 512, 128 * j, value)
            if j < 4:
                tall = jnp.concatenate([value, jnp.zeros((128 - rest, 128), F32)], axis=0)
                put(full, 128 * j, 512, tall.T)

    def one_group(group, carry):
        at = lax.rem(group, depth)
        base = (group * wide).astype(F32)
        lane = lax.broadcasted_iota(jnp.int32, (cols, 128), 1).astype(F32) + base
        pick = jnp.concatenate(
            [(slot_col[...] == lane).astype(BF16), (slot_col[...] == lane + 128.0).astype(BF16)], axis=1
        )
        s_high = dot(x_high[...], pick)
        s_low = dot(x_low[...], pick)
        load_g(group, at).wait()
        for pair in range(each // 2):
            lanes = slice(128 * pair, 128 * pair + 128)
            high = s_high[:, lanes]
            low = pltpu.roll(s_low[:, lanes], SLOT, 1)
            outs = []
            for side in range(2):
                mine = left_lanes if side == 0 else jnp.logical_not(left_lanes)
                right[side, 0:rows, :] = jnp.where(mine, high, low).astype(BF16)
                right[side, pad : pad + rows, :] = jnp.where(mine, high, 0.0).astype(BF16)
                unpack(packed.at[at, 2 * pair + side], full.at[side])
                outs.append(dot(full[side], right[side]))
            even, odd = outs
            answer = jnp.where(left_lanes, even + pltpu.roll(even, SLOT, 1), odd + pltpu.roll(odd, SLOT, 1))
            y_high[group, :, lanes], y_low[group, :, lanes] = split(answer)

        @pl.when(group + depth < groups)
        def _():
            load_g(group + depth, at).start()

        return carry

    lax.fori_loop(0, groups, one_group, 0)

    for c in range(chunks):
        load_s[c].wait()
    for tile in range(cols // 256):
        value = None
        lanes = slice(256 * tile, 256 * tile + 256)
        for group in range(groups):
            part = dot(y_high[group], place[group, :, lanes]) + dot(y_low[group], place[group, :, lanes])
            value = part if value is None else value + part
        for c in (2 * tile, 2 * tile + 1):
            swept[c] = swept[c] + value[:, (c % 2) * CHUNK : (c % 2 + 1) * CHUNK]
            store(swept, gradient_hbm, 1, c).start()
    for c in range(chunks):
        store(forward, state_hbm, 0, c).wait()
        store(swept, gradient_hbm, 1, c).wait()


def apply(owner, forward, swept, gathered):
    chunks, rows, _ = forward.shape
    cols = chunks * CHUNK
    hbm = pl.BlockSpec(memory_space=pl.ANY)
    pad = 640
    groups, wide, depth = 8, 4 * SLOT, 3
    return pl.pallas_call(
        apply_kernel,
        out_shape=(jax.ShapeDtypeStruct((rows, 1, cols), F32),) * 2,
        in_specs=[pl.BlockSpec(memory_space=pltpu.VMEM)] + [hbm] * 3,
        out_specs=(hbm, hbm),
        scratch_shapes=[
            pltpu.VMEM((chunks, rows, CHUNK), F32),
            pltpu.VMEM((chunks, rows, CHUNK), F32),
            pltpu.VMEM((depth, wide // SLOT, PACKED, 128), F32),
            pltpu.VMEM((rows, cols), BF16),
            pltpu.VMEM((rows, cols), BF16),
            pltpu.VMEM((cols, 128), F32),
            pltpu.VMEM((groups, wide, cols), BF16),
            pltpu.VMEM((2, rows, 2 * pad), BF16),
            pltpu.VMEM((2, 2 * pad, 128), BF16),
            pltpu.VMEM((groups, rows, wide), BF16),
            pltpu.VMEM((groups, rows, wide), BF16),
            pltpu.SemaphoreType.DMA((2, chunks)),
            pltpu.SemaphoreType.DMA((depth,)),
            pltpu.SemaphoreType.DMA((2, chunks)),
        ],
        compiler_params=pltpu.CompilerParams(vmem_limit_bytes=60 * 1024 * 1024),
        name="apply",
    )(owner, forward, swept, gathered)


def by_row(x):
    return jnp.transpose(x, (1, 0, 2))


def body(search_one, search_two, column_gain, model_matrix, obs_owner, observe_matrix, error_weight, channel_mask):
    forward, swept, gathered = sweep(
        by_row(search_one), by_row(search_two), by_row(column_gain), by_row(model_matrix),
        by_row(observe_matrix[0]), error_weight[0], channel_mask[0],
    )
    state, gradient = apply(obs_owner, forward, swept, gathered)
    return by_row(state), by_row(gradient)


def solution(mesh):
    return jax.shard_map(
        body,
        mesh=mesh,
        in_specs=(
            P("tm", None, "region"),
            P("tm", None, "region"),
            P("tm", None, "region"),
            P("tm", None, None),
            P("tm", "region"),
            P("tm", "region", None, None),
            P("tm", "region", None),
            P("tm", "region", None),
        ),
        out_specs=(P("tm", None, "region"), P("tm", None, "region")),
        check_vma=False,
    )
```

```python
import jax
import jax.numpy as jnp
from jax import lax
from jax.experimental import pallas as pl
from jax.experimental.pallas import tpu as pltpu
from jax.sharding import PartitionSpec as P

F32 = jnp.float32
BF16 = jnp.bfloat16
MESH = pl.DeviceIdType.MESH

OFFDIAG = ((0, 1), (0, 2), (0, 3), (1, 2), (1, 3), (2, 3))
FOLD_AT = 768
TAIL_AT = 1024
TAIL = 40
PACKED = TAIL_AT + 5 * TAIL
HALVES = ((0, 616, 312), (616, 608, 304))
SLOT = 64
CHUNK = 128
FOLDED = 276
LAG = 2


def split(x):
    high = x.astype(BF16)
    return high, (x - high.astype(F32)).astype(BF16)


def dot(a, b):
    return jnp.dot(a, b, preferred_element_type=F32)


def dot_nt(a, b):
    return lax.dot_general(a, b, (((1,), (1,)), ((), ())), preferred_element_type=F32)


def form_packed(matrix, weight, out_ref, depart):
    high, low = split(matrix)
    whigh, wlow = split(matrix * weight)

    def product(r0, r1, c0, c1):
        a, b = slice(r0, r1), slice(c0, c1)
        return dot_nt(whigh[a], high[b]) + (dot_nt(whigh[a], low[b]) + dot_nt(wlow[a], high[b]))

    nv = matrix.shape[0]
    rest = nv - 512
    row = lax.broadcasted_iota(jnp.int32, (128, 128), 0)
    col = lax.broadcasted_iota(jnp.int32, (128, 128), 1)
    top = product(0, 256, 0, 512)

    def block(i, j):
        if i < 2:
            return top[128 * i : 128 * i + 128, 128 * j : 128 * j + 128]
        return mid[128 * i - 256 : 128 * i - 128, 128 * j - 256 : 128 * j - 128]

    for at, (i, j) in enumerate(OFFDIAG[:5]):
        out_ref[128 * at : 128 * at + 128, :] = block(i, j)
    depart(0)
    mid = product(256, 512, 256, 512)
    tail = product(512, nv, 0, nv)
    out_ref[640:FOLD_AT, :] = block(2, 3)
    for pair in range(2):
        upper, lower = block(2 * pair, 2 * pair), block(2 * pair + 1, 2 * pair + 1)
        at = FOLD_AT + 128 * pair
        out_ref[at : at + 128, :] = jnp.where(row <= col, upper, lower)
    for j in range(5):
        at = TAIL_AT + TAIL * j
        if j < 4:
            out_ref[at : at + rest, :] = tail[:, 128 * j : 128 * j + 128]
            if j % 2 == 1:
                line = jnp.sum(jnp.where(row == col, block(j, j), 0.0), axis=0, keepdims=True)
            else:
                line = jnp.zeros((1, 128), F32)
            out_ref[at + rest : at + TAIL, :] = jnp.broadcast_to(line, (TAIL - rest, 128))
        else:
            out_ref[at : at + TAIL, :] = jnp.zeros((TAIL, 128), F32)
            out_ref[at : at + rest, 0:rest] = tail[:, 512:nv]
    depart(1)


def sweep_kernel(
    one_hbm, two_hbm, gain_hbm, matrix_hbm, jacobian_hbm, error_ref, mask_ref,
    forward_out, swept_out, gathered_ref,
    one, two, gain, forward, swept, into_f, into_b, out_f, out_b, matrix, jacobian, packed_ref,
    m_high, m_low, t_high, t_low,
    load_sem, store_sem, matrix_sem, f_send, f_recv, b_send, b_recv, g_send, g_recv, p_send, p_recv, own_sem,
):
    k = lax.axis_index("tm")
    region = lax.axis_index("region")
    core = region % 2
    x = (region // 2) % 4
    z = region // 8
    chunks, rows, _ = one.shape
    pieces = 2 * chunks
    cut = rows - FOLDED

    def chip(dz, dx):
        return ((z + dz + 4) % 4 * 4 + (x + dx + 4) % 4) * 2 + core

    partner = region + 1 - 2 * core

    def load(which, c):
        hbm, vmem = ((one_hbm, one), (two_hbm, two), (gain_hbm, gain))[which]
        return pltpu.make_async_copy(
            hbm.at[:, 0, pl.ds(c * CHUNK, CHUNK)], vmem.at[c], load_sem.at[which, c]
        )

    def load_at(which, c):
        hbm, vmem = ((one_hbm, one), (two_hbm, two), (gain_hbm, gain))[which]
        return pltpu.make_async_copy(
            hbm.at[:, 0, pl.ds(pl.multiple_of(c * CHUNK, CHUNK), CHUNK)], vmem.at[c], load_sem.at[which, c]
        )

    matrix_copy = pltpu.make_async_copy(matrix_hbm.at[:, 0, :], matrix, matrix_sem.at[0])
    jacobian_copy = pltpu.make_async_copy(jacobian_hbm.at[:, 0, :], jacobian, matrix_sem.at[1])
    load(0, 0).start()
    matrix_copy.start()
    load(1, 0).start()
    load(2, 0).start()
    jacobian_copy.start()
    for c in range(1, chunks):
        for which in range(3):
            load(which, c).start()

    def store_f(src, c):
        return pltpu.make_async_copy(src, forward_out.at[c], store_sem.at[0, c])

    def store_b(src, c):
        return pltpu.make_async_copy(src, swept_out.at[c], store_sem.at[1, c])

    barrier = pltpu.get_barrier_semaphore()
    around = [(k, chip(1, 0)), (k, chip(-1, 0)), (k, chip(0, 1)), (k, chip(0, -1)), (k, partner),
              ((k + 1) % 4, region), ((k + 3) % 4, region)]
    for who in around:
        pl.semaphore_signal(barrier, inc=1, device_id=who, device_id_type=MESH)
    pl.semaphore_wait(barrier, len(around))

    def send_f(s):
        return pltpu.make_async_remote_copy(
            src_ref=out_f.at[s], dst_ref=into_f.at[s], send_sem=f_send.at[s], recv_sem=f_recv.at[s],
            device_id=((k + 1) % 4, region), device_id_type=MESH,
        )

    def send_b(s):
        return pltpu.make_async_remote_copy(
            src_ref=out_b.at[s], dst_ref=into_b.at[s], send_sem=b_send.at[s], recv_sem=b_recv.at[s],
            device_id=((k + 3) % 4, region), device_id_type=MESH,
        )

    def step_to(primary, by):
        return chip(by, 0) if primary == "z" else chip(0, by)

    def block_at(half, dp, dq):
        if half == 0:
            return chip(dq, dp)
        return chip(dp, dq)

    axes = (("x", "z"), ("z", "x"))
    sends = []

    def span(half, piece):
        start, size, first_part = HALVES[half]
        if piece == 0:
            return start, first_part
        if piece == 1:
            return start + first_part, size - first_part
        return start, size

    def relay_copy(number, half, dp, dq, piece, axis, by):
        start, size = span(half, piece)
        block = block_at(half, dp, dq)
        own = dp == 0 and dq == 0
        place = pl.ds(start, size)
        rp, rq = dp % 4, dq % 4
        if axis == axes[half][0]:
            rp = (dp - by) % 4
        else:
            rq = (dq - by) % 4
        return pltpu.make_async_remote_copy(
            src_ref=packed_ref.at[place] if own else gathered_ref.at[block, place],
            dst_ref=gathered_ref.at[block, place],
            send_sem=g_send.at[number],
            recv_sem=g_recv.at[half, rp * 4 + rq, 1 if piece == 1 else 0],
            device_id=(k, step_to(axis, by)),
            device_id_type=MESH,
        )

    def relay(*what):
        relay_copy(len(sends), *what).start()
        sends.append(what)

    def arrived(half, dp, dq, piece):
        start, size = span(half, piece)
        block = block_at(half, dp, dq)
        ref = gathered_ref.at[block, pl.ds(start, size)]
        sem = g_recv.at[half, dp % 4 * 4 + dq % 4, 1 if piece == 1 else 0]
        pltpu.make_async_copy(ref, ref, sem).wait()

    shared = []

    def share_copy(half, dp, dq):
        start, size = span(half, None)
        block = block_at(half, dp, dq)
        place = pl.ds(start, size)
        own = dp == 0 and dq == 0
        at = dp % 4 * 4 + dq % 4
        return pltpu.make_async_remote_copy(
            src_ref=packed_ref.at[place] if own else gathered_ref.at[block, place],
            dst_ref=gathered_ref.at[block, place],
            send_sem=p_send.at[half, at],
            recv_sem=p_recv.at[half, at],
            device_id=(k, partner),
            device_id_type=MESH,
        )

    def share(*what):
        share_copy(*what).start()
        shared.append(what)

    def first(half, by):
        main, other = axes[half]
        arrived(half, by, 0, None)
        relay(half, by, 0, 0 if by == -1 else 1, main, -by)
        relay(half, by, 0, None, other, 1)
        relay(half, by, 0, None, other, -1)
        share(half, by, 0)

    def opposite(half):
        _, other = axes[half]
        arrived(half, 2, 0, 0)
        arrived(half, 2, 0, 1)
        relay(half, 2, 0, None, other, 1)
        relay(half, 2, 0, None, other, -1)
        share(half, 2, 0)

    def second(half, dp, by):
        _, other = axes[half]
        arrived(half, dp, by, None)
        relay(half, dp, by, 0 if by == -1 else 1, other, -by)
        share(half, dp, by)

    def last(half, dp):
        arrived(half, dp, 2, 0)
        arrived(half, dp, 2, 1)
        share(half, dp, 2)

    left = lax.broadcasted_iota(jnp.int32, (FOLDED, CHUNK), 1) < CHUNK // 2

    def fold(v, h):
        top = pltpu.roll(v[0:FOLDED], CHUNK // 2 * h, 1)
        low = pltpu.roll(v[cut:rows], CHUNK // 2 * (1 - h), 1)
        return jnp.where(left, top, low)

    def unfold(target, c, one_half, other_half, add):
        turned, returned = pltpu.roll(one_half, CHUNK // 2, 1), pltpu.roll(other_half, CHUNK // 2, 1)
        top, low = jnp.where(left, one_half, returned), jnp.where(left, turned, other_half)
        if add is not None:
            top, low = add[0:FOLDED] + top, add[cut:rows] + low
        target[c, 0:FOLDED, :] = top
        target[c, cut:rows, :] = low

    def times(a_high, a_low, v):
        high = v.astype(BF16).astype(F32)
        low = pltpu.roll(v - high, CHUNK // 2, 1)
        both = jnp.concatenate(
            [jnp.where(left, high, low)[0:cut].astype(BF16), jnp.where(left, low, high).astype(BF16)], axis=0
        )
        alone = jnp.concatenate(
            [jnp.where(left, high, 0.0)[0:cut].astype(BF16), jnp.where(left, 0.0, high).astype(BF16)], axis=0
        )
        total = dot(a_high[...], both) + dot(a_low[...], alone)
        total = total + pltpu.roll(total, CHUNK // 2, 1)
        return jnp.where(left, total[0:FOLDED], total[cut:rows])

    def leave(c):
        load_at(0, c).wait()
        value = one[c]
        for h in range(2):
            out_f[2 * c + h] = fold(value, h)
            send_f(2 * c + h).start()
        store_f(one.at[c], c).start()

    def prepare():
        matrix_copy.wait()
        value = matrix[...]
        m_high[...], m_low[...] = split(value)
        t_high[...], t_low[...] = split(value.T)

    def forward_step(s):
        c, h = s // 2, s % 2

        @pl.when(h == 0)
        def _():
            load_at(0, c).wait()

            @pl.when(k == 1)
            def _():
                load_at(2, c).wait()

        send_f(s).wait_recv()
        out_f[s] = fold(one[c], h) + fold(gain[c], h) * times(m_high, m_low, into_f[s])

        @pl.when(k < 3)
        def _():
            send_f(s).start()

        @pl.when(h == 1)
        def _():
            unfold(forward, c, out_f[s - 1], out_f[s], None)
            store_f(forward.at[c], c).start()

    def backward_step(s):
        c, h = s // 2, s % 2

        @pl.when(h == 0)
        def _():
            load_at(1, c).wait()

            @pl.when(k != 1)
            def _():
                load_at(2, c).wait()

        @pl.when(k < 3)
        def _():
            send_b(s).wait_recv()

        @pl.when(k == 3)
        def _():
            into_b[s] = jnp.zeros((FOLDED, CHUNK), F32)

        @pl.when(k > 0)
        def _():
            out_b[s] = times(t_high, t_low, fold(gain[c], h) * (fold(two[c], h) + into_b[s]))
            send_b(s).start()

        @pl.when(h == 1)
        def _():
            unfold(swept, c, into_b[s - 1], into_b[s], two[c])
            store_b(swept.at[c], c).start()

    @pl.when(k == 0)
    def _():
        leave(0)
        leave(1)

    prepare()

    @pl.when(k == 3)
    def _():
        backward_step(0)

    def depart(half):
        main, other = axes[half]
        for axis in (main, other):
            relay(half, 0, 0, None, axis, 1)
            relay(half, 0, 0, None, axis, -1)
        share(half, 0, 0)

    jacobian_copy.wait()
    form_packed(jacobian[...], error_ref[...] * mask_ref[...].astype(F32), packed_ref, depart)
    own_copy = pltpu.make_async_copy(packed_ref, gathered_ref.at[region], own_sem)
    own_copy.start()

    events = {
        5: [(first, 0, -1), (first, 1, -1), (first, 0, 1), (first, 1, 1)],
        8: [(second, 0, 0, -1), (second, 1, 0, -1), (second, 0, 0, 1), (second, 1, 0, 1)],
        9: [(opposite, 0), (opposite, 1)],
        12: [(second, 0, -1, -1), (second, 1, -1, -1), (second, 0, -1, 1), (second, 1, -1, 1)],
        14: [(second, 0, 1, -1), (second, 1, 1, -1), (second, 0, 1, 1), (second, 1, 1, 1)],
        15: [(last, 0, 0), (last, 1, 0)],
        16: [(second, 0, 2, -1), (second, 1, 2, -1), (second, 0, 2, 1), (second, 1, 2, 1)],
        18: [(last, 0, -1), (last, 1, -1), (last, 0, 1), (last, 1, 1)],
        20: [(last, 0, 2), (last, 1, 2)],
    }

    def tick(t, carry):
        @pl.when((k == 0) & (t >= 1) & (t < chunks - 1))
        def _():
            leave(t + 1)

        cf = t - LAG * k

        @pl.when((cf >= 0) & (cf < pieces) & (k > 0))
        def _():
            forward_step(cf)

        cb = t - LAG * (3 - k)

        @pl.when((cb >= jnp.where(k == 3, 1, 0)) & (cb < pieces))
        def _():
            backward_step(cb)

        for when, what in events.items():

            @pl.when(t == when)
            def _():
                for event in what:
                    event[0](*event[1:])

        return carry

    lax.fori_loop(0, pieces + 3 * LAG, tick, 0)

    for c in range(chunks):
        store_f(forward.at[c], c).wait()
        store_b(swept.at[c], c).wait()

    @pl.when(k < 3)
    def _():
        for s in range(pieces):
            send_f(s).wait_send()

    @pl.when(k > 0)
    def _():
        for s in range(pieces):
            send_b(s).wait_send()

    own_copy.wait()
    for number, what in enumerate(sends):
        relay_copy(number, *what).wait_send()
    for what in shared:
        share_copy(*what).wait_send()
        half, dp, dq = what
        start, size = span(half, None)
        block = block_at(half, dp, dq) + 1 - 2 * core
        ref = gathered_ref.at[block, pl.ds(start, size)]
        pltpu.make_async_copy(ref, ref, p_recv.at[half, dp % 4 * 4 + dq % 4]).wait()


def sweep(one, two, gain, matrix, jacobian, error, mask):
    rows, _, cols = one.shape
    chunks = cols // CHUNK
    vmem = pl.BlockSpec(memory_space=pltpu.VMEM)
    hbm = pl.BlockSpec(memory_space=pl.ANY)
    chunked = (chunks, rows, CHUNK)
    square = (rows, rows)
    return pl.pallas_call(
        sweep_kernel,
        out_shape=(
            jax.ShapeDtypeStruct(chunked, F32),
            jax.ShapeDtypeStruct(chunked, F32),
            jax.ShapeDtypeStruct((32, PACKED, 128), F32),
        ),
        in_specs=[hbm] * 5 + [vmem] * 2,
        out_specs=(hbm, hbm, hbm),
        scratch_shapes=[pltpu.VMEM(chunked, F32)] * 5
        + [pltpu.VMEM((2 * chunks, FOLDED, CHUNK), F32)] * 4
        + [pltpu.VMEM(square, F32), pltpu.VMEM((rows, cols), F32), pltpu.VMEM((PACKED, 128), F32)]
        + [pltpu.VMEM(square, BF16)] * 4
        + [
            pltpu.SemaphoreType.DMA((3, chunks)),
            pltpu.SemaphoreType.DMA((2, chunks)),
            pltpu.SemaphoreType.DMA((2,)),
            pltpu.SemaphoreType.DMA((2 * chunks,)),
            pltpu.SemaphoreType.DMA((2 * chunks,)),
            pltpu.SemaphoreType.DMA((2 * chunks,)),
            pltpu.SemaphoreType.DMA((2 * chunks,)),
            pltpu.SemaphoreType.DMA((40,)),
            pltpu.SemaphoreType.DMA((2, 16, 2)),
            pltpu.SemaphoreType.DMA((2, 16)),
            pltpu.SemaphoreType.DMA((2, 16)),
            pltpu.SemaphoreType.DMA,
        ],
        compiler_params=pltpu.CompilerParams(
            collective_id=0, has_side_effects=True, vmem_limit_bytes=60 * 1024 * 1024
        ),
        name="sweep",
    )(one, two, gain, matrix, jacobian, error, mask)


def apply_kernel(
    owner_ref, forward_hbm, swept_hbm, gathered_hbm,
    state_hbm, gradient_hbm,
    forward, swept, packed, x_high, x_low, slot_col, place, full, right, y_high, y_low,
    in_sem, packed_sem, out_sem,
):
    chunks, rows, _ = forward.shape
    groups, wide, cols = place.shape
    pad = full.shape[2] // 2
    depth = packed.shape[0]
    each = wide // SLOT
    load_f = [pltpu.make_async_copy(forward_hbm.at[c], forward.at[c], in_sem.at[0, c]) for c in range(chunks)]
    load_s = [pltpu.make_async_copy(swept_hbm.at[c], swept.at[c], in_sem.at[1, c]) for c in range(chunks)]

    def load_g(group, at):
        return pltpu.make_async_copy(
            gathered_hbm.at[pl.ds(group * each, each)], packed.at[at], packed_sem.at[at]
        )

    def store(source, target, which, c):
        return pltpu.make_async_copy(
            source.at[c], target.at[:, 0, pl.ds(c * CHUNK, CHUNK)], out_sem.at[which, c]
        )

    for copy in load_f:
        copy.start()
    for at in range(depth):
        load_g(at, at).start()
    for copy in load_s:
        copy.start()

    owner = owner_ref[...]
    onehot = (owner == lax.broadcasted_iota(jnp.int32, (32, cols), 0)).astype(F32)
    earlier = (
        lax.broadcasted_iota(jnp.int32, (cols, cols), 0) < lax.broadcasted_iota(jnp.int32, (cols, cols), 1)
    ).astype(BF16)
    before = dot(onehot.astype(BF16), earlier)
    placed = jnp.sum(before * onehot, axis=0, keepdims=True)
    slot = owner.astype(F32) * SLOT + placed
    slot_col[...] = jnp.broadcast_to(slot, (128, cols)).T
    line = lax.broadcasted_iota(jnp.int32, (wide, cols), 0).astype(F32)
    for group in range(groups):
        place[group] = (jnp.broadcast_to(slot - group * wide, (wide, cols)) == line).astype(BF16)
    right[...] = jnp.zeros_like(right)
    full[...] = jnp.zeros_like(full)

    for c in range(chunks):
        load_f[c].wait()
        lanes = slice(c * CHUNK, (c + 1) * CHUNK)
        x_high[:, lanes], x_low[:, lanes] = split(forward[c])
        store(forward, state_hbm, 0, c).start()

    row = lax.broadcasted_iota(jnp.int32, (128, 128), 0)
    col = lax.broadcasted_iota(jnp.int32, (128, 128), 1)
    left_lanes = lax.broadcasted_iota(jnp.int32, (rows, 128), 1) < SLOT
    rest = rows - 512

    def put(full, at_row, at_col, value):
        high, low = split(value)
        r, c = value.shape
        full[at_row : at_row + r, at_col : at_col + c] = high
        full[at_row : at_row + r, pad + at_col : pad + at_col + c] = low

    def unpack(g, full):
        for at, (i, j) in enumerate(OFFDIAG):
            value = g[128 * at : 128 * at + 128, :]
            put(full, 128 * i, 128 * j, value)
            put(full, 128 * j, 128 * i, value.T)
        for fold in range(2):
            at = FOLD_AT + 128 * fold
            value = g[at : at + 128, :]
            turned = value.T
            put(full, 256 * fold, 256 * fold, jnp.where(row <= col, value, turned))
            line_at = TAIL_AT + TAIL * (2 * fold + 1) + rest
            diagonal = jnp.broadcast_to(g[line_at : line_at + 1, :], (128, 128))
            lower = jnp.where(row > col, value, jnp.where(row < col, turned, diagonal))
            put(full, 256 * fold + 128, 256 * fold + 128, lower)
        for j in range(5):
            at = TAIL_AT + TAIL * j
            value = g[at : at + rest, :]
            put(full, 512, 128 * j, value)
            if j < 4:
                tall = jnp.concatenate([value, jnp.zeros((128 - rest, 128), F32)], axis=0)
                put(full, 128 * j, 512, tall.T)

    def sort(group):
        base = jnp.asarray(group * wide).astype(F32)
        lane = lax.broadcasted_iota(jnp.int32, (cols, 128), 1).astype(F32) + base
        pick = jnp.concatenate(
            [(slot_col[...] == lane).astype(BF16), (slot_col[...] == lane + 128.0).astype(BF16)], axis=1
        )
        s_high = dot(x_high[...], pick)
        s_low = dot(x_low[...], pick)
        for o in range(each):
            lanes = slice(128 * (o // 2), 128 * (o // 2) + 128)
            high = s_high[:, lanes]
            low = pltpu.roll(s_low[:, lanes], SLOT, 1)
            mine = left_lanes if o % 2 == 0 else jnp.logical_not(left_lanes)
            right[o, 0:rows, :] = jnp.where(mine, high, low).astype(BF16)
            right[o, pad : pad + rows, :] = jnp.where(mine, high, 0.0).astype(BF16)

    def finish(group, outs):
        for pair in range(each // 2):
            lanes = slice(128 * pair, 128 * pair + 128)
            even, odd = outs[2 * pair : 2 * pair + 2]
            answer = jnp.where(left_lanes, even + pltpu.roll(even, SLOT, 1), odd + pltpu.roll(odd, SLOT, 1))
            y_high[group, :, lanes], y_low[group, :, lanes] = split(answer)

    def one_group(group, now, later):
        ahead = group + 1
        at = lax.rem(ahead, depth)
        sort(group)

        @pl.when(ahead < groups)
        def _():
            load_g(ahead, at).wait()

        outs = []
        for o in range(each):
            outs.append(dot(full[now * each + o], right[o]))
            unpack(packed.at[at, o], full.at[later * each + o])
        finish(group, outs)

        @pl.when(ahead + depth < groups)
        def _():
            load_g(ahead + depth, at).start()

    load_g(0, 0).wait()
    for o in range(each):
        unpack(packed.at[0, o], full.at[o])
    load_g(depth, 0).start()

    def two_groups(i, carry):
        one_group(2 * i, 0, 1)
        one_group(2 * i + 1, 1, 0)
        return carry

    lax.fori_loop(0, groups // 2, two_groups, 0)

    for c in range(chunks):
        load_s[c].wait()
    for tile in range(cols // 256):
        value = None
        lanes = slice(256 * tile, 256 * tile + 256)
        for group in range(groups):
            part = dot(y_high[group], place[group, :, lanes]) + dot(y_low[group], place[group, :, lanes])
            value = part if value is None else value + part
        for c in (2 * tile, 2 * tile + 1):
            swept[c] = swept[c] + value[:, (c % 2) * CHUNK : (c % 2 + 1) * CHUNK]
            store(swept, gradient_hbm, 1, c).start()
    for c in range(chunks):
        store(forward, state_hbm, 0, c).wait()
        store(swept, gradient_hbm, 1, c).wait()


def apply(owner, forward, swept, gathered):
    chunks, rows, _ = forward.shape
    cols = chunks * CHUNK
    hbm = pl.BlockSpec(memory_space=pl.ANY)
    pad = 640
    groups, wide, depth = 8, 4 * SLOT, 3
    return pl.pallas_call(
        apply_kernel,
        out_shape=(jax.ShapeDtypeStruct((rows, 1, cols), F32),) * 2,
        in_specs=[pl.BlockSpec(memory_space=pltpu.VMEM)] + [hbm] * 3,
        out_specs=(hbm, hbm),
        scratch_shapes=[
            pltpu.VMEM((chunks, rows, CHUNK), F32),
            pltpu.VMEM((chunks, rows, CHUNK), F32),
            pltpu.VMEM((depth, wide // SLOT, PACKED, 128), F32),
            pltpu.VMEM((rows, cols), BF16),
            pltpu.VMEM((rows, cols), BF16),
            pltpu.VMEM((cols, 128), F32),
            pltpu.VMEM((groups, wide, cols), BF16),
            pltpu.VMEM((8, rows, 2 * pad), BF16),
            pltpu.VMEM((4, 2 * pad, 128), BF16),
            pltpu.VMEM((groups, rows, wide), BF16),
            pltpu.VMEM((groups, rows, wide), BF16),
            pltpu.SemaphoreType.DMA((2, chunks)),
            pltpu.SemaphoreType.DMA((depth,)),
            pltpu.SemaphoreType.DMA((2, chunks)),
        ],
        compiler_params=pltpu.CompilerParams(vmem_limit_bytes=60 * 1024 * 1024),
        name="apply",
    )(owner, forward, swept, gathered)


def by_row(x):
    return jnp.transpose(x, (1, 0, 2))


def body(search_one, search_two, column_gain, model_matrix, obs_owner, observe_matrix, error_weight, channel_mask):
    forward, swept, gathered = sweep(
        by_row(search_one), by_row(search_two), by_row(column_gain), by_row(model_matrix),
        by_row(observe_matrix[0]), error_weight[0], channel_mask[0],
    )
    state, gradient = apply(obs_owner, forward, swept, gathered)
    return by_row(state), by_row(gradient)


def solution(mesh):
    return jax.shard_map(
        body,
        mesh=mesh,
        in_specs=(
            P("tm", None, "region"),
            P("tm", None, "region"),
            P("tm", None, "region"),
            P("tm", None, None),
            P("tm", "region"),
            P("tm", "region", None, None),
            P("tm", "region", None),
            P("tm", "region", None),
        ),
        out_specs=(P("tm", None, "region"), P("tm", None, "region")),
        check_vma=False,
    )
```

```python
import jax
import jax.numpy as jnp
from jax import lax
from jax.experimental import pallas as pl
from jax.experimental.pallas import tpu as pltpu
from jax.sharding import PartitionSpec as P

F32 = jnp.float32
BF16 = jnp.bfloat16
MESH = pl.DeviceIdType.MESH

OFFDIAG = ((0, 1), (0, 2), (0, 3), (1, 2), (1, 3), (2, 3))
FOLD_AT = 768
TAIL_AT = 1024
TAIL = 40
PACKED = TAIL_AT + 5 * TAIL
HALVES = ((0, 616, 312), (616, 608, 304))
SLOT = 64
CHUNK = 128
FOLDED = 276
LAG = 2


def split(x):
    high = x.astype(BF16)
    return high, (x - high.astype(F32)).astype(BF16)


def dot(a, b):
    return jnp.dot(a, b, preferred_element_type=F32)


def dot_nt(a, b):
    return lax.dot_general(a, b, (((1,), (1,)), ((), ())), preferred_element_type=F32)


def form_packed(matrix, weight, out_ref, depart):
    high, low = split(matrix)
    whigh, wlow = split(matrix * weight)

    def product(r0, r1, c0, c1):
        a, b = slice(r0, r1), slice(c0, c1)
        return dot_nt(whigh[a], high[b]) + (dot_nt(whigh[a], low[b]) + dot_nt(wlow[a], high[b]))

    nv = matrix.shape[0]
    rest = nv - 512
    row = lax.broadcasted_iota(jnp.int32, (128, 128), 0)
    col = lax.broadcasted_iota(jnp.int32, (128, 128), 1)
    top = product(0, 256, 0, 512)

    def block(i, j):
        if i < 2:
            return top[128 * i : 128 * i + 128, 128 * j : 128 * j + 128]
        return mid[128 * i - 256 : 128 * i - 128, 128 * j - 256 : 128 * j - 128]

    for at, (i, j) in enumerate(OFFDIAG[:5]):
        out_ref[128 * at : 128 * at + 128, :] = block(i, j)
    depart(0)
    mid = product(256, 512, 256, 512)
    tail = product(512, nv, 0, nv)
    out_ref[640:FOLD_AT, :] = block(2, 3)
    for pair in range(2):
        upper, lower = block(2 * pair, 2 * pair), block(2 * pair + 1, 2 * pair + 1)
        at = FOLD_AT + 128 * pair
        out_ref[at : at + 128, :] = jnp.where(row <= col, upper, lower)
    for j in range(5):
        at = TAIL_AT + TAIL * j
        if j < 4:
            out_ref[at : at + rest, :] = tail[:, 128 * j : 128 * j + 128]
            if j % 2 == 1:
                line = jnp.sum(jnp.where(row == col, block(j, j), 0.0), axis=0, keepdims=True)
            else:
                line = jnp.zeros((1, 128), F32)
            out_ref[at + rest : at + TAIL, :] = jnp.broadcast_to(line, (TAIL - rest, 128))
        else:
            out_ref[at : at + TAIL, :] = jnp.zeros((TAIL, 128), F32)
            out_ref[at : at + rest, 0:rest] = tail[:, 512:nv]
    depart(1)


def sweep_kernel(
    one_hbm, two_hbm, gain_hbm, matrix_hbm, jacobian_hbm, error_ref, mask_ref,
    forward_out, swept_out, gathered_ref,
    one, two, gain, forward, swept, into_f, into_b, out_f, out_b, matrix, jacobian, packed_ref,
    m_high, m_low, t_high, t_low,
    load_sem, store_sem, matrix_sem, f_send, f_recv, b_send, b_recv, g_send, g_recv, p_send, p_recv, own_sem,
):
    k = lax.axis_index("tm")
    region = lax.axis_index("region")
    core = region % 2
    x = (region // 2) % 4
    z = region // 8
    chunks, rows, _ = one.shape
    pieces = 2 * chunks
    cut = rows - FOLDED

    def chip(dz, dx):
        return ((z + dz + 4) % 4 * 4 + (x + dx + 4) % 4) * 2 + core

    partner = region + 1 - 2 * core

    def load(which, c):
        hbm, vmem = ((one_hbm, one), (two_hbm, two), (gain_hbm, gain))[which]
        return pltpu.make_async_copy(
            hbm.at[:, 0, pl.ds(c * CHUNK, CHUNK)], vmem.at[c], load_sem.at[which, c]
        )

    def load_at(which, c):
        hbm, vmem = ((one_hbm, one), (two_hbm, two), (gain_hbm, gain))[which]
        return pltpu.make_async_copy(
            hbm.at[:, 0, pl.ds(pl.multiple_of(c * CHUNK, CHUNK), CHUNK)], vmem.at[c], load_sem.at[which, c]
        )

    matrix_copy = pltpu.make_async_copy(matrix_hbm.at[:, 0, :], matrix, matrix_sem.at[0])
    jacobian_copy = pltpu.make_async_copy(jacobian_hbm.at[:, 0, :], jacobian, matrix_sem.at[1])
    load(0, 0).start()
    matrix_copy.start()
    load(1, 0).start()
    load(2, 0).start()
    jacobian_copy.start()
    for c in range(1, chunks):
        for which in range(3):
            load(which, c).start()

    def store_f(src, c):
        return pltpu.make_async_copy(src, forward_out.at[c], store_sem.at[0, c])

    def store_b(src, c):
        return pltpu.make_async_copy(src, swept_out.at[c], store_sem.at[1, c])

    barrier = pltpu.get_barrier_semaphore()
    around = [(k, chip(1, 0)), (k, chip(-1, 0)), (k, chip(0, 1)), (k, chip(0, -1)), (k, partner),
              ((k + 1) % 4, region), ((k + 3) % 4, region)]
    for who in around:
        pl.semaphore_signal(barrier, inc=1, device_id=who, device_id_type=MESH)
    pl.semaphore_wait(barrier, len(around))

    def send_f(s):
        return pltpu.make_async_remote_copy(
            src_ref=out_f.at[s], dst_ref=into_f.at[s], send_sem=f_send.at[s], recv_sem=f_recv.at[s],
            device_id=((k + 1) % 4, region), device_id_type=MESH,
        )

    def send_b(s):
        return pltpu.make_async_remote_copy(
            src_ref=out_b.at[s], dst_ref=into_b.at[s], send_sem=b_send.at[s], recv_sem=b_recv.at[s],
            device_id=((k + 3) % 4, region), device_id_type=MESH,
        )

    def step_to(primary, by):
        return chip(by, 0) if primary == "z" else chip(0, by)

    def block_at(half, dp, dq):
        if half == 0:
            return chip(dq, dp)
        return chip(dp, dq)

    axes = (("x", "z"), ("z", "x"))
    sends = []

    def span(half, piece):
        start, size, first_part = HALVES[half]
        if piece == 0:
            return start, first_part
        if piece == 1:
            return start + first_part, size - first_part
        return start, size

    def relay_copy(number, half, dp, dq, piece, axis, by):
        start, size = span(half, piece)
        block = block_at(half, dp, dq)
        own = dp == 0 and dq == 0
        place = pl.ds(start, size)
        rp, rq = dp % 4, dq % 4
        if axis == axes[half][0]:
            rp = (dp - by) % 4
        else:
            rq = (dq - by) % 4
        return pltpu.make_async_remote_copy(
            src_ref=packed_ref.at[place] if own else gathered_ref.at[block, place],
            dst_ref=gathered_ref.at[block, place],
            send_sem=g_send.at[number],
            recv_sem=g_recv.at[half, rp * 4 + rq, 1 if piece == 1 else 0],
            device_id=(k, step_to(axis, by)),
            device_id_type=MESH,
        )

    def relay(*what):
        relay_copy(len(sends), *what).start()
        sends.append(what)

    def arrived(half, dp, dq, piece):
        start, size = span(half, piece)
        block = block_at(half, dp, dq)
        ref = gathered_ref.at[block, pl.ds(start, size)]
        sem = g_recv.at[half, dp % 4 * 4 + dq % 4, 1 if piece == 1 else 0]
        pltpu.make_async_copy(ref, ref, sem).wait()

    shared = []

    def share_copy(half, dp, dq):
        start, size = span(half, None)
        block = block_at(half, dp, dq)
        place = pl.ds(start, size)
        own = dp == 0 and dq == 0
        at = dp % 4 * 4 + dq % 4
        return pltpu.make_async_remote_copy(
            src_ref=packed_ref.at[place] if own else gathered_ref.at[block, place],
            dst_ref=gathered_ref.at[block, place],
            send_sem=p_send.at[half, at],
            recv_sem=p_recv.at[half, at],
            device_id=(k, partner),
            device_id_type=MESH,
        )

    def share(*what):
        share_copy(*what).start()
        shared.append(what)

    def first(half, by):
        main, other = axes[half]
        arrived(half, by, 0, None)
        relay(half, by, 0, 0 if by == -1 else 1, main, -by)
        relay(half, by, 0, None, other, 1)
        relay(half, by, 0, None, other, -1)
        share(half, by, 0)

    def opposite(half):
        _, other = axes[half]
        arrived(half, 2, 0, 0)
        arrived(half, 2, 0, 1)
        relay(half, 2, 0, None, other, 1)
        relay(half, 2, 0, None, other, -1)
        share(half, 2, 0)

    def second(half, dp, by):
        _, other = axes[half]
        arrived(half, dp, by, None)
        relay(half, dp, by, 0 if by == -1 else 1, other, -by)
        share(half, dp, by)

    def last(half, dp):
        arrived(half, dp, 2, 0)
        arrived(half, dp, 2, 1)
        share(half, dp, 2)

    left = lax.broadcasted_iota(jnp.int32, (FOLDED, CHUNK), 1) < CHUNK // 2

    def fold(v, h):
        top = pltpu.roll(v[0:FOLDED], CHUNK // 2 * h, 1)
        low = pltpu.roll(v[cut:rows], CHUNK // 2 * (1 - h), 1)
        return jnp.where(left, top, low)

    def unfold(target, c, one_half, other_half, add):
        turned, returned = pltpu.roll(one_half, CHUNK // 2, 1), pltpu.roll(other_half, CHUNK // 2, 1)
        top, low = jnp.where(left, one_half, returned), jnp.where(left, turned, other_half)
        if add is not None:
            top, low = add[0:FOLDED] + top, add[cut:rows] + low
        target[c, 0:FOLDED, :] = top
        target[c, cut:rows, :] = low

    def times(a_high, a_low, v):
        high = v.astype(BF16).astype(F32)
        low = pltpu.roll(v - high, CHUNK // 2, 1)
        both = jnp.concatenate(
            [jnp.where(left, high, low)[0:cut].astype(BF16), jnp.where(left, low, high).astype(BF16)], axis=0
        )
        alone = jnp.concatenate(
            [jnp.where(left, high, 0.0)[0:cut].astype(BF16), jnp.where(left, 0.0, high).astype(BF16)], axis=0
        )
        total = dot(a_high[...], both) + dot(a_low[...], alone)
        total = total + pltpu.roll(total, CHUNK // 2, 1)
        return jnp.where(left, total[0:FOLDED], total[cut:rows])

    def leave(c):
        load_at(0, c).wait()
        value = one[c]
        for h in range(2):
            out_f[2 * c + h] = fold(value, h)
            send_f(2 * c + h).start()
        store_f(one.at[c], c).start()

    def forward_step(s):
        c, h = s // 2, s % 2

        @pl.when(h == 0)
        def _():
            load_at(0, c).wait()

            @pl.when(k == 1)
            def _():
                load_at(2, c).wait()

        send_f(s).wait_recv()
        out_f[s] = fold(one[c], h) + fold(gain[c], h) * times(m_high, m_low, into_f[s])

        @pl.when(k < 3)
        def _():
            send_f(s).start()

        @pl.when(h == 1)
        def _():
            unfold(forward, c, out_f[s - 1], out_f[s], None)
            store_f(forward.at[c], c).start()

    def backward_step(s):
        c, h = s // 2, s % 2

        @pl.when(h == 0)
        def _():
            load_at(1, c).wait()

            @pl.when(k != 1)
            def _():
                load_at(2, c).wait()

        @pl.when(k < 3)
        def _():
            send_b(s).wait_recv()

        @pl.when(k == 3)
        def _():
            into_b[s] = jnp.zeros((FOLDED, CHUNK), F32)

        @pl.when(k > 0)
        def _():
            out_b[s] = times(t_high, t_low, fold(gain[c], h) * (fold(two[c], h) + into_b[s]))
            send_b(s).start()

        @pl.when(h == 1)
        def _():
            unfold(swept, c, into_b[s - 1], into_b[s], two[c])
            store_b(swept.at[c], c).start()

    @pl.when(k == 0)
    def _():
        leave(0)
        leave(1)

    matrix_copy.wait()
    t_high[...], t_low[...] = split(matrix[...].T)

    @pl.when(k == 3)
    def _():
        backward_step(0)
        backward_step(1)

    m_high[...], m_low[...] = split(matrix[...])

    def depart(half):
        main, other = axes[half]
        for axis in (main, other):
            relay(half, 0, 0, None, axis, 1)
            relay(half, 0, 0, None, axis, -1)
        share(half, 0, 0)

    jacobian_copy.wait()
    form_packed(jacobian[...], error_ref[...] * mask_ref[...].astype(F32), packed_ref, depart)
    own_copy = pltpu.make_async_copy(packed_ref, gathered_ref.at[region], own_sem)
    own_copy.start()

    events = {
        5: [(first, 0, -1), (first, 1, -1), (first, 0, 1), (first, 1, 1)],
        8: [(second, 0, 0, -1), (second, 1, 0, -1), (second, 0, 0, 1), (second, 1, 0, 1)],
        9: [(opposite, 0), (opposite, 1)],
        12: [(second, 0, -1, -1), (second, 1, -1, -1), (second, 0, -1, 1), (second, 1, -1, 1)],
        14: [(second, 0, 1, -1), (second, 1, 1, -1), (second, 0, 1, 1), (second, 1, 1, 1)],
        15: [(last, 0, 0), (last, 1, 0)],
        16: [(second, 0, 2, -1), (second, 1, 2, -1), (second, 0, 2, 1), (second, 1, 2, 1)],
        18: [(last, 0, -1), (last, 1, -1), (last, 0, 1), (last, 1, 1)],
        20: [(last, 0, 2), (last, 1, 2)],
    }

    def tick(t, carry):
        @pl.when((k == 0) & (t >= 1) & (t < chunks - 1))
        def _():
            leave(t + 1)

        cf = t - LAG * k

        @pl.when((cf >= 0) & (cf < pieces) & (k > 0))
        def _():
            forward_step(cf)

        cb = t - LAG * (3 - k)

        @pl.when((cb >= jnp.where(k == 3, 2, 0)) & (cb < pieces))
        def _():
            backward_step(cb)

        for when, what in events.items():

            @pl.when(t == when)
            def _():
                for event in what:
                    event[0](*event[1:])

        return carry

    lax.fori_loop(0, pieces + 3 * LAG, tick, 0)

    for c in range(chunks):
        store_f(forward.at[c], c).wait()
        store_b(swept.at[c], c).wait()

    @pl.when(k < 3)
    def _():
        for s in range(pieces):
            send_f(s).wait_send()

    @pl.when(k > 0)
    def _():
        for s in range(pieces):
            send_b(s).wait_send()

    own_copy.wait()
    for number, what in enumerate(sends):
        relay_copy(number, *what).wait_send()
    for what in shared:
        share_copy(*what).wait_send()
        half, dp, dq = what
        start, size = span(half, None)
        block = block_at(half, dp, dq) + 1 - 2 * core
        ref = gathered_ref.at[block, pl.ds(start, size)]
        pltpu.make_async_copy(ref, ref, p_recv.at[half, dp % 4 * 4 + dq % 4]).wait()


def sweep(one, two, gain, matrix, jacobian, error, mask):
    rows, _, cols = one.shape
    chunks = cols // CHUNK
    vmem = pl.BlockSpec(memory_space=pltpu.VMEM)
    hbm = pl.BlockSpec(memory_space=pl.ANY)
    chunked = (chunks, rows, CHUNK)
    square = (rows, rows)
    return pl.pallas_call(
        sweep_kernel,
        out_shape=(
            jax.ShapeDtypeStruct(chunked, F32),
            jax.ShapeDtypeStruct(chunked, F32),
            jax.ShapeDtypeStruct((32, PACKED, 128), F32),
        ),
        in_specs=[hbm] * 5 + [vmem] * 2,
        out_specs=(hbm, hbm, hbm),
        scratch_shapes=[pltpu.VMEM(chunked, F32)] * 5
        + [pltpu.VMEM((2 * chunks, FOLDED, CHUNK), F32)] * 4
        + [pltpu.VMEM(square, F32), pltpu.VMEM((rows, cols), F32), pltpu.VMEM((PACKED, 128), F32)]
        + [pltpu.VMEM(square, BF16)] * 4
        + [
            pltpu.SemaphoreType.DMA((3, chunks)),
            pltpu.SemaphoreType.DMA((2, chunks)),
            pltpu.SemaphoreType.DMA((2,)),
            pltpu.SemaphoreType.DMA((2 * chunks,)),
            pltpu.SemaphoreType.DMA((2 * chunks,)),
            pltpu.SemaphoreType.DMA((2 * chunks,)),
            pltpu.SemaphoreType.DMA((2 * chunks,)),
            pltpu.SemaphoreType.DMA((40,)),
            pltpu.SemaphoreType.DMA((2, 16, 2)),
            pltpu.SemaphoreType.DMA((2, 16)),
            pltpu.SemaphoreType.DMA((2, 16)),
            pltpu.SemaphoreType.DMA,
        ],
        compiler_params=pltpu.CompilerParams(
            collective_id=0, has_side_effects=True, vmem_limit_bytes=60 * 1024 * 1024
        ),
        name="sweep",
    )(one, two, gain, matrix, jacobian, error, mask)


def apply_kernel(
    owner_ref, forward_hbm, swept_hbm, gathered_hbm,
    state_hbm, gradient_hbm,
    forward, swept, packed, x_high, x_low, slot_col, place, full, right, y_high, y_low,
    in_sem, packed_sem, out_sem,
):
    chunks, rows, _ = forward.shape
    groups, wide, cols = place.shape
    pad = full.shape[2] // 2
    depth = packed.shape[0]
    each = wide // SLOT
    load_f = [pltpu.make_async_copy(forward_hbm.at[c], forward.at[c], in_sem.at[0, c]) for c in range(chunks)]
    load_s = [pltpu.make_async_copy(swept_hbm.at[c], swept.at[c], in_sem.at[1, c]) for c in range(chunks)]

    def load_g(group, at):
        return pltpu.make_async_copy(
            gathered_hbm.at[pl.ds(group * each, each)], packed.at[at], packed_sem.at[at]
        )

    def store(source, target, which, c):
        return pltpu.make_async_copy(
            source.at[c], target.at[:, 0, pl.ds(c * CHUNK, CHUNK)], out_sem.at[which, c]
        )

    load_g(0, 0).start()
    for copy in load_f:
        copy.start()

    owner = owner_ref[...]
    onehot = (owner == lax.broadcasted_iota(jnp.int32, (32, cols), 0)).astype(F32)
    earlier = (
        lax.broadcasted_iota(jnp.int32, (cols, cols), 0) < lax.broadcasted_iota(jnp.int32, (cols, cols), 1)
    ).astype(BF16)
    before = dot(onehot.astype(BF16), earlier)
    placed = jnp.sum(before * onehot, axis=0, keepdims=True)
    slot = owner.astype(F32) * SLOT + placed
    slot_col[...] = jnp.broadcast_to(slot, (128, cols)).T
    line = lax.broadcasted_iota(jnp.int32, (wide, cols), 0).astype(F32)
    for group in range(groups):
        place[group] = (jnp.broadcast_to(slot - group * wide, (wide, cols)) == line).astype(BF16)
    right[...] = jnp.zeros_like(right)

    for c in range(chunks):
        load_f[c].wait()
        lanes = slice(c * CHUNK, (c + 1) * CHUNK)
        x_high[:, lanes], x_low[:, lanes] = split(forward[c])
        store(forward, state_hbm, 0, c).start()

    row = lax.broadcasted_iota(jnp.int32, (128, 128), 0)
    col = lax.broadcasted_iota(jnp.int32, (128, 128), 1)
    left_lanes = lax.broadcasted_iota(jnp.int32, (rows, 128), 1) < SLOT
    rest = rows - 512

    def put(full, at_row, at_col, value):
        high, low = split(value)
        r, c = value.shape
        full[at_row : at_row + r, at_col : at_col + c] = high
        full[at_row : at_row + r, pad + at_col : pad + at_col + c] = low

    def unpack(g, full):
        for at, (i, j) in enumerate(OFFDIAG):
            value = g[128 * at : 128 * at + 128, :]
            put(full, 128 * i, 128 * j, value)
            put(full, 128 * j, 128 * i, value.T)
        for fold in range(2):
            at = FOLD_AT + 128 * fold
            value = g[at : at + 128, :]
            turned = value.T
            put(full, 256 * fold, 256 * fold, jnp.where(row <= col, value, turned))
            line_at = TAIL_AT + TAIL * (2 * fold + 1) + rest
            diagonal = jnp.broadcast_to(g[line_at : line_at + 1, :], (128, 128))
            lower = jnp.where(row > col, value, jnp.where(row < col, turned, diagonal))
            put(full, 256 * fold + 128, 256 * fold + 128, lower)
        for j in range(5):
            at = TAIL_AT + TAIL * j
            value = g[at : at + rest, :]
            put(full, 512, 128 * j, value)
            if j < 4:
                tall = jnp.concatenate([value, jnp.zeros((128 - rest, 128), F32)], axis=0)
                put(full, 128 * j, 512, tall.T)

    def sort(group):
        base = jnp.asarray(group * wide).astype(F32)
        lane = lax.broadcasted_iota(jnp.int32, (cols, 128), 1).astype(F32) + base
        pick = jnp.concatenate(
            [(slot_col[...] == lane).astype(BF16), (slot_col[...] == lane + 128.0).astype(BF16)], axis=1
        )
        s_high = dot(x_high[...], pick)
        s_low = dot(x_low[...], pick)
        for o in range(each):
            lanes = slice(128 * (o // 2), 128 * (o // 2) + 128)
            high = s_high[:, lanes]
            low = pltpu.roll(s_low[:, lanes], SLOT, 1)
            mine = left_lanes if o % 2 == 0 else jnp.logical_not(left_lanes)
            right[o, 0:rows, :] = jnp.where(mine, high, low).astype(BF16)
            right[o, pad : pad + rows, :] = jnp.where(mine, high, 0.0).astype(BF16)

    def finish(group, outs):
        for pair in range(each // 2):
            lanes = slice(128 * pair, 128 * pair + 128)
            even, odd = outs[2 * pair : 2 * pair + 2]
            answer = jnp.where(left_lanes, even + pltpu.roll(even, SLOT, 1), odd + pltpu.roll(odd, SLOT, 1))
            y_high[group, :, lanes], y_low[group, :, lanes] = split(answer)

    def one_group(group, now, later):
        ahead = group + 1
        at = lax.rem(ahead, depth)
        sort(group)

        @pl.when(ahead < groups)
        def _():
            load_g(ahead, at).wait()

        outs = []
        for o in range(each):
            outs.append(dot(full[now * each + o], right[o]))
            unpack(packed.at[at, o], full.at[later * each + o])
        finish(group, outs)

        @pl.when(ahead + depth < groups)
        def _():
            load_g(ahead + depth, at).start()

    load_g(0, 0).wait()
    for at in range(1, depth):
        load_g(at, at).start()
    for o in range(each):
        unpack(packed.at[0, o], full.at[o])
    load_g(depth, 0).start()
    for copy in load_s:
        copy.start()

    def two_groups(i, carry):
        one_group(2 * i, 0, 1)
        one_group(2 * i + 1, 1, 0)
        return carry

    lax.fori_loop(0, groups // 2, two_groups, 0)

    for c in range(chunks):
        load_s[c].wait()
    for tile in range(cols // 256):
        value = None
        lanes = slice(256 * tile, 256 * tile + 256)
        for group in range(groups):
            part = dot(y_high[group], place[group, :, lanes]) + dot(y_low[group], place[group, :, lanes])
            value = part if value is None else value + part
        for c in (2 * tile, 2 * tile + 1):
            swept[c] = swept[c] + value[:, (c % 2) * CHUNK : (c % 2 + 1) * CHUNK]
            store(swept, gradient_hbm, 1, c).start()
    for c in range(chunks):
        store(forward, state_hbm, 0, c).wait()
        store(swept, gradient_hbm, 1, c).wait()


def apply(owner, forward, swept, gathered):
    chunks, rows, _ = forward.shape
    cols = chunks * CHUNK
    hbm = pl.BlockSpec(memory_space=pl.ANY)
    pad = 640
    groups, wide, depth = 8, 4 * SLOT, 3
    return pl.pallas_call(
        apply_kernel,
        out_shape=(jax.ShapeDtypeStruct((rows, 1, cols), F32),) * 2,
        in_specs=[pl.BlockSpec(memory_space=pltpu.VMEM)] + [hbm] * 3,
        out_specs=(hbm, hbm),
        scratch_shapes=[
            pltpu.VMEM((chunks, rows, CHUNK), F32),
            pltpu.VMEM((chunks, rows, CHUNK), F32),
            pltpu.VMEM((depth, wide // SLOT, PACKED, 128), F32),
            pltpu.VMEM((rows, cols), BF16),
            pltpu.VMEM((rows, cols), BF16),
            pltpu.VMEM((cols, 128), F32),
            pltpu.VMEM((groups, wide, cols), BF16),
            pltpu.VMEM((8, rows, 2 * pad), BF16),
            pltpu.VMEM((4, 2 * pad, 128), BF16),
            pltpu.VMEM((groups, rows, wide), BF16),
            pltpu.VMEM((groups, rows, wide), BF16),
            pltpu.SemaphoreType.DMA((2, chunks)),
            pltpu.SemaphoreType.DMA((depth,)),
            pltpu.SemaphoreType.DMA((2, chunks)),
        ],
        compiler_params=pltpu.CompilerParams(vmem_limit_bytes=60 * 1024 * 1024),
        name="apply",
    )(owner, forward, swept, gathered)


def by_row(x):
    return jnp.transpose(x, (1, 0, 2))


def body(search_one, search_two, column_gain, model_matrix, obs_owner, observe_matrix, error_weight, channel_mask):
    forward, swept, gathered = sweep(
        by_row(search_one), by_row(search_two), by_row(column_gain), by_row(model_matrix),
        by_row(observe_matrix[0]), error_weight[0], channel_mask[0],
    )
    state, gradient = apply(obs_owner, forward, swept, gathered)
    return by_row(state), by_row(gradient)


def solution(mesh):
    return jax.shard_map(
        body,
        mesh=mesh,
        in_specs=(
            P("tm", None, "region"),
            P("tm", None, "region"),
            P("tm", None, "region"),
            P("tm", None, None),
            P("tm", "region"),
            P("tm", "region", None, None),
            P("tm", "region", None),
            P("tm", "region", None),
        ),
        out_specs=(P("tm", None, "region"), P("tm", None, "region")),
        check_vma=False,
    )
```

```python
import jax
import jax.numpy as jnp
from jax import lax
from jax.experimental import pallas as pl
from jax.experimental.pallas import tpu as pltpu
from jax.sharding import PartitionSpec as P

F32 = jnp.float32
BF16 = jnp.bfloat16
MESH = pl.DeviceIdType.MESH

OFFDIAG = ((0, 1), (0, 2), (0, 3), (1, 2), (1, 3), (2, 3))
FOLD_AT = 768
TAIL_AT = 1024
TAIL = 40
PACKED = TAIL_AT + 5 * TAIL
HALVES = ((0, 616, 312), (616, 608, 304))
SLOT = 64
CHUNK = 128
FOLDED = 276
LAG = 2


def split(x):
    high = x.astype(BF16)
    return high, (x - high.astype(F32)).astype(BF16)


def dot(a, b):
    return jnp.dot(a, b, preferred_element_type=F32)


def dot_nt(a, b):
    return lax.dot_general(a, b, (((1,), (1,)), ((), ())), preferred_element_type=F32)


def form_packed(matrix, weight, out_ref, depart):
    high, low = split(matrix)
    whigh, wlow = split(matrix * weight)

    def product(r0, r1, c0, c1):
        a, b = slice(r0, r1), slice(c0, c1)
        return dot_nt(whigh[a], high[b]) + (dot_nt(whigh[a], low[b]) + dot_nt(wlow[a], high[b]))

    nv = matrix.shape[0]
    rest = nv - 512
    row = lax.broadcasted_iota(jnp.int32, (128, 128), 0)
    col = lax.broadcasted_iota(jnp.int32, (128, 128), 1)
    top = product(0, 256, 0, 512)

    def block(i, j):
        if i < 2:
            return top[128 * i : 128 * i + 128, 128 * j : 128 * j + 128]
        return mid[128 * i - 256 : 128 * i - 128, 128 * j - 256 : 128 * j - 128]

    for at, (i, j) in enumerate(OFFDIAG[:5]):
        out_ref[128 * at : 128 * at + 128, :] = block(i, j)
    depart(0)
    mid = product(256, 512, 256, 512)
    tail = product(512, nv, 0, nv)
    out_ref[640:FOLD_AT, :] = block(2, 3)
    for pair in range(2):
        upper, lower = block(2 * pair, 2 * pair), block(2 * pair + 1, 2 * pair + 1)
        at = FOLD_AT + 128 * pair
        out_ref[at : at + 128, :] = jnp.where(row <= col, upper, lower)
    for j in range(5):
        at = TAIL_AT + TAIL * j
        if j < 4:
            out_ref[at : at + rest, :] = tail[:, 128 * j : 128 * j + 128]
            if j % 2 == 1:
                line = jnp.sum(jnp.where(row == col, block(j, j), 0.0), axis=0, keepdims=True)
            else:
                line = jnp.zeros((1, 128), F32)
            out_ref[at + rest : at + TAIL, :] = jnp.broadcast_to(line, (TAIL - rest, 128))
        else:
            out_ref[at : at + TAIL, :] = jnp.zeros((TAIL, 128), F32)
            out_ref[at : at + rest, 0:rest] = tail[:, 512:nv]
    depart(1)


def sweep_kernel(
    one_hbm, two_hbm, gain_hbm, matrix_hbm, jacobian_hbm, error_ref, mask_ref,
    forward_out, swept_out, gathered_ref,
    one, two, gain, forward, swept, into_f, into_b, out_f, out_b, matrix, jacobian, packed_ref,
    m_high, m_low, t_high, t_low,
    load_sem, store_sem, matrix_sem, f_send, f_recv, b_send, b_recv, g_send, g_recv, p_send, p_recv, own_sem,
):
    k = lax.axis_index("tm")
    region = lax.axis_index("region")
    core = region % 2
    x = (region // 2) % 4
    z = region // 8
    chunks, rows, _ = one.shape
    pieces = 2 * chunks
    cut = rows - FOLDED

    def chip(dz, dx):
        return ((z + dz + 4) % 4 * 4 + (x + dx + 4) % 4) * 2 + core

    partner = region + 1 - 2 * core

    def load(which, c):
        hbm, vmem = ((one_hbm, one), (two_hbm, two), (gain_hbm, gain))[which]
        return pltpu.make_async_copy(
            hbm.at[:, 0, pl.ds(c * CHUNK, CHUNK)], vmem.at[c], load_sem.at[which, c]
        )

    def load_at(which, c):
        hbm, vmem = ((one_hbm, one), (two_hbm, two), (gain_hbm, gain))[which]
        return pltpu.make_async_copy(
            hbm.at[:, 0, pl.ds(pl.multiple_of(c * CHUNK, CHUNK), CHUNK)], vmem.at[c], load_sem.at[which, c]
        )

    matrix_copy = pltpu.make_async_copy(matrix_hbm.at[:, 0, :], matrix, matrix_sem.at[0])
    jacobian_copy = pltpu.make_async_copy(jacobian_hbm.at[:, 0, :], jacobian, matrix_sem.at[1])
    load(0, 0).start()
    matrix_copy.start()
    load(1, 0).start()
    load(2, 0).start()
    jacobian_copy.start()
    for which in range(3):
        load(which, 1).start()

    def store_f(src, c):
        return pltpu.make_async_copy(src, forward_out.at[c], store_sem.at[0, c])

    def store_b(src, c):
        return pltpu.make_async_copy(src, swept_out.at[c], store_sem.at[1, c])

    barrier = pltpu.get_barrier_semaphore()
    around = [(k, chip(1, 0)), (k, chip(-1, 0)), (k, chip(0, 1)), (k, chip(0, -1)), (k, partner),
              ((k + 1) % 4, region), ((k + 3) % 4, region)]
    for who in around:
        pl.semaphore_signal(barrier, inc=1, device_id=who, device_id_type=MESH)
    pl.semaphore_wait(barrier, len(around))

    def send_f(s):
        return pltpu.make_async_remote_copy(
            src_ref=out_f.at[s], dst_ref=into_f.at[s], send_sem=f_send.at[s], recv_sem=f_recv.at[s],
            device_id=((k + 1) % 4, region), device_id_type=MESH,
        )

    def send_b(s):
        return pltpu.make_async_remote_copy(
            src_ref=out_b.at[s], dst_ref=into_b.at[s], send_sem=b_send.at[s], recv_sem=b_recv.at[s],
            device_id=((k + 3) % 4, region), device_id_type=MESH,
        )

    def step_to(primary, by):
        return chip(by, 0) if primary == "z" else chip(0, by)

    def block_at(half, dp, dq):
        if half == 0:
            return chip(dq, dp)
        return chip(dp, dq)

    axes = (("x", "z"), ("z", "x"))
    sends = []

    def span(half, piece):
        start, size, first_part = HALVES[half]
        if piece == 0:
            return start, first_part
        if piece == 1:
            return start + first_part, size - first_part
        return start, size

    def relay_copy(number, half, dp, dq, piece, axis, by):
        start, size = span(half, piece)
        block = block_at(half, dp, dq)
        own = dp == 0 and dq == 0
        place = pl.ds(start, size)
        rp, rq = dp % 4, dq % 4
        if axis == axes[half][0]:
            rp = (dp - by) % 4
        else:
            rq = (dq - by) % 4
        return pltpu.make_async_remote_copy(
            src_ref=packed_ref.at[place] if own else gathered_ref.at[block, place],
            dst_ref=gathered_ref.at[block, place],
            send_sem=g_send.at[number],
            recv_sem=g_recv.at[half, rp * 4 + rq, 1 if piece == 1 else 0],
            device_id=(k, step_to(axis, by)),
            device_id_type=MESH,
        )

    def relay(*what):
        relay_copy(len(sends), *what).start()
        sends.append(what)

    def arrived(half, dp, dq, piece):
        start, size = span(half, piece)
        block = block_at(half, dp, dq)
        ref = gathered_ref.at[block, pl.ds(start, size)]
        sem = g_recv.at[half, dp % 4 * 4 + dq % 4, 1 if piece == 1 else 0]
        pltpu.make_async_copy(ref, ref, sem).wait()

    shared = []

    def share_copy(half, dp, dq):
        start, size = span(half, None)
        block = block_at(half, dp, dq)
        place = pl.ds(start, size)
        own = dp == 0 and dq == 0
        at = dp % 4 * 4 + dq % 4
        return pltpu.make_async_remote_copy(
            src_ref=packed_ref.at[place] if own else gathered_ref.at[block, place],
            dst_ref=gathered_ref.at[block, place],
            send_sem=p_send.at[half, at],
            recv_sem=p_recv.at[half, at],
            device_id=(k, partner),
            device_id_type=MESH,
        )

    def share(*what):
        share_copy(*what).start()
        shared.append(what)

    def first(half, by):
        main, other = axes[half]
        arrived(half, by, 0, None)
        relay(half, by, 0, 0 if by == -1 else 1, main, -by)
        relay(half, by, 0, None, other, 1)
        relay(half, by, 0, None, other, -1)
        share(half, by, 0)

    def opposite(half):
        _, other = axes[half]
        arrived(half, 2, 0, 0)
        arrived(half, 2, 0, 1)
        relay(half, 2, 0, None, other, 1)
        relay(half, 2, 0, None, other, -1)
        share(half, 2, 0)

    def second(half, dp, by):
        _, other = axes[half]
        arrived(half, dp, by, None)
        relay(half, dp, by, 0 if by == -1 else 1, other, -by)
        share(half, dp, by)

    def last(half, dp):
        arrived(half, dp, 2, 0)
        arrived(half, dp, 2, 1)
        share(half, dp, 2)

    left = lax.broadcasted_iota(jnp.int32, (FOLDED, CHUNK), 1) < CHUNK // 2

    def fold(v, h):
        top = pltpu.roll(v[0:FOLDED], CHUNK // 2 * h, 1)
        low = pltpu.roll(v[cut:rows], CHUNK // 2 * (1 - h), 1)
        return jnp.where(left, top, low)

    def unfold(target, c, one_half, other_half, add):
        turned, returned = pltpu.roll(one_half, CHUNK // 2, 1), pltpu.roll(other_half, CHUNK // 2, 1)
        top, low = jnp.where(left, one_half, returned), jnp.where(left, turned, other_half)
        if add is not None:
            top, low = add[0:FOLDED] + top, add[cut:rows] + low
        target[c, 0:FOLDED, :] = top
        target[c, cut:rows, :] = low

    def times(a_high, a_low, v):
        high = v.astype(BF16).astype(F32)
        low = pltpu.roll(v - high, CHUNK // 2, 1)
        both = jnp.concatenate(
            [jnp.where(left, high, low)[0:cut].astype(BF16), jnp.where(left, low, high).astype(BF16)], axis=0
        )
        alone = jnp.concatenate(
            [jnp.where(left, high, 0.0)[0:cut].astype(BF16), jnp.where(left, 0.0, high).astype(BF16)], axis=0
        )
        total = dot(a_high[...], both) + dot(a_low[...], alone)
        total = total + pltpu.roll(total, CHUNK // 2, 1)
        return jnp.where(left, total[0:FOLDED], total[cut:rows])

    def leave(c):
        load_at(0, c).wait()
        value = one[c]
        for h in range(2):
            out_f[2 * c + h] = fold(value, h)
            send_f(2 * c + h).start()
        store_f(one.at[c], c).start()

    def forward_step(s):
        c, h = s // 2, s % 2

        @pl.when(h == 0)
        def _():
            load_at(0, c).wait()

            @pl.when(k == 1)
            def _():
                load_at(2, c).wait()

        send_f(s).wait_recv()
        out_f[s] = fold(one[c], h) + fold(gain[c], h) * times(m_high, m_low, into_f[s])

        @pl.when(k < 3)
        def _():
            send_f(s).start()

        @pl.when(h == 1)
        def _():
            unfold(forward, c, out_f[s - 1], out_f[s], None)
            store_f(forward.at[c], c).start()

    def backward_step(s):
        c, h = s // 2, s % 2

        @pl.when(h == 0)
        def _():
            load_at(1, c).wait()

            @pl.when(k != 1)
            def _():
                load_at(2, c).wait()

        @pl.when(k < 3)
        def _():
            send_b(s).wait_recv()

        @pl.when(k == 3)
        def _():
            into_b[s] = jnp.zeros((FOLDED, CHUNK), F32)

        @pl.when(k > 0)
        def _():
            out_b[s] = times(t_high, t_low, fold(gain[c], h) * (fold(two[c], h) + into_b[s]))
            send_b(s).start()

        @pl.when(h == 1)
        def _():
            unfold(swept, c, into_b[s - 1], into_b[s], two[c])
            store_b(swept.at[c], c).start()

    @pl.when(k == 0)
    def _():
        leave(0)
        leave(1)

    matrix_copy.wait()
    t_high[...], t_low[...] = split(matrix[...].T)

    @pl.when(k == 3)
    def _():
        backward_step(0)
        backward_step(1)

    m_high[...], m_low[...] = split(matrix[...])

    def depart(half):
        main, other = axes[half]
        for axis in (main, other):
            relay(half, 0, 0, None, axis, 1)
            relay(half, 0, 0, None, axis, -1)
        share(half, 0, 0)

    jacobian_copy.wait()
    for c in range(2, chunks):
        for which in range(3):
            load(which, c).start()
    form_packed(jacobian[...], error_ref[...] * mask_ref[...].astype(F32), packed_ref, depart)
    own_copy = pltpu.make_async_copy(packed_ref, gathered_ref.at[region], own_sem)
    own_copy.start()

    events = {
        5: [(first, 0, -1), (first, 1, -1), (first, 0, 1), (first, 1, 1)],
        8: [(second, 0, 0, -1), (second, 1, 0, -1), (second, 0, 0, 1), (second, 1, 0, 1)],
        9: [(opposite, 0), (opposite, 1)],
        12: [(second, 0, -1, -1), (second, 1, -1, -1), (second, 0, -1, 1), (second, 1, -1, 1)],
        14: [(second, 0, 1, -1), (second, 1, 1, -1), (second, 0, 1, 1), (second, 1, 1, 1)],
        15: [(last, 0, 0), (last, 1, 0)],
        16: [(second, 0, 2, -1), (second, 1, 2, -1), (second, 0, 2, 1), (second, 1, 2, 1)],
        18: [(last, 0, -1), (last, 1, -1), (last, 0, 1), (last, 1, 1)],
        20: [(last, 0, 2), (last, 1, 2)],
    }

    def tick(t, carry):
        @pl.when((k == 0) & (t >= 1) & (t < chunks - 1))
        def _():
            leave(t + 1)

        cf = t - LAG * k

        @pl.when((cf >= 0) & (cf < pieces) & (k > 0))
        def _():
            forward_step(cf)

        cb = t - LAG * (3 - k)

        @pl.when((cb >= jnp.where(k == 3, 2, 0)) & (cb < pieces))
        def _():
            backward_step(cb)

        for when, what in events.items():

            @pl.when(t == when)
            def _():
                for event in what:
                    event[0](*event[1:])

        return carry

    lax.fori_loop(0, pieces + 3 * LAG, tick, 0)

    for c in range(chunks):
        store_f(forward.at[c], c).wait()
        store_b(swept.at[c], c).wait()

    @pl.when(k < 3)
    def _():
        for s in range(pieces):
            send_f(s).wait_send()

    @pl.when(k > 0)
    def _():
        for s in range(pieces):
            send_b(s).wait_send()

    own_copy.wait()
    for number, what in enumerate(sends):
        relay_copy(number, *what).wait_send()
    for what in shared:
        share_copy(*what).wait_send()
        half, dp, dq = what
        start, size = span(half, None)
        block = block_at(half, dp, dq) + 1 - 2 * core
        ref = gathered_ref.at[block, pl.ds(start, size)]
        pltpu.make_async_copy(ref, ref, p_recv.at[half, dp % 4 * 4 + dq % 4]).wait()


def sweep(one, two, gain, matrix, jacobian, error, mask):
    rows, _, cols = one.shape
    chunks = cols // CHUNK
    vmem = pl.BlockSpec(memory_space=pltpu.VMEM)
    hbm = pl.BlockSpec(memory_space=pl.ANY)
    chunked = (chunks, rows, CHUNK)
    square = (rows, rows)
    return pl.pallas_call(
        sweep_kernel,
        out_shape=(
            jax.ShapeDtypeStruct(chunked, F32),
            jax.ShapeDtypeStruct(chunked, F32),
            jax.ShapeDtypeStruct((32, PACKED, 128), F32),
        ),
        in_specs=[hbm] * 5 + [vmem] * 2,
        out_specs=(hbm, hbm, hbm),
        scratch_shapes=[pltpu.VMEM(chunked, F32)] * 5
        + [pltpu.VMEM((2 * chunks, FOLDED, CHUNK), F32)] * 4
        + [pltpu.VMEM(square, F32), pltpu.VMEM((rows, cols), F32), pltpu.VMEM((PACKED, 128), F32)]
        + [pltpu.VMEM(square, BF16)] * 4
        + [
            pltpu.SemaphoreType.DMA((3, chunks)),
            pltpu.SemaphoreType.DMA((2, chunks)),
            pltpu.SemaphoreType.DMA((2,)),
            pltpu.SemaphoreType.DMA((2 * chunks,)),
            pltpu.SemaphoreType.DMA((2 * chunks,)),
            pltpu.SemaphoreType.DMA((2 * chunks,)),
            pltpu.SemaphoreType.DMA((2 * chunks,)),
            pltpu.SemaphoreType.DMA((40,)),
            pltpu.SemaphoreType.DMA((2, 16, 2)),
            pltpu.SemaphoreType.DMA((2, 16)),
            pltpu.SemaphoreType.DMA((2, 16)),
            pltpu.SemaphoreType.DMA,
        ],
        compiler_params=pltpu.CompilerParams(
            collective_id=0, has_side_effects=True, vmem_limit_bytes=60 * 1024 * 1024
        ),
        name="sweep",
    )(one, two, gain, matrix, jacobian, error, mask)


def apply_kernel(
    owner_ref, forward_hbm, swept_hbm, gathered_hbm,
    state_hbm, gradient_hbm,
    forward, swept, packed, x_high, x_low, slot_col, place, full, right, y_high, y_low,
    in_sem, packed_sem, out_sem,
):
    chunks, rows, _ = forward.shape
    groups, wide, cols = place.shape
    pad = full.shape[2] // 2
    depth = packed.shape[0]
    each = wide // SLOT
    load_f = [pltpu.make_async_copy(forward_hbm.at[c], forward.at[c], in_sem.at[0, c]) for c in range(chunks)]
    load_s = [pltpu.make_async_copy(swept_hbm.at[c], swept.at[c], in_sem.at[1, c]) for c in range(chunks)]

    def load_g(group, at):
        return pltpu.make_async_copy(
            gathered_hbm.at[pl.ds(group * each, each)], packed.at[at], packed_sem.at[at]
        )

    def store(source, target, which, c):
        return pltpu.make_async_copy(
            source.at[c], target.at[:, 0, pl.ds(c * CHUNK, CHUNK)], out_sem.at[which, c]
        )

    load_g(0, 0).start()
    for copy in load_f:
        copy.start()

    owner = owner_ref[...]
    onehot = (owner == lax.broadcasted_iota(jnp.int32, (32, cols), 0)).astype(F32)
    earlier = (
        lax.broadcasted_iota(jnp.int32, (cols, cols), 0) < lax.broadcasted_iota(jnp.int32, (cols, cols), 1)
    ).astype(BF16)
    before = dot(onehot.astype(BF16), earlier)
    placed = jnp.sum(before * onehot, axis=0, keepdims=True)
    slot = owner.astype(F32) * SLOT + placed
    slot_col[...] = jnp.broadcast_to(slot, (128, cols)).T
    line = lax.broadcasted_iota(jnp.int32, (wide, cols), 0).astype(F32)
    for group in range(groups):
        place[group] = (jnp.broadcast_to(slot - group * wide, (wide, cols)) == line).astype(BF16)
    right[...] = jnp.zeros_like(right)

    for c in range(chunks):
        load_f[c].wait()
        lanes = slice(c * CHUNK, (c + 1) * CHUNK)
        x_high[:, lanes], x_low[:, lanes] = split(forward[c])
        store(forward, state_hbm, 0, c).start()

    row = lax.broadcasted_iota(jnp.int32, (128, 128), 0)
    col = lax.broadcasted_iota(jnp.int32, (128, 128), 1)
    left_lanes = lax.broadcasted_iota(jnp.int32, (rows, 128), 1) < SLOT
    rest = rows - 512

    def put(full, at_row, at_col, value):
        high, low = split(value)
        r, c = value.shape
        full[at_row : at_row + r, at_col : at_col + c] = high
        full[at_row : at_row + r, pad + at_col : pad + at_col + c] = low

    def unpack(g, full):
        for at, (i, j) in enumerate(OFFDIAG):
            value = g[128 * at : 128 * at + 128, :]
            put(full, 128 * i, 128 * j, value)
            put(full, 128 * j, 128 * i, value.T)
        for fold in range(2):
            at = FOLD_AT + 128 * fold
            value = g[at : at + 128, :]
            turned = value.T
            put(full, 256 * fold, 256 * fold, jnp.where(row <= col, value, turned))
            line_at = TAIL_AT + TAIL * (2 * fold + 1) + rest
            diagonal = jnp.broadcast_to(g[line_at : line_at + 1, :], (128, 128))
            lower = jnp.where(row > col, value, jnp.where(row < col, turned, diagonal))
            put(full, 256 * fold + 128, 256 * fold + 128, lower)
        for j in range(5):
            at = TAIL_AT + TAIL * j
            value = g[at : at + rest, :]
            put(full, 512, 128 * j, value)
            if j < 4:
                tall = jnp.concatenate([value, jnp.zeros((128 - rest, 128), F32)], axis=0)
                put(full, 128 * j, 512, tall.T)

    def sort(group):
        base = jnp.asarray(group * wide).astype(F32)
        lane = lax.broadcasted_iota(jnp.int32, (cols, 128), 1).astype(F32) + base
        pick = jnp.concatenate(
            [(slot_col[...] == lane).astype(BF16), (slot_col[...] == lane + 128.0).astype(BF16)], axis=1
        )
        s_high = dot(x_high[...], pick)
        s_low = dot(x_low[...], pick)
        for o in range(each):
            lanes = slice(128 * (o // 2), 128 * (o // 2) + 128)
            high = s_high[:, lanes]
            low = pltpu.roll(s_low[:, lanes], SLOT, 1)
            mine = left_lanes if o % 2 == 0 else jnp.logical_not(left_lanes)
            right[o, 0:rows, :] = jnp.where(mine, high, low).astype(BF16)
            right[o, pad : pad + rows, :] = jnp.where(mine, high, 0.0).astype(BF16)

    def finish(group, outs):
        for pair in range(each // 2):
            lanes = slice(128 * pair, 128 * pair + 128)
            even, odd = outs[2 * pair : 2 * pair + 2]
            answer = jnp.where(left_lanes, even + pltpu.roll(even, SLOT, 1), odd + pltpu.roll(odd, SLOT, 1))
            y_high[group, :, lanes], y_low[group, :, lanes] = split(answer)

    def one_group(group, now, later):
        ahead = group + 1
        at = lax.rem(ahead, depth)
        sort(group)

        @pl.when(ahead < groups)
        def _():
            load_g(ahead, at).wait()

        outs = []
        for o in range(each):
            outs.append(dot(full[now * each + o], right[o]))
            unpack(packed.at[at, o], full.at[later * each + o])
        finish(group, outs)

        @pl.when(ahead + depth < groups)
        def _():
            load_g(ahead + depth, at).start()

    load_g(0, 0).wait()
    for at in range(1, depth):
        load_g(at, at).start()
    for o in range(each):
        unpack(packed.at[0, o], full.at[o])
    load_g(depth, 0).start()
    for copy in load_s:
        copy.start()

    def two_groups(i, carry):
        one_group(2 * i, 0, 1)
        one_group(2 * i + 1, 1, 0)
        return carry

    lax.fori_loop(0, groups // 2, two_groups, 0)

    for c in range(chunks):
        load_s[c].wait()
    for tile in range(cols // 256):
        value = None
        lanes = slice(256 * tile, 256 * tile + 256)
        for group in range(groups):
            part = dot(y_high[group], place[group, :, lanes]) + dot(y_low[group], place[group, :, lanes])
            value = part if value is None else value + part
        for c in (2 * tile, 2 * tile + 1):
            swept[c] = swept[c] + value[:, (c % 2) * CHUNK : (c % 2 + 1) * CHUNK]
            store(swept, gradient_hbm, 1, c).start()
    for c in range(chunks):
        store(forward, state_hbm, 0, c).wait()
        store(swept, gradient_hbm, 1, c).wait()


def apply(owner, forward, swept, gathered):
    chunks, rows, _ = forward.shape
    cols = chunks * CHUNK
    hbm = pl.BlockSpec(memory_space=pl.ANY)
    pad = 640
    groups, wide, depth = 8, 4 * SLOT, 3
    return pl.pallas_call(
        apply_kernel,
        out_shape=(jax.ShapeDtypeStruct((rows, 1, cols), F32),) * 2,
        in_specs=[pl.BlockSpec(memory_space=pltpu.VMEM)] + [hbm] * 3,
        out_specs=(hbm, hbm),
        scratch_shapes=[
            pltpu.VMEM((chunks, rows, CHUNK), F32),
            pltpu.VMEM((chunks, rows, CHUNK), F32),
            pltpu.VMEM((depth, wide // SLOT, PACKED, 128), F32),
            pltpu.VMEM((rows, cols), BF16),
            pltpu.VMEM((rows, cols), BF16),
            pltpu.VMEM((cols, 128), F32),
            pltpu.VMEM((groups, wide, cols), BF16),
            pltpu.VMEM((8, rows, 2 * pad), BF16),
            pltpu.VMEM((4, 2 * pad, 128), BF16),
            pltpu.VMEM((groups, rows, wide), BF16),
            pltpu.VMEM((groups, rows, wide), BF16),
            pltpu.SemaphoreType.DMA((2, chunks)),
            pltpu.SemaphoreType.DMA((depth,)),
            pltpu.SemaphoreType.DMA((2, chunks)),
        ],
        compiler_params=pltpu.CompilerParams(vmem_limit_bytes=60 * 1024 * 1024),
        name="apply",
    )(owner, forward, swept, gathered)


def by_row(x):
    return jnp.transpose(x, (1, 0, 2))


def body(search_one, search_two, column_gain, model_matrix, obs_owner, observe_matrix, error_weight, channel_mask):
    forward, swept, gathered = sweep(
        by_row(search_one), by_row(search_two), by_row(column_gain), by_row(model_matrix),
        by_row(observe_matrix[0]), error_weight[0], channel_mask[0],
    )
    state, gradient = apply(obs_owner, forward, swept, gathered)
    return by_row(state), by_row(gradient)


def solution(mesh):
    return jax.shard_map(
        body,
        mesh=mesh,
        in_specs=(
            P("tm", None, "region"),
            P("tm", None, "region"),
            P("tm", None, "region"),
            P("tm", None, None),
            P("tm", "region"),
            P("tm", "region", None, None),
            P("tm", "region", None),
            P("tm", "region", None),
        ),
        out_specs=(P("tm", None, "region"), P("tm", None, "region")),
        check_vma=False,
    )
```
